32 devices in a mesh: sec: 4 (over y, x), blk: 8 (over z, core).
Axes of the slice: x: 2, y: 2, z: 4, core: 2. Of those that a mesh axis runs over, the one named last changes fastest.
Arguments:
- state: float32 [2, 72, 4096], P(None, None, ('sec', 'blk')), may hold values from -6 to 6
- neighbors: int32 [4, 4096], P(None, ('sec', 'blk')), may hold values from 0 to 4095, as said below
- owner: int32 [4096, 1], P(('sec', 'blk')), may hold values from 0 to 31; in each aligned block of 128 rows (0 to 127, 128 to 255, ...) at most 8 rows name the same one
- crm_state: bfloat16 [8192, 9216], P(('sec', 'blk')), may hold values from -6 to 6
- phase_mask: int32 [8192, 4608], P(('sec', 'blk')), may hold values 0 or 1
Outputs:
- new_state: float32 [2, 72, 4096], P(None, None, ('sec', 'blk'))
The draws below stay inside these ranges and needn't reach their ends.
Inputs may be any that keep to these rules, and one draw needn't show every extreme that they name: `neighbors`: each entry is a column index within 8 of its own column's index, counted cyclically over 4096. Among the columns of one device no owner is named more than 8 times.
All inputs are finite; a program needn't handle non-finite values. No bound on the sum of `phase_mask` on one device may be relied on, other than what follows from the above.
Results may differ from the reference program's by a relative error of at most 0.0003.
Values sent between devices are 32-bit elements; how exact they have to be, the bound alone decides.
No kernel may reach another device: no remote copies, remote signals or barrier semaphores. Data moves between devices by JAX's collectives and lax.ppermute only.
A program may use at most 128 MiB of HBM per device.

```python
import math
import jax
import jax.numpy as jnp
import numpy as np
from jax import lax

LEV = 72
CRMX = 64
SUB = 4
REACH = 8
COL_DEV = 128
COLS = 4096
CAP = 8
SLOTS = 256
INSTANCES = 8192
N_SEC = 4
N_BLK = 8


def draw_neighbors(key, part):
    offsets = jax.random.randint(key, (4, COLS), -REACH, REACH + 1).astype(jnp.int32)
    offsets = offsets.at[0, 0].set(REACH).at[1, 0].set(-REACH).at[2, 0].set(-1).at[3, 1].set(-1)
    base = jnp.arange(COLS, dtype=jnp.int32)[None, :]
    return jnp.mod(base + offsets, COLS).astype(jnp.int32)


def touch_ends(array, rng, least, top_value):
    spot = [jax.random.randint(jax.random.fold_in(rng, axis), (), 0, length) for axis, length in enumerate(array.shape)]
    longest = array.shape.index(max(array.shape))
    next_to = spot[:longest] + [(spot[longest] + 1) % array.shape[longest]] + spot[longest + 1:]
    return array.at[tuple(spot)].set(least).at[tuple(next_to)].set(top_value)


def block_levels(key, dims, pieces, smallest, largest):
    gain = 1.0
    for axis_at, blocks in pieces:
        steps = jax.random.uniform(jax.random.fold_in(jax.random.fold_in(key, 6), axis_at), (blocks,), jnp.float32, smallest / len(pieces), largest / len(pieces))
        gain = gain * jnp.repeat(jnp.exp(steps), dims[axis_at] // blocks).reshape((-1,) + (1,) * (len(dims) - 1 - axis_at))
    return gain


def assign_block(rng, own, number, rows, number_of, top, reach, slope):
    ranking = jax.random.permutation(rng, number_of)
    heavy_load, usual = portions_of(number_of, rows * top, reach, slope, True), portions_of(number_of, rows * top, reach, slope, False)
    places = jnp.arange(number_of)

    def named(lengths, rotation):
        used = int((lengths > 0).sum())
        fixed = max(1, used // 4)
        shifted = fixed + (places - fixed + rotation * (used - fixed)) % max(1, number_of - fixed)
        return jnp.zeros((number_of,), jnp.int32).at[ranking[jnp.where(places < fixed, places, shifted)]].set(jnp.asarray(lengths, jnp.int32))

    lengths = jnp.where(number % 4 == 0, named(heavy_load, number // 4), named(usual, number - number // 4 - 1))
    mixed = jax.random.permutation(jax.random.fold_in(own, 3), number_of)
    source_of, sink = mixed[0:number_of // 2 * 2:2], mixed[1:number_of // 2 * 2:2]
    room = jnp.minimum(lengths[source_of] - 1, reach - lengths[sink]) // 2
    room = jnp.where((source_of == ranking[0]) | (sink == ranking[0]) | (lengths[sink] == 0), 0, jnp.maximum(room, 0))
    shifted = jax.random.randint(jax.random.fold_in(own, 4), (number_of // 2,), 0, 1 << 20) % (room + 1)
    lengths = lengths.at[source_of].add(-shifted).at[sink].add(shifted)
    labels = jnp.searchsorted(jnp.cumsum(lengths), jnp.arange(rows * top), side="right").astype(jnp.int32)
    listing = labels.reshape(top, rows).T
    listing = listing[jax.random.permutation(jax.random.fold_in(own, 1), rows)]
    rotation = jax.random.randint(jax.random.fold_in(own, 2), (rows, 1), 0, top)
    return jnp.take_along_axis(listing, (jnp.arange(top)[None, :] + rotation) % top, axis=1)


def portions_of(number_of, total, most, skew, full):
    weights = [(1 << 20) // math.isqrt(rank ** skew) + 1 for rank in range(1, number_of + 1)]
    largest = most if full else min(most, max(-(-total // number_of), total * weights[0] // sum(weights)))
    least = 1 if total - largest >= number_of - 1 else 0
    holding, spare = [largest] + [least] * (number_of - 1), total - largest - least * (number_of - 1)
    while spare > 0:
        movable = [i for i in range(1, number_of) if holding[i] < largest] or [i for i in range(1, number_of) if holding[i] < most]
        whole, left = sum([weights[i] for i in movable]), spare
        for i in movable:
            more = min(most - holding[i], max(1, left * weights[i] // whole), spare)
            holding[i] = holding[i] + more
            spare = spare - more
    return np.array(holding)


def scatter_about(rng, shape, width, bound, split=(), kind=jnp.bfloat16):
    array = jax.random.normal(rng, shape, jnp.float32) * width
    if len(split) > 0:
        array = block_levels(rng, shape, split, -0.22, 0.18) * array
    return jnp.clip(array, min=-bound, max=bound).astype(kind)


def setup_inputs(seed: int = 0) -> dict:
    arg_keys = jax.random.split(jax.random.key(seed), 6)
    state = scatter_about(arg_keys[0], (2, LEV, COLS), 1.0, 6.0, ((2, 32),), jnp.float32)
    neighbors = draw_neighbors(jax.random.fold_in(arg_keys[5], 71), 0)
    owner_keys = jax.random.split(jax.random.fold_in(arg_keys[2], 1), COLS // COL_DEV)
    owner_turns = jax.random.permutation(jax.random.fold_in(arg_keys[2], 3), COLS // COL_DEV)
    owner = jax.vmap(lambda own, number: assign_block(jax.random.fold_in(arg_keys[2], 2), own, number, COL_DEV, N_SEC * N_BLK, 1, CAP, 2))(owner_keys, owner_turns).reshape((COLS, 1))
    crm_state = scatter_about(arg_keys[3], (INSTANCES, 2 * LEV * CRMX), 1.0, 6.0, ((0, 32),))
    phase_mask = touch_ends((jax.random.randint(arg_keys[4], (INSTANCES, LEV * CRMX), 0, 2) < 1).astype(jnp.int32), jax.random.fold_in(arg_keys[4], 1), 0, 1)
    return dict(state=state, neighbors=neighbors, owner=owner, crm_state=crm_state, phase_mask=phase_mask)


def condense(temp_col, moist_col, temp_force, moist_force, pert, flags):
    count = pert.shape[0]
    levels = temp_col.shape[1]
    fields = pert.astype(jnp.float32).reshape(count, 2, levels, -1)
    temper = temp_col[:, :, None] + fields[:, 0]
    moisture = moist_col[:, :, None] + fields[:, 1]
    is_ice = flags.reshape(count, levels, -1) == 1
    rate = jnp.where(is_ice, 0.3, 0.7).astype(jnp.float32)
    heat = jnp.where(is_ice, 1.3, 1.0).astype(jnp.float32)
    for substep in range(SUB):
        temper = temper + 0.2 * (jnp.roll(temper, 1, 2) + jnp.roll(temper, -1, 2) - 2.0 * temper)
        moisture = moisture + 0.2 * (jnp.roll(moisture, 1, 2) + jnp.roll(moisture, -1, 2) - 2.0 * moisture)
        temper = temper + temp_force[:, :, None] / SUB
        moisture = moisture + moist_force[:, :, None] / SUB
        excess = moisture - 0.8 * jnp.exp(0.3 * temper)
        cond = rate * jnp.maximum(excess, 0.0)
        moisture = moisture - cond
        temper = temper + heat * cond
    return jnp.mean(temper, axis=2) - temp_col, jnp.mean(moisture, axis=2) - moist_col


def reference(state, neighbors, owner, crm_state, phase_mask):
    ndev = N_SEC * N_BLK
    cdev = COL_DEV
    near = jnp.zeros_like(state)
    for k in range(4):
        near = near + jnp.take(state, neighbors[k], axis=2)
    dyn = 0.15 * (near - 4.0 * state)
    owners = owner[:, 0].reshape(ndev, cdev)
    order = jnp.arange(cdev, dtype=jnp.int32)

    def one_block(source):
        block_owner = lax.dynamic_index_in_dim(owners, source, 0, keepdims=False)
        same = (block_owner[:, None] == block_owner[None, :]) & (order[None, :] < order[:, None])
        rank = jnp.sum(same.astype(jnp.int32), axis=1).astype(jnp.int32)
        instance = (block_owner * SLOTS + source * CAP + rank).astype(jnp.int32)
        pert = jnp.take(crm_state, instance, axis=0)
        flags = jnp.take(phase_mask, instance, axis=0)
        cols = lax.dynamic_slice_in_dim(state, (source * cdev).astype(jnp.int32), cdev, 2)
        force = lax.dynamic_slice_in_dim(dyn, (source * cdev).astype(jnp.int32), cdev, 2)
        tend_temp, tend_moist = condense(cols[0].T, cols[1].T, force[0].T, force[1].T, pert, flags)
        return jnp.stack([tend_temp.T, tend_moist.T])

    tends = lax.map(one_block, jnp.arange(ndev, dtype=jnp.int32))
    tends = jnp.transpose(tends, (1, 2, 0, 3)).reshape(state.shape)
    return state + dyn + tends
```

```python
import functools
import math

import jax
import jax.numpy as jnp
from jax import lax
from jax.experimental import pallas as pl
from jax.experimental.pallas import tpu as pltpu
from jax.sharding import PartitionSpec as P

SUB = 4
REACH = 8
GROUP = 4
AXES = ("sec", "blk")
F32 = jnp.float32
BF16 = jnp.bfloat16
NT = (((1,), (1,)), ((), ()))
NN = (((1,), (0,)), ((), ()))
TN = (((0,), (0,)), ((), ()))
VMEM = pl.BlockSpec(memory_space=pltpu.VMEM)
SMEM = pl.BlockSpec(memory_space=pltpu.SMEM)


def parts_of(x):
    high = x.astype(BF16)
    rest = x - high.astype(F32)
    middle = rest.astype(BF16)
    low = (rest - middle.astype(F32)).astype(BF16)
    return high, middle, low


def select_dot(x, onehot, dims, flip=False):
    total = None
    for part in parts_of(x):
        pair = (onehot, part) if flip else (part, onehot)
        term = lax.dot_general(*pair, dims, preferred_element_type=F32)
        total = term if total is None else total + term
    return total


def pack_kernel(cap, slots, total, first_ref, state_ref, before_ref, after_ref, near_ref, owner_ref, out_ref, dyn_ref, hot_ref):
    rows, cdev = state_ref.shape
    state = state_ref[...]
    index = near_ref[...] - (first_ref[0] - REACH)
    index = jnp.where(index < 0, index + total, index)
    index = jnp.where(index >= total, index - total, index)
    own = lax.broadcasted_iota(jnp.int32, (cdev, cdev), 0) + REACH
    edge = lax.broadcasted_iota(jnp.int32, (REACH, cdev), 0)
    counts = [jnp.zeros((cdev, cdev), F32), jnp.zeros((REACH, cdev), F32), jnp.zeros((REACH, cdev), F32)]
    for k in range(near_ref.shape[0]):
        row = index[k:k + 1, :]
        for i, place in enumerate((own, edge, edge + (REACH + cdev))):
            counts[i] = counts[i] + jnp.where(place == row, 1.0, 0.0)
    counts = [c.astype(BF16) for c in counts]
    near = select_dot(state, counts[0], NN)
    near = near + select_dot(before_ref[...], counts[1], NN)
    near = near + select_dot(after_ref[...], counts[2], NN)
    dyn = 0.15 * (near - 4.0 * state)
    dyn_ref[...] = dyn
    mine = jnp.broadcast_to(owner_ref[...], (cdev, cdev)).astype(F32)
    other = mine.T
    lower = lax.broadcasted_iota(jnp.int32, (cdev, cdev), 0) < lax.broadcasted_iota(jnp.int32, (cdev, cdev), 1)
    rank = jnp.sum(jnp.where((mine == other) & lower, 1.0, 0.0), axis=0, keepdims=True)
    target = owner_ref[...] * cap + rank.astype(jnp.int32)
    hot = jnp.where(lax.broadcasted_iota(jnp.int32, (slots, cdev), 0) == target, 1.0, 0.0).astype(BF16)
    hot_ref[...] = hot
    out_ref[:, 0:rows] = select_dot(state, hot, NT, True)
    out_ref[:, rows:2 * rows] = select_dot(dyn, hot, NT, True)


def prepare_kernel(crmx, ct_ref, cm_ref, mask_ref, yt_ref, ym_ref, rate_ref, both_ref):
    step = pl.program_id(0)
    width = ct_ref.shape[1]
    per = GROUP * crmx
    row = lax.broadcasted_iota(jnp.int32, (per, per), 0)
    col = lax.broadcasted_iota(jnp.int32, (per, per), 1)
    place = row % crmx
    apart = (((place % 8) * (crmx // 8) + place // 8) - col) & (crmx - 1)
    same = (row // crmx) == (col // crmx)
    move = jnp.where(same & (apart == 0), 1.0, 0.0)
    spread = jnp.where(same & ((apart == 1) | (apart == crmx - 1)), 1.0, 3.0 * move)
    move, spread = move.astype(BF16), spread.astype(BF16)
    for q in range(width // per):
        part = slice(q * per, (q + 1) * per)
        to = pl.ds(pl.multiple_of(step * width + q * per, per), per)
        yt_ref[to, :] = lax.dot_general(spread, ct_ref[:, part], NT, preferred_element_type=F32)
        ym_ref[to, :] = lax.dot_general(spread, cm_ref[:, part], NT, preferred_element_type=F32)
        ice = lax.dot_general(move, mask_ref[:, part].astype(F32).astype(BF16), NT, preferred_element_type=F32)
        rate_ref[to, :] = 0.7 - 0.4 * ice
        both_ref[to, :] = 0.7 - 0.31 * ice


def physics_kernel(levels, crmx, arrived_ref, yt_ref, ym_ref, rate_ref, both_ref, out_ref, rows_ref, sums_ref):
    slots = yt_ref.shape[1]
    steps = crmx // 8
    scale = 0.3 * math.log2(math.e)
    shift = [math.log(0.8 * 5.0 ** j) / 0.3 for j in range(SUB + 1)]
    columns = []
    for start in range(0, 4 * levels, 128):
        size = min(128, 4 * levels - start)
        block = arrived_ref[:, start:start + size]
        if size < 128:
            block = jnp.concatenate([block, jnp.zeros((slots, 128 - size), F32)], axis=1)
        columns.append(block.T[:size])
    arrived = jnp.concatenate(columns, axis=0)
    temp, moist, push, wet = [arrived[i * levels:(i + 1) * levels] for i in range(4)]
    push, wet = push * (1.0 / SUB), wet * (1.0 / SUB)
    tables = [5.0 * (temp + push + shift[1]), 5.0 * (moist + wet)]
    for j in range(2, SUB + 1):
        tables += [5.0 ** j * (push + (shift[j] - shift[j - 1])), 5.0 ** j * wet]
    for i, table in enumerate(tables):
        for half in range(slots // 128):
            rows_ref[half, i * levels:(i + 1) * levels] = table[:, half * 128:(half + 1) * 128]

    def unit(level, half):
        lanes = pl.ds(half * 128, 128)
        base = pl.multiple_of(level * crmx, crmx)
        get = lambda ref, k: ref[pl.ds(base + 8 * k, 8), lanes]
        const = lambda i: rows_ref[half, pl.ds(level + i * levels, 8, stride=0), :]
        add_t, add_m = const(0), const(1)
        temp = [get(yt_ref, k) + add_t for k in range(steps)]
        moist = [get(ym_ref, k) + add_m for k in range(steps)]
        for j in range(1, SUB + 1):
            if j > 1:
                spread = []
                for field, add in ((temp, const(2 * j - 2)), (moist, const(2 * j - 1))):
                    after = pltpu.roll(field[0], 7, 0)
                    before = pltpu.roll(field[steps - 1], 1, 0)
                    ring = [before] + field + [after]
                    spread.append([((ring[k] + ring[k + 2]) + 3.0 * field[k]) + add for k in range(steps)])
                temp, moist = spread
            temp, moist = list(temp), list(moist)
            for k in range(steps):
                over = jnp.maximum(moist[k] - jnp.exp2((scale / 5.0 ** j) * temp[k]), 0.0)
                moist[k] = moist[k] - get(rate_ref, k) * over
                temp[k] = temp[k] + get(both_ref, k) * over
        for i, field in enumerate((temp, moist)):
            while len(field) > 1:
                field = [a + b for a, b in zip(field[0::2], field[1::2])]
            sums_ref[half, pl.ds(pl.multiple_of((i * levels + level) * 8, 8), 8), :] = field[0]

    @pl.loop(0, levels)
    def _(level):
        for half in range(slots // 128):
            unit(level, half)

    factor = 1.0 / (crmx * 5.0 ** SUB)
    total = 2 * levels
    for half in range(slots // 128):
        summed = sums_ref[half, pl.ds(0, total, stride=8), :]
        for s in range(1, 8):
            summed = summed + sums_ref[half, pl.ds(s, total, stride=8), :]
        mean = summed * factor
        mean = jnp.concatenate([mean[:levels] - shift[SUB], mean[levels:], jnp.zeros((256 - total, 128), F32)], axis=0)
        out_ref[pl.ds(half * 128, 128), :] = mean.T[:, :total]


def finish_kernel(state_ref, dyn_ref, hot_ref, back_ref, out_ref):
    rows = state_ref.shape[0]
    out_ref[...] = dyn_ref[...] + select_dot(back_ref[...], hot_ref[...], TN)


def local(state, neighbors, owner, crm_state, phase_mask):
    ndev = lax.axis_size(AXES)
    me = lax.axis_index(AXES)
    fields, levels, cdev = state.shape
    rows = fields * levels
    slots, wide = crm_state.shape
    crmx = wide // rows
    cap = slots // ndev
    flat = state.reshape(rows, cdev)
    up = [(i, (i + 1) % ndev) for i in range(ndev)]
    down = [(j, i) for i, j in up]
    before = lax.ppermute(flat[:, cdev - REACH:], AXES, up)
    after = lax.ppermute(flat[:, :REACH], AXES, down)
    sds = jax.ShapeDtypeStruct

    outgoing, dyn, hot = pl.pallas_call(
        functools.partial(pack_kernel, cap, slots, cdev * ndev),
        in_specs=[SMEM] + [VMEM] * 5,
        out_specs=[VMEM] * 3,
        out_shape=[sds((slots, 2 * rows), F32), sds((rows, cdev), F32), sds((slots, cdev), BF16)],
        compiler_params=pltpu.CompilerParams(vmem_limit_bytes=16 << 20),
        name="pack",
    )((me * cdev).reshape(1), flat, before, after, neighbors, owner.reshape(1, cdev))
    arrived = lax.all_to_all(outgoing.reshape(ndev, cap * 2 * rows), AXES, split_axis=0, concat_axis=0, tiled=True)
    arrived = arrived.reshape(slots, 2 * rows)

    block = 2 * GROUP * crmx
    count = levels * crmx // block
    take = lambda offset: pl.BlockSpec((slots, block), lambda g: (0, g + offset))
    big = sds((levels * crmx, slots), F32)
    prepared = pl.pallas_call(
        functools.partial(prepare_kernel, crmx),
        grid=(count,),
        in_specs=[take(0), take(count), take(0)],
        out_specs=[VMEM] * 4,
        out_shape=[big] * 4,
        compiler_params=pltpu.CompilerParams(vmem_limit_bytes=32 << 20),
        cost_estimate=pl.CostEstimate(flops=6 * slots * levels * crmx * GROUP * crmx, transcendentals=0, bytes_accessed=4 * slots * wide),
        name="prepare",
    )(crm_state, crm_state, phase_mask)

    back = pl.pallas_call(
        functools.partial(physics_kernel, levels, crmx),
        in_specs=[VMEM] * 5,
        out_specs=VMEM,
        out_shape=sds((slots, rows), F32),
        scratch_shapes=[
            pltpu.VMEM((slots // 128, 2 * SUB * levels + 8, 128), F32),
            pltpu.VMEM((slots // 128, 8 * rows, 128), F32),
        ],
        compiler_params=pltpu.CompilerParams(vmem_limit_bytes=32 << 20),
        name="physics",
    )(arrived, *prepared)
    back = lax.all_to_all(back.reshape(ndev, cap * rows), AXES, split_axis=0, concat_axis=0, tiled=True)
    back = back.reshape(slots, rows)
    out = pl.pallas_call(
        finish_kernel,
        in_specs=[VMEM] * 4,
        out_specs=VMEM,
        out_shape=sds((rows, cdev), F32),
        compiler_params=pltpu.CompilerParams(vmem_limit_bytes=16 << 20),
        name="finish",
    )(flat, dyn, hot, back)
    return out.reshape(state.shape)


def solution(mesh):
    return jax.shard_map(
        local,
        mesh=mesh,
        in_specs=(
            P(None, None, AXES),
            P(None, AXES),
            P(AXES, None),
            P(AXES, None),
            P(AXES, None),
        ),
        out_specs=P(None, None, AXES),
        check_vma=False,
    )
```

```python
import functools
import math

import jax
import jax.numpy as jnp
from jax import lax
from jax.experimental import pallas as pl
from jax.experimental.pallas import tpu as pltpu
from jax.sharding import PartitionSpec as P

SUB = 4
REACH = 8
GROUP = 4
AXES = ("sec", "blk")
F32 = jnp.float32
BF16 = jnp.bfloat16
NT = (((1,), (1,)), ((), ()))
NN = (((1,), (0,)), ((), ()))
TN = (((0,), (0,)), ((), ()))
VMEM = pl.BlockSpec(memory_space=pltpu.VMEM)
FULL = 60 * 1024 * 1024
SMEM = pl.BlockSpec(memory_space=pltpu.SMEM)


def parts_of(x):
    high = x.astype(BF16)
    rest = x - high.astype(F32)
    middle = rest.astype(BF16)
    low = (rest - middle.astype(F32)).astype(BF16)
    return high, middle, low


def select_dot(x, onehot, dims, flip=False):
    total = None
    for part in parts_of(x):
        pair = (onehot, part) if flip else (part, onehot)
        term = lax.dot_general(*pair, dims, preferred_element_type=F32)
        total = term if total is None else total + term
    return total


def index_kernel(plan, first_ref, state_ref, near_ref, owner_ref, same_ref, part_ref, edge_ref, hot_ref, place_ref):
    cap, slots, total, dense = plan
    cdev = state_ref.shape[1]
    index = near_ref[...] - (first_ref[0] - REACH)
    index = jnp.where(index < 0, index + total, index)
    index = jnp.where(index >= total, index - total, index)
    own = lax.broadcasted_iota(jnp.int32, (cdev, cdev), 0) + REACH
    edge = lax.broadcasted_iota(jnp.int32, (2 * REACH, cdev), 0)
    edge = jnp.where(edge < REACH, edge, edge + cdev)
    inner, outer = jnp.zeros((cdev, cdev), F32), jnp.zeros((2 * REACH, cdev), F32)
    for k in range(near_ref.shape[0]):
        row = index[k:k + 1, :]
        inner = inner + jnp.where(own == row, 1.0, 0.0)
        outer = outer + jnp.where(edge == row, 1.0, 0.0)
    edge_ref[...] = outer.astype(BF16)
    same_ref[...] = state_ref[...]
    part_ref[...] = select_dot(state_ref[...], inner.astype(BF16), NN)
    mine = jnp.broadcast_to(owner_ref[...], (cdev, cdev)).astype(F32)
    lower = lax.broadcasted_iota(jnp.int32, (cdev, cdev), 0) < lax.broadcasted_iota(jnp.int32, (cdev, cdev), 1)
    rank = jnp.sum(jnp.where((mine == mine.T) & lower, 1.0, 0.0), axis=0, keepdims=True).astype(jnp.int32)
    to = owner_ref[...]
    if dense is None:
        target = to * cap + rank
        place_ref[0:1, :] = target
        wanted = [target]
    else:
        tiles, back = dense
        rest = (rank * 32) // 128
        wanted = [to * (tiles * cap + 2) + t * cap + rank for t in range(tiles)]
        wanted += [jnp.where(rank % 4 == q, to * (tiles * cap + 2) + tiles * cap + rest, -1) for q in range(4)]
        for t in range(back):
            place_ref[t:t + 1, :] = to * (back * cap + 1) + t * cap + rank
        place_ref[back:back + 1, :] = to * (back * cap + 1) + back * cap
        place_ref[back + 1:back + 2, :] = rank
    rows = lax.broadcasted_iota(jnp.int32, (hot_ref.shape[0], cdev), 0)
    for i, row in enumerate(wanted):
        hot_ref[:, i * cdev:(i + 1) * cdev] = jnp.where(rows == row, 1.0, 0.0).astype(BF16)


def pack_kernel(dense, odd_ref, state_ref, part_ref, edge_ref, far_ref, mate_ref, hot_ref, out_ref, dyn_ref):
    rows = state_ref.shape[0]
    state = state_ref[...]
    odd = jnp.broadcast_to(odd_ref[0], far_ref.shape) == 1
    before = jnp.where(odd, mate_ref[...], far_ref[...])
    after = jnp.where(odd, far_ref[...], mate_ref[...])
    halo = select_dot(before, edge_ref[0:REACH], NN) + select_dot(after, edge_ref[REACH:2 * REACH], NN)
    dyn = 0.15 * ((part_ref[...] + halo) - 4.0 * state)
    dyn_ref[...] = dyn
    if dense is None:
        out_ref[:, 0:rows] = select_dot(state, hot_ref[...], NT, True)
        out_ref[:, rows:2 * rows] = select_dot(dyn, hot_ref[...], NT, True)
        return
    load = jnp.concatenate([state, dyn], axis=0)
    tail = load[dense[0] * 128:]
    blocks = [load[t * 128:(t + 1) * 128] for t in range(dense[0])]
    for q in range(4):
        blocks.append(jnp.concatenate([tail if i == q else jnp.zeros_like(tail) for i in range(4)], axis=0))
    out_ref[...] = select_dot(jnp.concatenate(blocks, axis=1), hot_ref[...], NT, True)


def prepare_kernel(crmx, ct_ref, cm_ref, mask_ref, yt_ref, ym_ref, rate_ref, both_ref):
    width = ct_ref.shape[1]
    per = GROUP * crmx
    row = lax.broadcasted_iota(jnp.int32, (per, per), 0)
    col = lax.broadcasted_iota(jnp.int32, (per, per), 1)
    place = row % crmx
    apart = (((place % 8) * (crmx // 8) + place // 8) - col) & (crmx - 1)
    same = (row // crmx) == (col // crmx)
    move = jnp.where(same & (apart == 0), 1.0, 0.0)
    spread = jnp.where(same & ((apart == 1) | (apart == crmx - 1)), 1.0, 3.0 * move)
    move, spread = move.astype(BF16), spread.astype(BF16)
    for q in range(width // per):
        part = slice(q * per, (q + 1) * per)
        yt_ref[part, :] = lax.dot_general(spread, ct_ref[:, part], NT, preferred_element_type=F32)
        ym_ref[part, :] = lax.dot_general(spread, cm_ref[:, part], NT, preferred_element_type=F32)
        ice = lax.dot_general(move, mask_ref[:, part].astype(F32).astype(BF16), NT, preferred_element_type=F32)
        rate_ref[part, :] = 0.7 - 0.4 * ice
        both_ref[part, :] = 0.7 - 0.31 * ice


def arrivals(dense, arrived_ref, slots, wide):
    columns = []
    if dense is None:
        for start in range(0, wide, 128):
            size = min(128, wide - start)
            block = arrived_ref[:, start:start + size]
            if size < 128:
                block = jnp.concatenate([block, jnp.zeros((slots, 128 - size), F32)], axis=1)
            columns.append(block.T[:size])
        return jnp.concatenate(columns, axis=0)
    tiles, cap = dense[0], 8
    each = tiles * cap + 2
    for t in range(tiles):
        block = [arrived_ref[s * each + t * cap:s * each + (t + 1) * cap, :] for s in range(slots // cap)]
        columns.append(jnp.concatenate(block, axis=0).T)
    low = lax.broadcasted_iota(jnp.int32, (cap, 128), 0) < 4
    block = []
    for s in range(slots // cap):
        pair = [arrived_ref[s * each + tiles * cap + i:s * each + tiles * cap + i + 1, :] for i in range(2)]
        block.append(jnp.where(low, *[jnp.broadcast_to(p, (cap, 128)) for p in pair]))
    tail = jnp.concatenate(block, axis=0).T
    which = lax.broadcasted_iota(jnp.int32, (32, slots), 1) % 4
    columns.append(sum(jnp.where(which == q, tail[q * 32:(q + 1) * 32], 0.0) for q in range(4)))
    return jnp.concatenate(columns, axis=0)


def physics_kernel(levels, crmx, dense, arrived_ref, yt_ref, ym_ref, rate_ref, both_ref, out_ref, rows_ref, sums_ref):
    slots = yt_ref.shape[1]
    steps = crmx // 8
    scale = 0.3 * math.log2(math.e)
    shift = [math.log(0.8 * 5.0 ** j) / 0.3 for j in range(SUB + 1)]
    step = pl.program_id(0)
    per = yt_ref.shape[0] // crmx

    @pl.when(step == 0)
    def _():
        arrived = arrivals(dense, arrived_ref, slots, 4 * levels)
        temp, moist, push, wet = [arrived[i * levels:(i + 1) * levels] for i in range(4)]
        push, wet = push * (1.0 / SUB), wet * (1.0 / SUB)
        tables = [5.0 * (temp + push + shift[1]), 5.0 * (moist + wet)]
        for j in range(2, SUB + 1):
            tables += [5.0 ** j * (push + (shift[j] - shift[j - 1])), 5.0 ** j * wet]
        for i, table in enumerate(tables):
            for half in range(slots // 128):
                rows_ref[half, i * levels:(i + 1) * levels] = table[:, half * 128:(half + 1) * 128]

    def unit(inner, half):
        lanes = pl.ds(half * 128, 128)
        base = inner * crmx
        level = step * per + inner
        get = lambda ref, k: ref[pl.ds(base + 8 * k, 8), lanes]
        const = lambda i: rows_ref[half, pl.ds(level + i * levels, 8, stride=0), :]
        add_t, add_m = const(0), const(1)
        temp = [get(yt_ref, k) + add_t for k in range(steps)]
        moist = [get(ym_ref, k) + add_m for k in range(steps)]
        for j in range(1, SUB + 1):
            if j > 1:
                spread = []
                for field, add in ((temp, const(2 * j - 2)), (moist, const(2 * j - 1))):
                    after = pltpu.roll(field[0], 7, 0)
                    before = pltpu.roll(field[steps - 1], 1, 0)
                    ring = [before] + field + [after]
                    spread.append([((ring[k] + ring[k + 2]) + 3.0 * field[k]) + add for k in range(steps)])
                temp, moist = spread
            temp, moist = list(temp), list(moist)
            for k in range(steps):
                over = jnp.maximum(moist[k] - jnp.exp2((scale / 5.0 ** j) * temp[k]), 0.0)
                moist[k] = moist[k] - get(rate_ref, k) * over
                temp[k] = temp[k] + get(both_ref, k) * over
        for i, field in enumerate((temp, moist)):
            while len(field) > 1:
                field = [a + b for a, b in zip(field[0::2], field[1::2])]
            sums_ref[half, pl.ds(pl.multiple_of((i * levels + level) * 8, 8), 8), :] = field[0]

    for inner in range(per):
        for half in range(slots // 128):
            unit(inner, half)

    @pl.when(step == pl.num_programs(0) - 1)
    def _():
        factor = 1.0 / (crmx * 5.0 ** SUB)
        total = 2 * levels
        for half in range(slots // 128):
            summed = sums_ref[half, pl.ds(0, total, stride=8), :]
            for s in range(1, 8):
                summed = summed + sums_ref[half, pl.ds(s, total, stride=8), :]
            mean = summed * factor
            mean = jnp.concatenate([mean[:levels] - shift[SUB], mean[levels:]], axis=0)
            if dense is None:
                mean = jnp.concatenate([mean, jnp.zeros((256 - total, 128), F32)], axis=0)
                out_ref[pl.ds(half * 128, 128), :] = mean.T[:, :total]
                continue
            back, cap = dense[1], 8
            each = back * cap + 1
            for t in range(back):
                block = mean[t * 128:(t + 1) * 128].T
                for s in range(128 // cap):
                    to = (half * (128 // cap) + s) * each + t * cap
                    out_ref[to:to + cap, :] = block[s * cap:(s + 1) * cap]
            tail = jnp.concatenate([mean[back * 128:]] * cap, axis=0).T
            group = lax.broadcasted_iota(jnp.int32, (128, 128), 1) // (128 // cap)
            tail = jnp.where(group == lax.broadcasted_iota(jnp.int32, (128, 128), 0) % cap, tail, 0.0)
            for s in range(128 // cap):
                to = (half * (128 // cap) + s) * each + back * cap
                out_ref[to:to + 1, :] = jnp.sum(tail[s * cap:(s + 1) * cap], axis=0, keepdims=True)


def finish_kernel(dense, dyn_ref, place_ref, back_ref, out_ref):
    cdev = dyn_ref.shape[1]
    rows = lax.broadcasted_iota(jnp.int32, (back_ref.shape[0], cdev), 0)
    count = 1 if dense is None else dense[1] + 1
    hot = [jnp.where(rows == place_ref[i:i + 1, :], 1.0, 0.0).astype(BF16) for i in range(count)]
    means = select_dot(back_ref[...], jnp.concatenate(hot, axis=1), TN)
    if dense is None:
        out_ref[...] = dyn_ref[...] + means
        return
    back = dense[1]
    for t in range(back):
        out_ref[t * 128:(t + 1) * 128] = dyn_ref[t * 128:(t + 1) * 128] + means[:, t * cdev:(t + 1) * cdev]
    tail = means[:, back * cdev:]
    size = dyn_ref.shape[0] - back * 128
    rank = place_ref[back + 1:back + 2, :]
    mine = sum(jnp.where(rank == q, tail[q * size:(q + 1) * size], 0.0) for q in range(128 // size))
    out_ref[back * 128:] = dyn_ref[back * 128:] + mine


def local(state, neighbors, owner, crm_state, phase_mask):
    ndev = lax.axis_size(AXES)
    me = lax.axis_index(AXES)
    fields, levels, cdev = state.shape
    rows = fields * levels
    slots, wide = crm_state.shape
    crmx = wide // rows
    cap = slots // ndev
    flat = state.reshape(rows, cdev)
    sds = jax.ShapeDtypeStruct
    dense = (2 * rows // 128, rows // 128) if cap == 8 and rows % 128 == 16 else None
    out_each, back_each = 2 * rows * cap // 128, rows * cap // 128
    far = [(i, (i + 1) % ndev if i % 2 else (i - 1) % ndev) for i in range(ndev)]
    mate = [(i, i ^ 1) for i in range(ndev)]
    odd = me % 2
    first, last = flat[:, :REACH], flat[:, cdev - REACH:]
    from_far = lax.ppermute(jnp.where(odd == 1, last, first), AXES, far)
    from_mate = lax.ppermute(jnp.where(odd == 1, first, last), AXES, mate)

    def whole(*shape):
        return pl.BlockSpec(shape, lambda i: (0,) * len(shape))

    if dense is None:
        hot_shape, places = (slots, cdev), 1
    else:
        hot_shape, places = (ndev * out_each, cdev * (dense[0] + 4)), dense[1] + 2
    same, part, edge, hot, place = pl.pallas_call(
        functools.partial(index_kernel, (cap, slots, cdev * ndev, dense)),
        grid=(1,),
        in_specs=[SMEM, whole(rows, cdev), whole(*neighbors.shape), whole(1, cdev)],
        out_specs=[VMEM] * 5,
        out_shape=[sds((rows, cdev), F32)] * 2 + [sds((2 * REACH, cdev), BF16), sds(hot_shape, BF16), sds((places, cdev), jnp.int32)],
        compiler_params=pltpu.CompilerParams(vmem_limit_bytes=12 << 20),
        name="index",
    )((me * cdev).reshape(1), flat, neighbors, owner.reshape(1, cdev))
    outgoing, dyn = pl.pallas_call(
        functools.partial(pack_kernel, dense),
        in_specs=[SMEM] + [VMEM] * 6,
        out_specs=[VMEM] * 2,
        out_shape=[sds((slots, 2 * rows) if dense is None else (ndev * out_each, 128), F32), sds((rows, cdev), F32)],
        compiler_params=pltpu.CompilerParams(vmem_limit_bytes=12 << 20),
        name="pack",
    )(odd.reshape(1), same, part, edge, from_far, from_mate, hot)
    arrived = lax.all_to_all(outgoing.reshape(ndev, cap * 2 * rows), AXES, split_axis=0, concat_axis=0, tiled=True)
    arrived = arrived.reshape(outgoing.shape)

    block = 2 * GROUP * crmx
    count = levels * crmx // block
    take = lambda offset: pl.BlockSpec((slots, block), lambda g: (0, g + offset))
    big = sds((levels * crmx, slots), F32)
    prepared = pl.pallas_call(
        functools.partial(prepare_kernel, crmx),
        grid=(count,),
        in_specs=[take(0), take(count), take(0)],
        out_specs=[pl.BlockSpec((block, slots), lambda g: (g, 0))] * 4,
        out_shape=[big] * 4,
        compiler_params=pltpu.CompilerParams(vmem_limit_bytes=FULL),
        cost_estimate=pl.CostEstimate(flops=6 * slots * levels * crmx * GROUP * crmx, transcendentals=0, bytes_accessed=4 * slots * wide),
        name="prepare",
    )(crm_state, crm_state, phase_mask)

    back = pl.pallas_call(
        functools.partial(physics_kernel, levels, crmx, dense),
        grid=(count,),
        in_specs=[VMEM] + [pl.BlockSpec((block, slots), lambda g: (g, 0))] * 4,
        out_specs=VMEM,
        out_shape=sds((slots, rows) if dense is None else (ndev * back_each, 128), F32),
        scratch_shapes=[
            pltpu.VMEM((slots // 128, 2 * SUB * levels + 8, 128), F32),
            pltpu.VMEM((slots // 128, 8 * rows, 128), F32),
        ],
        compiler_params=pltpu.CompilerParams(vmem_limit_bytes=53000 << 10),
        name="physics",
    )(arrived, *prepared)
    returned = lax.all_to_all(back.reshape(ndev, cap * rows), AXES, split_axis=0, concat_axis=0, tiled=True)
    out = pl.pallas_call(
        functools.partial(finish_kernel, dense),
        in_specs=[VMEM] * 3,
        out_specs=VMEM,
        out_shape=sds((rows, cdev), F32),
        compiler_params=pltpu.CompilerParams(vmem_limit_bytes=12 << 20),
        name="finish",
    )(dyn, place, returned.reshape(back.shape))
    return out.reshape(state.shape)


def solution(mesh):
    return jax.shard_map(
        local,
        mesh=mesh,
        in_specs=(
            P(None, None, AXES),
            P(None, AXES),
            P(AXES, None),
            P(AXES, None),
            P(AXES, None),
        ),
        out_specs=P(None, None, AXES),
        check_vma=False,
    )
```

```python
import functools
import math

import jax
import jax.numpy as jnp
from jax import lax
from jax.experimental import pallas as pl
from jax.experimental.pallas import tpu as pltpu
from jax.sharding import PartitionSpec as P

SUB = 4
REACH = 8
GROUP = 4
AXES = ("sec", "blk")
F32 = jnp.float32
BF16 = jnp.bfloat16
NT = (((1,), (1,)), ((), ()))
NN = (((1,), (0,)), ((), ()))
TN = (((0,), (0,)), ((), ()))
VMEM = pl.BlockSpec(memory_space=pltpu.VMEM)
FULL = 60 * 1024 * 1024


def parts_of(x):
    high = x.astype(BF16)
    rest = x - high.astype(F32)
    middle = rest.astype(BF16)
    low = (rest - middle.astype(F32)).astype(BF16)
    return high, middle, low


def select_dot(x, onehot, dims, flip=False):
    axis = 1 - dims[0][1 if flip else 0][0]
    size = x.shape[axis]
    wide = jnp.concatenate(parts_of(x), axis=axis)
    pair = (onehot, wide) if flip else (wide, onehot)
    out = lax.dot_general(*pair, dims, preferred_element_type=F32)
    cut = (lambda i: out[:, i * size:(i + 1) * size]) if flip else (lambda i: out[i * size:(i + 1) * size])
    return (cut(0) + cut(1)) + cut(2)


def index_kernel(plan, state_ref, near_ref, owner_ref, same_ref, part_ref, edge_ref, hot_ref, place_ref, *tail_ref):
    cap, slots, total, dense = plan
    cdev = state_ref.shape[1]
    index = near_ref[...] - (lax.axis_index(AXES) * cdev - REACH)
    index = jnp.where(index < 0, index + total, index)
    index = jnp.where(index >= total, index - total, index)
    own = lax.broadcasted_iota(jnp.int32, (cdev, cdev), 0) + REACH
    edge = lax.broadcasted_iota(jnp.int32, (2 * REACH, cdev), 0)
    edge = jnp.where(edge < REACH, edge, edge + cdev)
    inner, outer = jnp.zeros((cdev, cdev), F32), jnp.zeros((2 * REACH, cdev), F32)
    for k in range(near_ref.shape[0]):
        row = index[k:k + 1, :]
        inner = inner + jnp.where(own == row, 1.0, 0.0)
        outer = outer + jnp.where(edge == row, 1.0, 0.0)
    edge_ref[...] = outer.astype(BF16)
    same_ref[...] = state_ref[...]
    part_ref[...] = select_dot(state_ref[...], inner.astype(BF16), NN)
    mine = jnp.broadcast_to(owner_ref[...], (cdev, cdev)).astype(F32)
    lower = lax.broadcasted_iota(jnp.int32, (cdev, cdev), 0) < lax.broadcasted_iota(jnp.int32, (cdev, cdev), 1)
    rank = jnp.sum(jnp.where((mine == mine.T) & lower, 1.0, 0.0), axis=0, keepdims=True).astype(jnp.int32)
    to = owner_ref[...]
    target = to * cap + rank
    rows = lax.broadcasted_iota(jnp.int32, (slots, cdev), 0)
    hot_ref[...] = jnp.where(rows == target, 1.0, 0.0).astype(BF16)
    if dense is None:
        place_ref[0:1, :] = target
        return
    back = dense[1]
    for t in range(back):
        place_ref[t:t + 1, :] = to * (back * cap + 1) + t * cap + rank
    place_ref[back:back + 1, :] = to * (back * cap + 1) + back * cap
    place_ref[back + 1:back + 2, :] = rank
    rows = lax.broadcasted_iota(jnp.int32, (slots // 4, cdev), 0) * 4
    for q in range(4):
        tail_ref[0][:, q * cdev:(q + 1) * cdev] = jnp.where(rows + q == target, 1.0, 0.0).astype(BF16)


def pack_kernel(dense, state_ref, part_ref, edge_ref, hot_ref, far_ref, mate_ref, *refs):
    out_ref, dyn_ref = refs[-2:]
    rows = state_ref.shape[0]
    state = state_ref[...]
    odd = jnp.broadcast_to(lax.axis_index(AXES) % 2, far_ref.shape) == 1
    before = jnp.where(odd, mate_ref[...], far_ref[...])
    after = jnp.where(odd, far_ref[...], mate_ref[...])
    halo = select_dot(before, edge_ref[0:REACH], NN) + select_dot(after, edge_ref[REACH:2 * REACH], NN)
    dyn = 0.15 * ((part_ref[...] + halo) - 4.0 * state)
    dyn_ref[...] = dyn
    if dense is None:
        out_ref[:, 0:rows] = select_dot(state, hot_ref[...], NT, True)
        out_ref[:, rows:2 * rows] = select_dot(dyn, hot_ref[...], NT, True)
        return
    load = jnp.concatenate([state, dyn], axis=0)
    tiles, cap = dense[0], 8
    each = tiles * cap + 2
    main = select_dot(load[:tiles * 128], hot_ref[...], NT, True)
    tail = load[tiles * 128:]
    blank = jnp.zeros_like(tail)
    tail = [jnp.concatenate([tail if i == q else blank for i in range(4)], axis=0) for q in range(4)]
    tail = select_dot(jnp.concatenate(tail, axis=1), refs[0][...], NT, True)
    for s in range(hot_ref.shape[0] // cap):
        for t in range(tiles):
            out_ref[s * each + t * cap:s * each + (t + 1) * cap, :] = main[s * cap:(s + 1) * cap, t * 128:(t + 1) * 128]
        out_ref[s * each + tiles * cap:(s + 1) * each, :] = tail[2 * s:2 * s + 2]


def prepare_kernel(crmx, ct_ref, cm_ref, mask_ref, yt_ref, ym_ref, rate_ref, both_ref):
    width = ct_ref.shape[1]
    per = GROUP * crmx
    row = lax.broadcasted_iota(jnp.int32, (per, per), 0)
    col = lax.broadcasted_iota(jnp.int32, (per, per), 1)
    place = row % crmx
    apart = (((place % 8) * (crmx // 8) + place // 8) - col) & (crmx - 1)
    same = (row // crmx) == (col // crmx)
    move = jnp.where(same & (apart == 0), 1.0, 0.0)
    spread = jnp.where(same & ((apart == 1) | (apart == crmx - 1)), 1.0, 3.0 * move)
    move, spread = move.astype(BF16), spread.astype(BF16)
    for q in range(width // per):
        part = slice(q * per, (q + 1) * per)
        yt_ref[part, :] = lax.dot_general(spread, ct_ref[:, part], NT, preferred_element_type=F32)
        ym_ref[part, :] = lax.dot_general(spread, cm_ref[:, part], NT, preferred_element_type=F32)
        ice = lax.dot_general(move, mask_ref[:, part].astype(F32).astype(BF16), NT, preferred_element_type=F32)
        rate_ref[part, :] = 0.7 - 0.4 * ice
        both_ref[part, :] = 0.7 - 0.31 * ice


def arrivals(dense, arrived_ref, slots, wide):
    columns = []
    if dense is None:
        for start in range(0, wide, 128):
            size = min(128, wide - start)
            block = arrived_ref[:, start:start + size]
            if size < 128:
                block = jnp.concatenate([block, jnp.zeros((slots, 128 - size), F32)], axis=1)
            columns.append(block.T[:size])
        return jnp.concatenate(columns, axis=0)
    tiles, cap = dense[0], 8
    each = tiles * cap + 2
    for t in range(tiles):
        block = [arrived_ref[s * each + t * cap:s * each + (t + 1) * cap, :] for s in range(slots // cap)]
        columns.append(jnp.concatenate(block, axis=0).T)
    low = lax.broadcasted_iota(jnp.int32, (cap, 128), 0) < 4
    block = []
    for s in range(slots // cap):
        pair = [arrived_ref[s * each + tiles * cap + i:s * each + tiles * cap + i + 1, :] for i in range(2)]
        block.append(jnp.where(low, *[jnp.broadcast_to(p, (cap, 128)) for p in pair]))
    tail = jnp.concatenate(block, axis=0).T
    which = lax.broadcasted_iota(jnp.int32, (32, slots), 1) % 4
    columns.append(sum(jnp.where(which == q, tail[q * 32:(q + 1) * 32], 0.0) for q in range(4)))
    return jnp.concatenate(columns, axis=0)


def physics_kernel(levels, crmx, dense, arrived_ref, yt_ref, ym_ref, rate_ref, both_ref, out_ref, rows_ref, sums_ref):
    slots = yt_ref.shape[1]
    steps = crmx // 8
    scale = 0.3 * math.log2(math.e)
    shift = [math.log(0.8 * 5.0 ** j) / 0.3 for j in range(SUB + 1)]
    step = pl.program_id(0)
    per = yt_ref.shape[0] // crmx

    @pl.when(step == 0)
    def _():
        arrived = arrivals(dense, arrived_ref, slots, 4 * levels)
        temp, moist, push, wet = [arrived[i * levels:(i + 1) * levels] for i in range(4)]
        push, wet = push * (1.0 / SUB), wet * (1.0 / SUB)
        tables = [5.0 * (temp + push + shift[1]), 5.0 * (moist + wet)]
        for j in range(2, SUB + 1):
            tables += [5.0 ** j * (push + (shift[j] - shift[j - 1])), 5.0 ** j * wet]
        for i, table in enumerate(tables):
            for half in range(slots // 128):
                rows_ref[half, i * levels:(i + 1) * levels] = table[:, half * 128:(half + 1) * 128]

    def unit(inner, half):
        lanes = pl.ds(half * 128, 128)
        base = inner * crmx
        level = step * per + inner
        get = lambda ref, k: ref[pl.ds(base + 8 * k, 8), lanes]
        const = lambda i: rows_ref[half, pl.ds(level + i * levels, 8, stride=0), :]
        add_t, add_m = const(0), const(1)
        temp = [get(yt_ref, k) + add_t for k in range(steps)]
        moist = [get(ym_ref, k) + add_m for k in range(steps)]
        for j in range(1, SUB + 1):
            if j > 1:
                spread = []
                for field, add in ((temp, const(2 * j - 2)), (moist, const(2 * j - 1))):
                    after = pltpu.roll(field[0], 7, 0)
                    before = pltpu.roll(field[steps - 1], 1, 0)
                    ring = [before] + field + [after]
                    spread.append([((ring[k] + ring[k + 2]) + 3.0 * field[k]) + add for k in range(steps)])
                temp, moist = spread
            temp, moist = list(temp), list(moist)
            for k in range(steps):
                over = jnp.maximum(moist[k] - jnp.exp2((scale / 5.0 ** j) * temp[k]), 0.0)
                moist[k] = moist[k] - get(rate_ref, k) * over
                temp[k] = temp[k] + get(both_ref, k) * over
        for i, field in enumerate((temp, moist)):
            while len(field) > 1:
                field = [a + b for a, b in zip(field[0::2], field[1::2])]
            sums_ref[half, pl.ds(pl.multiple_of((i * levels + level) * 8, 8), 8), :] = field[0]

    for inner in range(per):
        for half in range(slots // 128):
            unit(inner, half)

    @pl.when(step == pl.num_programs(0) - 1)
    def _():
        factor = 1.0 / (crmx * 5.0 ** SUB)
        total = 2 * levels
        for half in range(slots // 128):
            summed = sums_ref[half, pl.ds(0, total, stride=8), :]
            for s in range(1, 8):
                summed = summed + sums_ref[half, pl.ds(s, total, stride=8), :]
            mean = summed * factor
            mean = jnp.concatenate([mean[:levels] - shift[SUB], mean[levels:]], axis=0)
            if dense is None:
                mean = jnp.concatenate([mean, jnp.zeros((256 - total, 128), F32)], axis=0)
                out_ref[pl.ds(half * 128, 128), :] = mean.T[:, :total]
                continue
            back, cap = dense[1], 8
            each = back * cap + 1
            for t in range(back):
                block = mean[t * 128:(t + 1) * 128].T
                for s in range(128 // cap):
                    to = (half * (128 // cap) + s) * each + t * cap
                    out_ref[to:to + cap, :] = block[s * cap:(s + 1) * cap]
            tail = jnp.concatenate([mean[back * 128:]] * cap, axis=0).T
            group = lax.broadcasted_iota(jnp.int32, (128, 128), 1) // (128 // cap)
            tail = jnp.where(group == lax.broadcasted_iota(jnp.int32, (128, 128), 0) % cap, tail, 0.0)
            for s in range(128 // cap):
                to = (half * (128 // cap) + s) * each + back * cap
                out_ref[to:to + 1, :] = jnp.sum(tail[s * cap:(s + 1) * cap], axis=0, keepdims=True)


def finish_kernel(dense, dyn_ref, place_ref, back_ref, out_ref):
    cdev = dyn_ref.shape[1]
    rows = lax.broadcasted_iota(jnp.int32, (back_ref.shape[0], cdev), 0)
    count = 1 if dense is None else dense[1] + 1
    hot = [jnp.where(rows == place_ref[i:i + 1, :], 1.0, 0.0).astype(BF16) for i in range(count)]
    means = select_dot(back_ref[...], jnp.concatenate(hot, axis=1), TN)
    if dense is None:
        out_ref[...] = dyn_ref[...] + means
        return
    back = dense[1]
    for t in range(back):
        out_ref[t * 128:(t + 1) * 128] = dyn_ref[t * 128:(t + 1) * 128] + means[:, t * cdev:(t + 1) * cdev]
    tail = means[:, back * cdev:]
    size = dyn_ref.shape[0] - back * 128
    rank = place_ref[back + 1:back + 2, :]
    mine = sum(jnp.where(rank == q, tail[q * size:(q + 1) * size], 0.0) for q in range(128 // size))
    out_ref[back * 128:] = dyn_ref[back * 128:] + mine


def local(state, neighbors, owner, crm_state, phase_mask):
    ndev = lax.axis_size(AXES)
    me = lax.axis_index(AXES)
    fields, levels, cdev = state.shape
    rows = fields * levels
    slots, wide = crm_state.shape
    crmx = wide // rows
    cap = slots // ndev
    flat = state.reshape(rows, cdev)
    sds = jax.ShapeDtypeStruct
    dense = (2 * rows // 128, rows // 128) if cap == 8 and rows % 128 == 16 else None
    out_each, back_each = 2 * rows * cap // 128, rows * cap // 128
    far = [(i, (i + 1) % ndev if i % 2 else (i - 1) % ndev) for i in range(ndev)]
    mate = [(i, i ^ 1) for i in range(ndev)]
    odd = me % 2
    first, last = flat[:, :REACH], flat[:, cdev - REACH:]
    from_far = lax.ppermute(jnp.where(odd == 1, last, first), AXES, far)
    from_mate = lax.ppermute(jnp.where(odd == 1, first, last), AXES, mate)

    def whole(*shape):
        return pl.BlockSpec(shape, lambda i: (0,) * len(shape))

    index_out = [sds((rows, cdev), F32)] * 2 + [sds((2 * REACH, cdev), BF16), sds((slots, cdev), BF16)]
    index_out.append(sds((1 if dense is None else dense[1] + 2, cdev), jnp.int32))
    if dense is not None:
        index_out.append(sds((slots // 4, 4 * cdev), BF16))
    same, part, edge, hot, place, *tail = pl.pallas_call(
        functools.partial(index_kernel, (cap, slots, cdev * ndev, dense)),
        grid=(1,),
        in_specs=[whole(rows, cdev), whole(*neighbors.shape), whole(1, cdev)],
        out_specs=[VMEM] * len(index_out),
        out_shape=index_out,
        compiler_params=pltpu.CompilerParams(vmem_limit_bytes=12 << 20),
        name="index",
    )(flat, neighbors, owner.reshape(1, cdev))
    outgoing, dyn = pl.pallas_call(
        functools.partial(pack_kernel, dense),
        in_specs=[VMEM] * (6 + len(tail)),
        out_specs=[VMEM] * 2,
        out_shape=[sds((slots, 2 * rows) if dense is None else (ndev * out_each, 128), F32), sds((rows, cdev), F32)],
        compiler_params=pltpu.CompilerParams(vmem_limit_bytes=12 << 20),
        name="pack",
    )(same, part, edge, hot, from_far, from_mate, *tail)
    arrived = lax.all_to_all(outgoing.reshape(ndev, cap * 2 * rows), AXES, split_axis=0, concat_axis=0, tiled=True)
    arrived = arrived.reshape(outgoing.shape)

    block = 3 * GROUP * crmx
    count = levels * crmx // block
    take = lambda offset: pl.BlockSpec((slots, block), lambda g: (0, g + offset))
    big = sds((levels * crmx, slots), F32)
    prepared = pl.pallas_call(
        functools.partial(prepare_kernel, crmx),
        grid=(count,),
        in_specs=[take(0), take(count), take(0)],
        out_specs=[pl.BlockSpec((block, slots), lambda g: (g, 0))] * 4,
        out_shape=[big] * 4,
        compiler_params=pltpu.CompilerParams(vmem_limit_bytes=FULL),
        cost_estimate=pl.CostEstimate(flops=6 * slots * levels * crmx * GROUP * crmx, transcendentals=0, bytes_accessed=4 * slots * wide),
        name="prepare",
    )(crm_state, crm_state, phase_mask)

    back = pl.pallas_call(
        functools.partial(physics_kernel, levels, crmx, dense),
        grid=(count,),
        in_specs=[VMEM] + [pl.BlockSpec((block, slots), lambda g: (g, 0))] * 4,
        out_specs=VMEM,
        out_shape=sds((slots, rows) if dense is None else (ndev * back_each, 128), F32),
        scratch_shapes=[
            pltpu.VMEM((slots // 128, 2 * SUB * levels + 8, 128), F32),
            pltpu.VMEM((slots // 128, 8 * rows, 128), F32),
        ],
        compiler_params=pltpu.CompilerParams(vmem_limit_bytes=53000 << 10),
        name="physics",
    )(arrived, *prepared)
    returned = lax.all_to_all(back.reshape(ndev, cap * rows), AXES, split_axis=0, concat_axis=0, tiled=True)
    out = pl.pallas_call(
        functools.partial(finish_kernel, dense),
        in_specs=[VMEM] * 3,
        out_specs=VMEM,
        out_shape=sds((rows, cdev), F32),
        compiler_params=pltpu.CompilerParams(vmem_limit_bytes=12 << 20),
        name="finish",
    )(dyn, place, returned.reshape(back.shape))
    return out.reshape(state.shape)


def solution(mesh):
    return jax.shard_map(
        local,
        mesh=mesh,
        in_specs=(
            P(None, None, AXES),
            P(None, AXES),
            P(AXES, None),
            P(AXES, None),
            P(AXES, None),
        ),
        out_specs=P(None, None, AXES),
        check_vma=False,
    )
```

```python
import functools
import math

import jax
import jax.numpy as jnp
from jax import lax
from jax.experimental import pallas as pl
from jax.experimental.pallas import tpu as pltpu
from jax.sharding import PartitionSpec as P

SUB = 4
REACH = 8
GROUP = 4
AXES = ("sec", "blk")
F32 = jnp.float32
BF16 = jnp.bfloat16
NT = (((1,), (1,)), ((), ()))
NN = (((1,), (0,)), ((), ()))
TN = (((0,), (0,)), ((), ()))
VMEM = pl.BlockSpec(memory_space=pltpu.VMEM)
FULL = 60 * 1024 * 1024
LOG = 0.3 * math.log2(math.e)
TRIO = 3


def parts_of(x):
    high = x.astype(BF16)
    rest = x - high.astype(F32)
    middle = rest.astype(BF16)
    low = (rest - middle.astype(F32)).astype(BF16)
    return high, middle, low


def select_dot(x, onehot, dims, flip=False):
    axis = 1 - dims[0][1 if flip else 0][0]
    size = x.shape[axis]
    wide = jnp.concatenate(parts_of(x), axis=axis)
    pair = (onehot, wide) if flip else (wide, onehot)
    out = lax.dot_general(*pair, dims, preferred_element_type=F32)
    cut = (lambda i: out[:, i * size:(i + 1) * size]) if flip else (lambda i: out[i * size:(i + 1) * size])
    return (cut(0) + cut(1)) + cut(2)


def index_kernel(plan, state_ref, near_ref, owner_ref, same_ref, part_ref, edge_ref, hot_ref, place_ref, *tail_ref):
    cap, slots, total, dense = plan
    cdev = state_ref.shape[1]
    index = near_ref[...] - (lax.axis_index(AXES) * cdev - REACH)
    index = jnp.where(index < 0, index + total, index)
    index = jnp.where(index >= total, index - total, index)
    own = lax.broadcasted_iota(jnp.int32, (cdev, cdev), 0) + REACH
    edge = lax.broadcasted_iota(jnp.int32, (2 * REACH, cdev), 0)
    edge = jnp.where(edge < REACH, edge, edge + cdev)
    inner, outer = jnp.zeros((cdev, cdev), F32), jnp.zeros((2 * REACH, cdev), F32)
    for k in range(near_ref.shape[0]):
        row = index[k:k + 1, :]
        inner = inner + jnp.where(own == row, 1.0, 0.0)
        outer = outer + jnp.where(edge == row, 1.0, 0.0)
    edge_ref[...] = outer.astype(BF16)
    same_ref[...] = state_ref[...]
    part_ref[...] = select_dot(state_ref[...], inner.astype(BF16), NN)
    mine = jnp.broadcast_to(owner_ref[...], (cdev, cdev)).astype(F32)
    lower = lax.broadcasted_iota(jnp.int32, (cdev, cdev), 0) < lax.broadcasted_iota(jnp.int32, (cdev, cdev), 1)
    rank = jnp.sum(jnp.where((mine == mine.T) & lower, 1.0, 0.0), axis=0, keepdims=True).astype(jnp.int32)
    to = owner_ref[...]
    target = to * cap + rank
    rows = lax.broadcasted_iota(jnp.int32, (slots, cdev), 0)
    hot_ref[...] = jnp.where(rows == target, 1.0, 0.0).astype(BF16)
    if dense is None:
        place_ref[0:1, :] = target
        return
    back = dense[1]
    for t in range(back):
        place_ref[t:t + 1, :] = to * (back * cap + 1) + t * cap + rank
    place_ref[back:back + 1, :] = to * (back * cap + 1) + back * cap
    place_ref[back + 1:back + 2, :] = rank
    rows = lax.broadcasted_iota(jnp.int32, (slots // 4, cdev), 0) * 4
    for q in range(4):
        tail_ref[0][:, q * cdev:(q + 1) * cdev] = jnp.where(rows + q == target, 1.0, 0.0).astype(BF16)


def pack_kernel(dense, state_ref, part_ref, edge_ref, hot_ref, far_ref, mate_ref, *refs):
    out_ref, dyn_ref = refs[-2:]
    rows = state_ref.shape[0]
    state = state_ref[...]
    odd = jnp.broadcast_to(lax.axis_index(AXES) % 2, far_ref.shape) == 1
    before = jnp.where(odd, mate_ref[...], far_ref[...])
    after = jnp.where(odd, far_ref[...], mate_ref[...])
    halo = select_dot(before, edge_ref[0:REACH], NN) + select_dot(after, edge_ref[REACH:2 * REACH], NN)
    dyn = 0.15 * ((part_ref[...] + halo) - 4.0 * state)
    dyn_ref[...] = dyn
    if dense is None:
        out_ref[:, 0:rows] = select_dot(state, hot_ref[...], NT, True)
        out_ref[:, rows:2 * rows] = select_dot(dyn, hot_ref[...], NT, True)
        return
    load = jnp.concatenate([state, dyn], axis=0)
    tiles, cap = dense[0], 8
    each = tiles * cap + 2
    main = select_dot(load[:tiles * 128], hot_ref[...], NT, True)
    tail = load[tiles * 128:]
    blank = jnp.zeros_like(tail)
    tail = [jnp.concatenate([tail if i == q else blank for i in range(4)], axis=0) for q in range(4)]
    tail = select_dot(jnp.concatenate(tail, axis=1), refs[0][...], NT, True)
    for s in range(hot_ref.shape[0] // cap):
        for t in range(tiles):
            out_ref[s * each + t * cap:s * each + (t + 1) * cap, :] = main[s * cap:(s + 1) * cap, t * 128:(t + 1) * 128]
        out_ref[s * each + tiles * cap:(s + 1) * each, :] = tail[2 * s:2 * s + 2]


def near_matrix(rows, columns, crmx, centre, side):
    row = lax.broadcasted_iota(jnp.int32, (rows, columns), 0)
    col = lax.broadcasted_iota(jnp.int32, (rows, columns), 1)
    apart = (row - col) & (crmx - 1)
    same = (row // crmx) == (col // crmx)
    off = jnp.where((apart == 1) | (apart == crmx - 1), side, 0.0)
    return jnp.where(same, jnp.where(apart == 0, centre, off), 0.0)


def prepare_kernel(crmx, mask_ref, rate_ref, both_ref):
    per = GROUP * crmx
    move = near_matrix(per, per, crmx, 1.0, 0.0).astype(BF16)
    for q in range(mask_ref.shape[1] // per):
        part = slice(q * per, (q + 1) * per)
        ice = lax.dot_general(move, mask_ref[:, part].astype(F32).astype(BF16), NT, preferred_element_type=F32)
        rate_ref[part, :] = 0.7 - 0.4 * ice
        both_ref[part, :] = 0.7 * LOG - (0.31 * LOG) * ice


def arrivals(dense, arrived_ref, slots, wide):
    columns = []
    if dense is None:
        for start in range(0, wide, 128):
            size = min(128, wide - start)
            block = arrived_ref[:, start:start + size]
            if size < 128:
                block = jnp.concatenate([block, jnp.zeros((slots, 128 - size), F32)], axis=1)
            columns.append(block.T[:size])
        return jnp.concatenate(columns, axis=0)
    tiles, cap = dense[0], 8
    each = tiles * cap + 2
    for t in range(tiles):
        block = [arrived_ref[s * each + t * cap:s * each + (t + 1) * cap, :] for s in range(slots // cap)]
        columns.append(jnp.concatenate(block, axis=0).T)
    low = lax.broadcasted_iota(jnp.int32, (cap, 128), 0) < 4
    block = []
    for s in range(slots // cap):
        pair = [arrived_ref[s * each + tiles * cap + i:s * each + tiles * cap + i + 1, :] for i in range(2)]
        block.append(jnp.where(low, *[jnp.broadcast_to(p, (cap, 128)) for p in pair]))
    tail = jnp.concatenate(block, axis=0).T
    which = lax.broadcasted_iota(jnp.int32, (32, slots), 1) % 4
    columns.append(sum(jnp.where(which == q, tail[q * 32:(q + 1) * 32], 0.0) for q in range(4)))
    return jnp.concatenate(columns, axis=0)


def physics_kernel(levels, crmx, dense, arrived_ref, ct_ref, cm_ref, rate_ref, both_ref, out_ref, *scratch):
    rows_ref, sums_ref, t_ref, m_ref, bt_ref, bm_ref, ft_ref, fm_ref, w_ref = scratch
    slots = ct_ref.shape[0]
    halves = slots // 128
    step = pl.program_id(0)
    here = rate_ref.shape[0] // crmx
    deep = TRIO * crmx
    shift = math.log2(0.8)

    @pl.when(step == 0)
    def _():
        arrived = arrivals(dense, arrived_ref, slots, 4 * levels)
        temp, moist, push, wet = [arrived[i * levels:(i + 1) * levels] for i in range(4)]
        push, wet = push * (1.0 / SUB), wet * (1.0 / SUB)
        for i, table in enumerate((LOG * (temp + push) + shift, moist + wet)):
            for half in range(halves):
                rows_ref[half, i * levels:(i + 1) * levels] = table[:, half * 128:(half + 1) * 128]
        for ref, force in ((ft_ref, LOG * push), (fm_ref, wet)):
            high = force.astype(BF16).astype(F32)
            low = force - high
            blank = jnp.zeros((16 - 2 * TRIO, slots), F32)
            for g in range(levels // TRIO):
                cut = slice(g * TRIO, (g + 1) * TRIO)
                ref[g * 16:(g + 1) * 16, :] = jnp.concatenate([high[cut], low[cut], blank], axis=0).astype(BF16)
        w_ref[:, :deep] = near_matrix(deep, deep, crmx, -0.4, 0.2).astype(BF16)
        row = lax.broadcasted_iota(jnp.int32, (deep, 16), 0) // crmx
        col = lax.broadcasted_iota(jnp.int32, (deep, 16), 1)
        w_ref[:, deep:] = jnp.where((col < 2 * TRIO) & (row == col % TRIO), 1.0, 0.0).astype(BF16)

    first = near_matrix(GROUP * crmx, GROUP * crmx, crmx, 3.0, 1.0).astype(BF16)
    for q in range(here // GROUP):
        part = slice(q * GROUP * crmx, (q + 1) * GROUP * crmx)
        t_ref[part, :] = lax.dot_general(first, ct_ref[:, part], NT, preferred_element_type=F32)
        m_ref[part, :] = lax.dot_general(first, cm_ref[:, part], NT, preferred_element_type=F32)

    def spread(group):
        rows = slice(group * deep, (group + 1) * deep)
        at = pl.ds(pl.multiple_of((step * (here // TRIO) + group) * 16, 16), 16)
        weights = w_ref[...]
        return [
            lax.dot_general(weights, jnp.concatenate([b_ref[rows, :], f_ref[at, :]], axis=0), NN, preferred_element_type=F32)
            for b_ref, f_ref in ((bt_ref, ft_ref), (bm_ref, fm_ref))
        ]

    def advance(group, sub, moved):
        for level in range(TRIO):
            inner = group * TRIO + level
            for half in range(halves):
                lanes = slice(half * 128, (half + 1) * 128)
                if sub == 1:
                    add_t, add_m = [
                        rows_ref[half, pl.ds(step * here + inner + i * levels, 8, stride=0), :] for i in range(2)
                    ]
                ends = [[], []]
                for k in range(0, crmx, 16):
                    pair = [[], []]
                    for i in (k, k + 8):
                        at = slice(inner * crmx + i, inner * crmx + i + 8)
                        temp, moist = t_ref[at, lanes], m_ref[at, lanes]
                        if sub == 1:
                            temp, moist = temp * (LOG * 0.2) + add_t, moist * 0.2 + add_m
                        else:
                            local_at = slice(level * crmx + i, level * crmx + i + 8)
                            temp, moist = temp + moved[0][local_at, lanes], moist + moved[1][local_at, lanes]
                        over = jnp.maximum(moist - jnp.exp2(temp), 0.0)
                        moist = moist - rate_ref[at, lanes] * over
                        temp = temp + both_ref[at, lanes] * over
                        if sub < SUB:
                            t_ref[at, lanes], m_ref[at, lanes] = temp, moist
                        pair[0].append(temp)
                        pair[1].append(moist)
                    if sub < SUB:
                        wide = slice(inner * crmx + k, inner * crmx + k + 16)
                        bt_ref[wide, lanes] = jnp.concatenate(pair[0], axis=0).astype(BF16)
                        bm_ref[wide, lanes] = jnp.concatenate(pair[1], axis=0).astype(BF16)
                    else:
                        for i in range(2):
                            ends[i].append(pair[i][0] + pair[i][1])
                if sub == SUB:
                    for i, field in enumerate(ends):
                        while len(field) > 1:
                            field = [a + b for a, b in zip(field[0::2], field[1::2])]
                        at = pl.ds(pl.multiple_of((i * levels + step * here + inner) * 8, 8), 8)
                        sums_ref[half, at, :] = field[0]

    for pair in range(0, here // TRIO, 2):
        moved = [None, None]
        for sub in range(1, SUB + 1):
            for i in range(2):
                advance(pair + i, sub, moved[i])
                if sub < SUB:
                    moved[i] = spread(pair + i)

    @pl.when(step == pl.num_programs(0) - 1)
    def _():
        total = 2 * levels
        for half in range(halves):
            summed = sums_ref[half, pl.ds(0, total, stride=8), :]
            for s in range(1, 8):
                summed = summed + sums_ref[half, pl.ds(s, total, stride=8), :]
            mean = summed * (1.0 / crmx)
            mean = jnp.concatenate([(mean[:levels] - shift) * (1.0 / LOG), mean[levels:]], axis=0)
            if dense is None:
                mean = jnp.concatenate([mean, jnp.zeros((256 - total, 128), F32)], axis=0)
                out_ref[pl.ds(half * 128, 128), :] = mean.T[:, :total]
                continue
            back, cap = dense[1], 8
            each = back * cap + 1
            for t in range(back):
                block = mean[t * 128:(t + 1) * 128].T
                for s in range(128 // cap):
                    to = (half * (128 // cap) + s) * each + t * cap
                    out_ref[to:to + cap, :] = block[s * cap:(s + 1) * cap]
            tail = jnp.concatenate([mean[back * 128:]] * cap, axis=0).T
            group = lax.broadcasted_iota(jnp.int32, (128, 128), 1) // (128 // cap)
            tail = jnp.where(group == lax.broadcasted_iota(jnp.int32, (128, 128), 0) % cap, tail, 0.0)
            for s in range(128 // cap):
                to = (half * (128 // cap) + s) * each + back * cap
                out_ref[to:to + 1, :] = jnp.sum(tail[s * cap:(s + 1) * cap], axis=0, keepdims=True)


def finish_kernel(dense, dyn_ref, place_ref, back_ref, out_ref):
    cdev = dyn_ref.shape[1]
    rows = lax.broadcasted_iota(jnp.int32, (back_ref.shape[0], cdev), 0)
    count = 1 if dense is None else dense[1] + 1
    hot = [jnp.where(rows == place_ref[i:i + 1, :], 1.0, 0.0).astype(BF16) for i in range(count)]
    means = select_dot(back_ref[...], jnp.concatenate(hot, axis=1), TN)
    if dense is None:
        out_ref[...] = dyn_ref[...] + means
        return
    back = dense[1]
    for t in range(back):
        out_ref[t * 128:(t + 1) * 128] = dyn_ref[t * 128:(t + 1) * 128] + means[:, t * cdev:(t + 1) * cdev]
    tail = means[:, back * cdev:]
    size = dyn_ref.shape[0] - back * 128
    rank = place_ref[back + 1:back + 2, :]
    mine = sum(jnp.where(rank == q, tail[q * size:(q + 1) * size], 0.0) for q in range(128 // size))
    out_ref[back * 128:] = dyn_ref[back * 128:] + mine


def local(state, neighbors, owner, crm_state, phase_mask):
    ndev = lax.axis_size(AXES)
    me = lax.axis_index(AXES)
    fields, levels, cdev = state.shape
    rows = fields * levels
    slots, wide = crm_state.shape
    crmx = wide // rows
    cap = slots // ndev
    flat = state.reshape(rows, cdev)
    sds = jax.ShapeDtypeStruct
    dense = (2 * rows // 128, rows // 128) if cap == 8 and rows % 128 == 16 else None
    out_each, back_each = 2 * rows * cap // 128, rows * cap // 128
    far = [(i, (i + 1) % ndev if i % 2 else (i - 1) % ndev) for i in range(ndev)]
    mate = [(i, i ^ 1) for i in range(ndev)]
    odd = me % 2
    first, last = flat[:, :REACH], flat[:, cdev - REACH:]
    from_far = lax.ppermute(jnp.where(odd == 1, last, first), AXES, far)
    from_mate = lax.ppermute(jnp.where(odd == 1, first, last), AXES, mate)

    def whole(*shape):
        return pl.BlockSpec(shape, lambda i: (0,) * len(shape))

    index_out = [sds((rows, cdev), F32)] * 2 + [sds((2 * REACH, cdev), BF16), sds((slots, cdev), BF16)]
    index_out.append(sds((1 if dense is None else dense[1] + 2, cdev), jnp.int32))
    if dense is not None:
        index_out.append(sds((slots // 4, 4 * cdev), BF16))
    same, part, edge, hot, place, *tail = pl.pallas_call(
        functools.partial(index_kernel, (cap, slots, cdev * ndev, dense)),
        grid=(1,),
        in_specs=[whole(rows, cdev), whole(*neighbors.shape), whole(1, cdev)],
        out_specs=[VMEM] * len(index_out),
        out_shape=index_out,
        compiler_params=pltpu.CompilerParams(vmem_limit_bytes=12 << 20),
        name="index",
    )(flat, neighbors, owner.reshape(1, cdev))
    outgoing, dyn = pl.pallas_call(
        functools.partial(pack_kernel, dense),
        in_specs=[VMEM] * (6 + len(tail)),
        out_specs=[VMEM] * 2,
        out_shape=[sds((slots, 2 * rows) if dense is None else (ndev * out_each, 128), F32), sds((rows, cdev), F32)],
        compiler_params=pltpu.CompilerParams(vmem_limit_bytes=12 << 20),
        name="pack",
    )(same, part, edge, hot, from_far, from_mate, *tail)
    arrived = lax.all_to_all(outgoing.reshape(ndev, cap * 2 * rows), AXES, split_axis=0, concat_axis=0, tiled=True)
    arrived = arrived.reshape(outgoing.shape)

    block = TRIO * GROUP * crmx
    count = levels * crmx // block
    take = lambda offset: pl.BlockSpec((slots, block), lambda g: (0, g + offset))
    rates_spec = [pl.BlockSpec((block, slots), lambda g: (g, 0))] * 2
    rates = pl.pallas_call(
        functools.partial(prepare_kernel, crmx),
        grid=(count,),
        in_specs=[take(0)],
        out_specs=rates_spec,
        out_shape=[sds((levels * crmx, slots), F32)] * 2,
        compiler_params=pltpu.CompilerParams(vmem_limit_bytes=FULL),
        cost_estimate=pl.CostEstimate(flops=2 * slots * levels * crmx * GROUP * crmx, transcendentals=0, bytes_accessed=6 * slots * wide),
        name="prepare",
    )(phase_mask)

    back = pl.pallas_call(
        functools.partial(physics_kernel, levels, crmx, dense),
        grid=(count,),
        in_specs=[VMEM, take(0), take(count)] + rates_spec,
        out_specs=VMEM,
        out_shape=sds((slots, rows) if dense is None else (ndev * back_each, 128), F32),
        scratch_shapes=[
            pltpu.VMEM((slots // 128, 2 * levels + 8, 128), F32),
            pltpu.VMEM((slots // 128, 8 * rows, 128), F32),
            pltpu.VMEM((block, slots), F32),
            pltpu.VMEM((block, slots), F32),
            pltpu.VMEM((block, slots), BF16),
            pltpu.VMEM((block, slots), BF16),
            pltpu.VMEM((levels // TRIO * 16, slots), BF16),
            pltpu.VMEM((levels // TRIO * 16, slots), BF16),
            pltpu.VMEM((TRIO * crmx, TRIO * crmx + 16), BF16),
        ],
        compiler_params=pltpu.CompilerParams(vmem_limit_bytes=53000 << 10),
        name="physics",
    )(arrived, crm_state, crm_state, *rates)
    returned = lax.all_to_all(back.reshape(ndev, cap * rows), AXES, split_axis=0, concat_axis=0, tiled=True)
    out = pl.pallas_call(
        functools.partial(finish_kernel, dense),
        in_specs=[VMEM] * 3,
        out_specs=VMEM,
        out_shape=sds((rows, cdev), F32),
        compiler_params=pltpu.CompilerParams(vmem_limit_bytes=12 << 20),
        name="finish",
    )(dyn, place, returned.reshape(back.shape))
    return out.reshape(state.shape)


def solution(mesh):
    return jax.shard_map(
        local,
        mesh=mesh,
        in_specs=(
            P(None, None, AXES),
            P(None, AXES),
            P(AXES, None),
            P(AXES, None),
            P(AXES, None),
        ),
        out_specs=P(None, None, AXES),
        check_vma=False,
    )
```

```python
import functools
import math

import jax
import jax.numpy as jnp
from jax import lax
from jax.experimental import pallas as pl
from jax.experimental.pallas import tpu as pltpu
from jax.sharding import PartitionSpec as P


SUB = 4
REACH = 8
GROUP = 4
AXES = ("sec", "blk")
F32 = jnp.float32
BF16 = jnp.bfloat16
NT = (((1,), (1,)), ((), ()))
NN = (((1,), (0,)), ((), ()))
TN = (((0,), (0,)), ((), ()))
VMEM = pl.BlockSpec(memory_space=pltpu.VMEM)
FULL = 60 * 1024 * 1024
LOG = 0.3 * math.log2(math.e)
TRIO = 3


def parts_of(x):
    high = x.astype(BF16)
    rest = x - high.astype(F32)
    middle = rest.astype(BF16)
    low = (rest - middle.astype(F32)).astype(BF16)
    return high, middle, low


def select_dot(x, onehot, dims, flip=False):
    axis = 1 - dims[0][1 if flip else 0][0]
    size = x.shape[axis]
    wide = jnp.concatenate(parts_of(x), axis=axis)
    pair = (onehot, wide) if flip else (wide, onehot)
    out = lax.dot_general(*pair, dims, preferred_element_type=F32)
    cut = (lambda i: out[:, i * size:(i + 1) * size]) if flip else (lambda i: out[i * size:(i + 1) * size])
    return (cut(0) + cut(1)) + cut(2)


def index_kernel(plan, state_ref, near_ref, owner_ref, same_ref, part_ref, edge_ref, hot_ref, place_ref, *tail_ref):
    cap, slots, total, dense = plan
    cdev = state_ref.shape[1]
    index = near_ref[...] - (lax.axis_index(AXES) * cdev - REACH)
    index = jnp.where(index < 0, index + total, index)
    index = jnp.where(index >= total, index - total, index)
    own = lax.broadcasted_iota(jnp.int32, (cdev, cdev), 0) + REACH
    edge = lax.broadcasted_iota(jnp.int32, (2 * REACH, cdev), 0)
    edge = jnp.where(edge < REACH, edge, edge + cdev)
    inner, outer = jnp.zeros((cdev, cdev), F32), jnp.zeros((2 * REACH, cdev), F32)
    for k in range(near_ref.shape[0]):
        row = index[k:k + 1, :]
        inner = inner + jnp.where(own == row, 1.0, 0.0)
        outer = outer + jnp.where(edge == row, 1.0, 0.0)
    edge_ref[...] = outer.astype(BF16)
    same_ref[...] = state_ref[...]
    part_ref[...] = select_dot(state_ref[...], inner.astype(BF16), NN)
    mine = jnp.broadcast_to(owner_ref[...], (cdev, cdev)).astype(F32)
    lower = lax.broadcasted_iota(jnp.int32, (cdev, cdev), 0) < lax.broadcasted_iota(jnp.int32, (cdev, cdev), 1)
    rank = jnp.sum(jnp.where((mine == mine.T) & lower, 1.0, 0.0), axis=0, keepdims=True).astype(jnp.int32)
    to = owner_ref[...]
    target = to * cap + rank
    rows = lax.broadcasted_iota(jnp.int32, (slots, cdev), 0)
    hot_ref[...] = jnp.where(rows == target, 1.0, 0.0).astype(BF16)
    if dense is None:
        place_ref[0:1, :] = target
        return
    back = dense[1]
    for t in range(back):
        place_ref[t:t + 1, :] = to * (back * cap + 1) + t * cap + rank
    place_ref[back:back + 1, :] = to * (back * cap + 1) + back * cap
    place_ref[back + 1:back + 2, :] = rank
    rows = lax.broadcasted_iota(jnp.int32, (slots // 4, cdev), 0) * 4
    for q in range(4):
        tail_ref[0][:, q * cdev:(q + 1) * cdev] = jnp.where(rows + q == target, 1.0, 0.0).astype(BF16)


def pack_kernel(dense, state_ref, part_ref, edge_ref, hot_ref, far_ref, mate_ref, *refs):
    out_ref, dyn_ref = refs[-2:]
    rows = state_ref.shape[0]
    state = state_ref[...]
    odd = jnp.broadcast_to(lax.axis_index(AXES) % 2, far_ref.shape) == 1
    before = jnp.where(odd, mate_ref[...], far_ref[...])
    after = jnp.where(odd, far_ref[...], mate_ref[...])
    halo = select_dot(before, edge_ref[0:REACH], NN) + select_dot(after, edge_ref[REACH:2 * REACH], NN)
    dyn = 0.15 * ((part_ref[...] + halo) - 4.0 * state)
    dyn_ref[...] = dyn
    if dense is None:
        out_ref[:, 0:rows] = select_dot(state, hot_ref[...], NT, True)
        out_ref[:, rows:2 * rows] = select_dot(dyn, hot_ref[...], NT, True)
        return
    load = jnp.concatenate([state, dyn], axis=0)
    tiles, cap = dense[0], 8
    each = tiles * cap + 2
    main = select_dot(load[:tiles * 128], hot_ref[...], NT, True)
    tail = load[tiles * 128:]
    blank = jnp.zeros_like(tail)
    tail = [jnp.concatenate([tail if i == q else blank for i in range(4)], axis=0) for q in range(4)]
    tail = select_dot(jnp.concatenate(tail, axis=1), refs[0][...], NT, True)
    for s in range(hot_ref.shape[0] // cap):
        for t in range(tiles):
            out_ref[s * each + t * cap:s * each + (t + 1) * cap, :] = main[s * cap:(s + 1) * cap, t * 128:(t + 1) * 128]
        out_ref[s * each + tiles * cap:(s + 1) * each, :] = tail[2 * s:2 * s + 2]


def near_matrix(rows, columns, crmx, centre, side):
    row = lax.broadcasted_iota(jnp.int32, (rows, columns), 0)
    col = lax.broadcasted_iota(jnp.int32, (rows, columns), 1)
    place = row & (crmx - 1)
    apart = (((place & 7) * (crmx // 8) + (place >> 3)) - col) & (crmx - 1)
    same = (row // crmx) == (col // crmx)
    off = jnp.where((apart == 1) | (apart == crmx - 1), side, 0.0)
    return jnp.where(same, jnp.where(apart == 0, centre, off), 0.0)


def prepare_kernel(crmx, mask_ref, rate_ref, both_ref):
    per = GROUP * crmx
    move = near_matrix(per, per, crmx, 1.0, 0.0).astype(BF16)
    for q in range(mask_ref.shape[1] // per):
        part = slice(q * per, (q + 1) * per)
        ice = lax.dot_general(move, mask_ref[:, part].astype(F32).astype(BF16), NT, preferred_element_type=F32)
        rate_ref[part, :] = 0.7 - 0.4 * ice
        both_ref[part, :] = 0.7 - 0.31 * ice


def arrivals(dense, arrived_ref, slots, wide):
    columns = []
    if dense is None:
        for start in range(0, wide, 128):
            size = min(128, wide - start)
            block = arrived_ref[:, start:start + size]
            if size < 128:
                block = jnp.concatenate([block, jnp.zeros((slots, 128 - size), F32)], axis=1)
            columns.append(block.T[:size])
        return jnp.concatenate(columns, axis=0)
    tiles, cap = dense[0], 8
    each = tiles * cap + 2
    for t in range(tiles):
        block = [arrived_ref[s * each + t * cap:s * each + (t + 1) * cap, :] for s in range(slots // cap)]
        columns.append(jnp.concatenate(block, axis=0).T)
    low = lax.broadcasted_iota(jnp.int32, (cap, 128), 0) < 4
    block = []
    for s in range(slots // cap):
        pair = [arrived_ref[s * each + tiles * cap + i:s * each + tiles * cap + i + 1, :] for i in range(2)]
        block.append(jnp.where(low, *[jnp.broadcast_to(p, (cap, 128)) for p in pair]))
    tail = jnp.concatenate(block, axis=0).T
    which = lax.broadcasted_iota(jnp.int32, (32, slots), 1) % 4
    columns.append(sum(jnp.where(which == q, tail[q * 32:(q + 1) * 32], 0.0) for q in range(4)))
    return jnp.concatenate(columns, axis=0)


def physics_kernel(levels, crmx, dense, arrived_ref, ct_ref, cm_ref, nt_ref, nm_ref, rate_ref, both_ref, out_ref, *scratch):
    rows_ref, sums_ref, first_ref = scratch[:3]
    ahead = scratch[3:]
    slots = ct_ref.shape[0]
    halves = slots // 128
    steps = crmx // 8
    step = pl.program_id(0)
    here = rate_ref.shape[0] // crmx
    part = GROUP * crmx
    shift = [math.log(0.8 * 5.0 ** j) / 0.3 for j in range(SUB + 1)]

    def diffuse(q, temp, moist):
        for ref, source in zip(ahead[2 * q:2 * q + 2], (temp, moist)):
            ref[...] = lax.dot_general(first_ref[...], source, NT, preferred_element_type=F32)

    @pl.when(step == 0)
    def _():
        first_ref[...] = near_matrix(part, part, crmx, 3.0, 1.0).astype(BF16)
        diffuse(0, ct_ref[:, :part], cm_ref[:, :part])
        arrived = arrivals(dense, arrived_ref, slots, 4 * levels)
        temp, moist, push, wet = [arrived[i * levels:(i + 1) * levels] for i in range(4)]
        push, wet = push * (1.0 / SUB), wet * (1.0 / SUB)
        tables = [5.0 * (temp + push + shift[1]), 5.0 * (moist + wet)]
        for j in range(2, SUB + 1):
            tables += [5.0 ** j * (push + (shift[j] - shift[j - 1])), 5.0 ** j * wet]
        for i, table in enumerate(tables):
            for half in range(halves):
                rows_ref[half, i * levels:(i + 1) * levels] = table[:, half * 128:(half + 1) * 128]

    def unit(inner, half):
        lanes = pl.ds(half * 128, 128)
        base = inner * crmx
        level = step * here + inner
        get = lambda ref, k: ref[pl.ds(base + 8 * k, 8), lanes]
        const = lambda i: rows_ref[half, pl.ds(level + i * levels, 8, stride=0), :]
        q, within = inner // GROUP, inner % GROUP * crmx
        temp, moist = [
            [ahead[2 * q + i][pl.ds(within + 8 * k, 8), lanes] + add for k in range(steps)]
            for i, add in enumerate((const(0), const(1)))
        ]
        for j in range(1, SUB + 1):
            if j > 1:
                spread = []
                for field, add in ((temp, const(2 * j - 2)), (moist, const(2 * j - 1))):
                    after = pltpu.roll(field[0], 7, 0)
                    before = pltpu.roll(field[steps - 1], 1, 0)
                    ring = [before] + field + [after]
                    spread.append([((ring[k] + ring[k + 2]) + 3.0 * field[k]) + add for k in range(steps)])
                temp, moist = spread
            for k in range(steps):
                over = jnp.maximum(moist[k] - jnp.exp2((LOG / 5.0 ** j) * temp[k]), 0.0)
                moist[k] = moist[k] - get(rate_ref, k) * over
                temp[k] = temp[k] + get(both_ref, k) * over
        for i, field in enumerate((temp, moist)):
            while len(field) > 1:
                field = [a + b for a, b in zip(field[0::2], field[1::2])]
            sums_ref[half, pl.ds(pl.multiple_of((i * levels + level) * 8, 8), 8), :] = field[0]

    for q in range(1, here // GROUP):
        diffuse(q, ct_ref[:, q * part:(q + 1) * part], cm_ref[:, q * part:(q + 1) * part])
    for inner in range(here):
        if inner == GROUP:
            diffuse(0, nt_ref[...], nm_ref[...])
        for half in range(halves):
            unit(inner, half)

    @pl.when(step == pl.num_programs(0) - 1)
    def _():
        total = 2 * levels
        for half in range(halves):
            summed = sums_ref[half, pl.ds(0, total, stride=8), :]
            for s in range(1, 8):
                summed = summed + sums_ref[half, pl.ds(s, total, stride=8), :]
            mean = summed * (1.0 / (crmx * 5.0 ** SUB))
            mean = jnp.concatenate([mean[:levels] - shift[SUB], mean[levels:]], axis=0)
            if dense is None:
                mean = jnp.concatenate([mean, jnp.zeros((256 - total, 128), F32)], axis=0)
                out_ref[pl.ds(half * 128, 128), :] = mean.T[:, :total]
                continue
            back, cap = dense[1], 8
            each = back * cap + 1
            for t in range(back):
                block = mean[t * 128:(t + 1) * 128].T
                for s in range(128 // cap):
                    to = (half * (128 // cap) + s) * each + t * cap
                    out_ref[to:to + cap, :] = block[s * cap:(s + 1) * cap]
            tail = jnp.concatenate([mean[back * 128:]] * cap, axis=0).T
            group = lax.broadcasted_iota(jnp.int32, (128, 128), 1) // (128 // cap)
            tail = jnp.where(group == lax.broadcasted_iota(jnp.int32, (128, 128), 0) % cap, tail, 0.0)
            for s in range(128 // cap):
                to = (half * (128 // cap) + s) * each + back * cap
                out_ref[to:to + 1, :] = jnp.sum(tail[s * cap:(s + 1) * cap], axis=0, keepdims=True)


def finish_kernel(dense, dyn_ref, place_ref, back_ref, out_ref):
    cdev = dyn_ref.shape[1]
    rows = lax.broadcasted_iota(jnp.int32, (back_ref.shape[0], cdev), 0)
    count = 1 if dense is None else dense[1] + 1
    hot = [jnp.where(rows == place_ref[i:i + 1, :], 1.0, 0.0).astype(BF16) for i in range(count)]
    means = select_dot(back_ref[...], jnp.concatenate(hot, axis=1), TN)
    if dense is None:
        out_ref[...] = dyn_ref[...] + means
        return
    back = dense[1]
    for t in range(back):
        out_ref[t * 128:(t + 1) * 128] = dyn_ref[t * 128:(t + 1) * 128] + means[:, t * cdev:(t + 1) * cdev]
    tail = means[:, back * cdev:]
    size = dyn_ref.shape[0] - back * 128
    rank = place_ref[back + 1:back + 2, :]
    mine = sum(jnp.where(rank == q, tail[q * size:(q + 1) * size], 0.0) for q in range(128 // size))
    out_ref[back * 128:] = dyn_ref[back * 128:] + mine


def local(state, neighbors, owner, crm_state, phase_mask):
    ndev = lax.axis_size(AXES)
    me = lax.axis_index(AXES)
    fields, levels, cdev = state.shape
    rows = fields * levels
    slots, wide = crm_state.shape
    crmx = wide // rows
    cap = slots // ndev
    flat = state.reshape(rows, cdev)
    sds = jax.ShapeDtypeStruct
    dense = (2 * rows // 128, rows // 128) if cap == 8 and rows % 128 == 16 else None
    out_each, back_each = 2 * rows * cap // 128, rows * cap // 128
    far = [(i, (i + 1) % ndev if i % 2 else (i - 1) % ndev) for i in range(ndev)]
    mate = [(i, i ^ 1) for i in range(ndev)]
    odd = me % 2
    first, last = flat[:, :REACH], flat[:, cdev - REACH:]
    to_far, to_mate = jnp.where(odd == 1, last, first), jnp.where(odd == 1, first, last)
    from_far = lax.ppermute(to_far, AXES, far)
    from_mate = lax.ppermute(to_mate, AXES, mate)

    index_out = [sds((rows, cdev), F32)] * 2 + [sds((2 * REACH, cdev), BF16), sds((slots, cdev), BF16)]
    index_out.append(sds((1 if dense is None else dense[1] + 2, cdev), jnp.int32))
    if dense is not None:
        index_out.append(sds((slots // 4, 4 * cdev), BF16))
    same, part, edge, hot, place, *tail = pl.pallas_call(
        functools.partial(index_kernel, (cap, slots, cdev * ndev, dense)),
        in_specs=[VMEM] * 3,
        out_specs=[VMEM] * len(index_out),
        out_shape=index_out,
        compiler_params=pltpu.CompilerParams(vmem_limit_bytes=12 << 20),
        name="index",
    )(flat, neighbors, owner.reshape(1, cdev))
    outgoing, dyn = pl.pallas_call(
        functools.partial(pack_kernel, dense),
        in_specs=[VMEM] * (6 + len(tail)),
        out_specs=[VMEM] * 2,
        out_shape=[sds((slots, 2 * rows) if dense is None else (ndev * out_each, 128), F32), sds((rows, cdev), F32)],
        compiler_params=pltpu.CompilerParams(vmem_limit_bytes=12 << 20),
        name="pack",
    )(same, part, edge, hot, from_far, from_mate, *tail)
    arrived = lax.all_to_all(outgoing.reshape(ndev, cap * 2 * rows), AXES, split_axis=0, concat_axis=0, tiled=True)
    arrived = arrived.reshape(outgoing.shape)

    block = TRIO * GROUP * crmx
    count = levels * crmx // block
    take = lambda offset: pl.BlockSpec((slots, block), lambda g: (0, g + offset))
    last = TRIO * (count - 1)
    soon = lambda offset: pl.BlockSpec((slots, GROUP * crmx), lambda g: (0, TRIO * offset + jnp.minimum(TRIO * (g + 1), last)))
    rates_spec = [pl.BlockSpec((block, slots), lambda g: (g, 0))] * 2
    rates = pl.pallas_call(
        functools.partial(prepare_kernel, crmx),
        grid=(count,),
        in_specs=[take(0)],
        out_specs=rates_spec,
        out_shape=[sds((levels * crmx, slots), F32)] * 2,
        compiler_params=pltpu.CompilerParams(vmem_limit_bytes=FULL),
        cost_estimate=pl.CostEstimate(flops=2 * slots * levels * crmx * GROUP * crmx, transcendentals=0, bytes_accessed=6 * slots * wide),
        name="prepare",
    )(phase_mask)

    back = pl.pallas_call(
        functools.partial(physics_kernel, levels, crmx, dense),
        grid=(count,),
        in_specs=[VMEM, take(0), take(count), soon(0), soon(count)] + rates_spec,
        out_specs=VMEM,
        out_shape=sds((slots, rows) if dense is None else (ndev * back_each, 128), F32),
        scratch_shapes=[
            pltpu.VMEM((slots // 128, 2 * SUB * levels + 8, 128), F32),
            pltpu.VMEM((slots // 128, 8 * rows, 128), F32),
            pltpu.VMEM((GROUP * crmx, GROUP * crmx), BF16),
        ] + [pltpu.VMEM((GROUP * crmx, slots), F32)] * (2 * TRIO),
        compiler_params=pltpu.CompilerParams(vmem_limit_bytes=53000 << 10),
        name="physics",
    )(arrived, crm_state, crm_state, crm_state, crm_state, *rates)
    returned = lax.all_to_all(back.reshape(ndev, cap * rows), AXES, split_axis=0, concat_axis=0, tiled=True)
    out = pl.pallas_call(
        functools.partial(finish_kernel, dense),
        in_specs=[VMEM] * 3,
        out_specs=VMEM,
        out_shape=sds((rows, cdev), F32),
        compiler_params=pltpu.CompilerParams(vmem_limit_bytes=12 << 20),
        name="finish",
    )(dyn, place, returned.reshape(back.shape))
    return out.reshape(state.shape)


def solution(mesh):
    return jax.shard_map(
        local,
        mesh=mesh,
        in_specs=(
            P(None, None, AXES),
            P(None, AXES),
            P(AXES, None),
            P(AXES, None),
            P(AXES, None),
        ),
        out_specs=P(None, None, AXES),
        check_vma=False,
    )
```

```python
import functools
import math

import jax
import jax.numpy as jnp
from jax import lax
from jax.experimental import pallas as pl
from jax.experimental.pallas import tpu as pltpu
from jax.sharding import PartitionSpec as P


SUB = 4
REACH = 8
GROUP = 4
AXES = ("sec", "blk")
F32 = jnp.float32
BF16 = jnp.bfloat16
NT = (((1,), (1,)), ((), ()))
NN = (((1,), (0,)), ((), ()))
TN = (((0,), (0,)), ((), ()))
VMEM = pl.BlockSpec(memory_space=pltpu.VMEM)
LOG = 0.3 * math.log2(math.e)
TRIO = 3
HEAD = 8


def parts_of(x):
    high = x.astype(BF16)
    rest = x - high.astype(F32)
    middle = rest.astype(BF16)
    low = (rest - middle.astype(F32)).astype(BF16)
    return high, middle, low


def select_dot(x, onehot, dims, flip=False):
    axis = 1 - dims[0][1 if flip else 0][0]
    size = x.shape[axis]
    wide = jnp.concatenate(parts_of(x), axis=axis)
    pair = (onehot, wide) if flip else (wide, onehot)
    out = lax.dot_general(*pair, dims, preferred_element_type=F32)
    cut = (lambda i: out[:, i * size:(i + 1) * size]) if flip else (lambda i: out[i * size:(i + 1) * size])
    return (cut(0) + cut(1)) + cut(2)


def index_kernel(plan, state_ref, near_ref, owner_ref, same_ref, part_ref, edge_ref, hot_ref, place_ref, *tail_ref):
    cap, slots, total, dense = plan
    cdev = state_ref.shape[1]
    index = near_ref[...] - (lax.axis_index(AXES) * cdev - REACH)
    index = jnp.where(index < 0, index + total, index)
    index = jnp.where(index >= total, index - total, index)
    own = lax.broadcasted_iota(jnp.int32, (cdev, cdev), 0) + REACH
    edge = lax.broadcasted_iota(jnp.int32, (2 * REACH, cdev), 0)
    edge = jnp.where(edge < REACH, edge, edge + cdev)
    inner, outer = jnp.zeros((cdev, cdev), F32), jnp.zeros((2 * REACH, cdev), F32)
    for k in range(near_ref.shape[0]):
        row = index[k:k + 1, :]
        inner = inner + jnp.where(own == row, 1.0, 0.0)
        outer = outer + jnp.where(edge == row, 1.0, 0.0)
    edge_ref[...] = outer.astype(BF16)
    same_ref[...] = state_ref[...]
    part_ref[...] = select_dot(state_ref[...], inner.astype(BF16), NN)
    mine = jnp.broadcast_to(owner_ref[...], (cdev, cdev)).astype(F32)
    lower = lax.broadcasted_iota(jnp.int32, (cdev, cdev), 0) < lax.broadcasted_iota(jnp.int32, (cdev, cdev), 1)
    rank = jnp.sum(jnp.where((mine == mine.T) & lower, 1.0, 0.0), axis=0, keepdims=True).astype(jnp.int32)
    to = owner_ref[...]
    target = to * cap + rank
    rows = lax.broadcasted_iota(jnp.int32, (slots, cdev), 0)
    hot_ref[...] = jnp.where(rows == target, 1.0, 0.0).astype(BF16)
    if dense is None:
        place_ref[0:1, :] = target
        return
    back = dense[1]
    for t in range(back):
        place_ref[t:t + 1, :] = to * (back * cap + 1) + t * cap + rank
    place_ref[back:back + 1, :] = to * (back * cap + 1) + back * cap
    place_ref[back + 1:back + 2, :] = rank
    rows = lax.broadcasted_iota(jnp.int32, (slots // 4, cdev), 0) * 4
    for q in range(4):
        tail_ref[0][:, q * cdev:(q + 1) * cdev] = jnp.where(rows + q == target, 1.0, 0.0).astype(BF16)


def pack_kernel(dense, state_ref, part_ref, edge_ref, hot_ref, far_ref, mate_ref, *refs):
    out_ref, dyn_ref = refs[-2:]
    rows = state_ref.shape[0]
    state = state_ref[...]
    odd = jnp.broadcast_to(lax.axis_index(AXES) % 2, far_ref.shape) == 1
    before = jnp.where(odd, mate_ref[...], far_ref[...])
    after = jnp.where(odd, far_ref[...], mate_ref[...])
    halo = select_dot(before, edge_ref[0:REACH], NN) + select_dot(after, edge_ref[REACH:2 * REACH], NN)
    dyn = 0.15 * ((part_ref[...] + halo) - 4.0 * state)
    dyn_ref[...] = dyn
    if dense is None:
        out_ref[:, 0:rows] = select_dot(state, hot_ref[...], NT, True)
        out_ref[:, rows:2 * rows] = select_dot(dyn, hot_ref[...], NT, True)
        return
    load = jnp.concatenate([state, dyn], axis=0)
    tiles, cap = dense[0], 8
    each = tiles * cap + 2
    main = select_dot(load[:tiles * 128], hot_ref[...], NT, True)
    tail = load[tiles * 128:]
    blank = jnp.zeros_like(tail)
    tail = [jnp.concatenate([tail if i == q else blank for i in range(4)], axis=0) for q in range(4)]
    tail = select_dot(jnp.concatenate(tail, axis=1), refs[0][...], NT, True)
    for s in range(hot_ref.shape[0] // cap):
        for t in range(tiles):
            out_ref[s * each + t * cap:s * each + (t + 1) * cap, :] = main[s * cap:(s + 1) * cap, t * 128:(t + 1) * 128]
        out_ref[s * each + tiles * cap:(s + 1) * each, :] = tail[2 * s:2 * s + 2]


def near_matrix(rows, columns, crmx, centre, side):
    row = lax.broadcasted_iota(jnp.int32, (rows, columns), 0)
    col = lax.broadcasted_iota(jnp.int32, (rows, columns), 1)
    place = row & (crmx - 1)
    apart = (((place & 7) * (crmx // 8) + (place >> 3)) - col) & (crmx - 1)
    same = (row // crmx) == (col // crmx)
    off = jnp.where((apart == 1) | (apart == crmx - 1), side, 0.0)
    return jnp.where(same, jnp.where(apart == 0, centre, off), 0.0)


def diffusion(first, source):
    return lax.dot_general(first, source, NT, preferred_element_type=F32)


def prepare_kernel(crmx, mask_ref, ct_ref, cm_ref, rate_ref, both_ref, *head_refs):
    per = GROUP * crmx
    move = near_matrix(per, per, crmx, 1.0, 0.0).astype(BF16)
    for q in range(mask_ref.shape[1] // per):
        part = slice(q * per, (q + 1) * per)
        ice = lax.dot_general(move, mask_ref[:, part].astype(F32).astype(BF16), NT, preferred_element_type=F32)
        rate_ref[part, :] = 0.7 - 0.4 * ice
        both_ref[part, :] = 0.7 - 0.31 * ice

    @pl.when(pl.program_id(0) == 0)
    def _():
        yt_ref, ym_ref, head_rate_ref = head_refs
        size = yt_ref.shape[0]
        first = near_matrix(per, per, crmx, 3.0, 1.0).astype(BF16)
        for q in range(size // per):
            part = slice(q * per, (q + 1) * per)
            yt_ref[part, :] = diffusion(first, ct_ref[:, part])
            ym_ref[part, :] = diffusion(first, cm_ref[:, part])
        head_rate_ref[...] = rate_ref[:size]


def arrivals(dense, arrived_ref, slots, wide):
    columns = []
    if dense is None:
        for start in range(0, wide, 128):
            size = min(128, wide - start)
            block = arrived_ref[:, start:start + size]
            if size < 128:
                block = jnp.concatenate([block, jnp.zeros((slots, 128 - size), F32)], axis=1)
            columns.append(block.T[:size])
        return jnp.concatenate(columns, axis=0)
    tiles, cap = dense[0], 8
    each = tiles * cap + 2
    for t in range(tiles):
        block = [arrived_ref[s * each + t * cap:s * each + (t + 1) * cap, :] for s in range(slots // cap)]
        columns.append(jnp.concatenate(block, axis=0).T)
    low = lax.broadcasted_iota(jnp.int32, (cap, 128), 0) < 4
    block = []
    for s in range(slots // cap):
        pair = [arrived_ref[s * each + tiles * cap + i:s * each + tiles * cap + i + 1, :] for i in range(2)]
        block.append(jnp.where(low, *[jnp.broadcast_to(p, (cap, 128)) for p in pair]))
    tail = jnp.concatenate(block, axis=0).T
    which = lax.broadcasted_iota(jnp.int32, (32, slots), 1) % 4
    columns.append(sum(jnp.where(which == q, tail[q * 32:(q + 1) * 32], 0.0) for q in range(4)))
    return jnp.concatenate(columns, axis=0)


def physics_kernel(levels, crmx, dense, arrived_ref, *refs):
    head, (crm_hbm, rate_hbm, both_hbm, out_ref), refs = refs[:3], refs[3:7], refs[7:]
    rows_ref, sums_ref, first_ref, crm_sems, rate_sems = refs[:5]
    head = (*head, refs[17])
    fields, coefs, crm_bufs = (refs[5:7], refs[7:9]), (refs[9:11], refs[11:13]), (refs[13:15], refs[15:17])
    slots = crm_hbm.shape[0]
    halves = slots // 128
    steps = crmx // 8
    part = GROUP * crmx
    size = head[0].shape[0]
    here = size // crmx
    count = levels // here
    shift = [math.log(0.8 * 5.0 ** j) / 0.3 for j in range(SUB + 1)]

    def crm_copies(group, k):
        width = levels * crmx
        at = [pl.ds(pl.multiple_of(i * width + group * size, 128), size) for i in range(2)]
        return [pltpu.make_async_copy(crm_hbm.at[:, at[i]], crm_bufs[k][i], crm_sems.at[k, i]) for i in range(2)]

    def rate_copies(group, k):
        at = pl.ds(pl.multiple_of(group * size, 8), size)
        return [
            pltpu.make_async_copy(ref.at[at, :], coefs[k][i], rate_sems.at[k, i])
            for i, ref in enumerate((rate_hbm, both_hbm))
        ]

    def start(copies):
        for copy in copies:
            copy.start()

    def wait(copies):
        for copy in copies:
            copy.wait()

    def diffuse(k):
        for ref, source in zip(fields[k], crm_bufs[k]):
            for q in range(size // part):
                cut = slice(q * part, (q + 1) * part)
                ref[cut, :] = diffusion(first_ref[...], source[:, cut])

    for group in (1, 2):
        start(crm_copies(group, (group - 1) % 2))
        start(rate_copies(group, (group - 1) % 2))
    first_ref[...] = near_matrix(part, part, crmx, 3.0, 1.0).astype(BF16)
    arrived = arrivals(dense, arrived_ref, slots, 4 * levels)
    temp, moist, push, wet = [arrived[i * levels:(i + 1) * levels] for i in range(4)]
    push, wet = push * (1.0 / SUB), wet * (1.0 / SUB)
    tables = [5.0 * (temp + push + shift[1]), 5.0 * (moist + wet)]
    for j in range(2, SUB + 1):
        tables += [5.0 ** j * (push + (shift[j] - shift[j - 1])), 5.0 ** j * wet]
    for i, table in enumerate(tables):
        for half in range(halves):
            rows_ref[half, i * levels:(i + 1) * levels] = table[:, half * 128:(half + 1) * 128]

    def unit(group, inner, half, sources):
        lanes = pl.ds(half * 128, 128)
        base = inner * crmx
        level = group * here + inner
        get = lambda ref, k: ref[pl.ds(base + 8 * k, 8), lanes]
        const = lambda i: rows_ref[half, pl.ds(level + i * levels, 8, stride=0), :]
        temp, moist = [[get(sources[i], k) + add for k in range(steps)] for i, add in enumerate((const(0), const(1)))]
        for j in range(1, SUB + 1):
            if j > 1:
                spread = []
                for field, add in ((temp, const(2 * j - 2)), (moist, const(2 * j - 1))):
                    after = pltpu.roll(field[0], 7, 0)
                    before = pltpu.roll(field[steps - 1], 1, 0)
                    ring = [before] + field + [after]
                    spread.append([((ring[k] + ring[k + 2]) + 3.0 * field[k]) + add for k in range(steps)])
                temp, moist = spread
            for k in range(steps):
                over = jnp.maximum(moist[k] - jnp.exp2((LOG / 5.0 ** j) * temp[k]), 0.0)
                moist[k] = moist[k] - get(sources[2], k) * over
                temp[k] = temp[k] + get(sources[3], k) * over
        for i, field in enumerate((temp, moist)):
            while len(field) > 1:
                field = [a + b for a, b in zip(field[0::2], field[1::2])]
            sums_ref[half, pl.ds(pl.multiple_of((i * levels + level) * 8, 8), 8), :] = field[0]

    def run(group, sources):
        for inner in range(here):
            for half in range(halves):
                unit(group, inner, half, sources)

    head[3][...] = 0.7 - 0.775 * (0.7 - head[2][...])
    wait(crm_copies(1, 0))
    diffuse(0)
    run(0, head)

    @pl.loop(0, (count - 1) // 2)
    def _(trip):
        for k in range(2):
            group = 1 + 2 * trip + k

            @pl.when(group + 2 < count)
            def _():
                start(crm_copies(group + 2, k))

            wait(rate_copies(group, k))

            @pl.when(group + 1 < count)
            def _():
                wait(crm_copies(group + 1, 1 - k))

            diffuse(1 - k)
            run(group, fields[k] + coefs[k])

            @pl.when(group + 2 < count)
            def _():
                start(rate_copies(group + 2, k))

    total = 2 * levels
    for half in range(halves):
        summed = sums_ref[half, pl.ds(0, total, stride=8), :]
        for s in range(1, 8):
            summed = summed + sums_ref[half, pl.ds(s, total, stride=8), :]
        mean = summed * (1.0 / (crmx * 5.0 ** SUB))
        mean = jnp.concatenate([mean[:levels] - shift[SUB], mean[levels:]], axis=0)
        if dense is None:
            mean = jnp.concatenate([mean, jnp.zeros((256 - total, 128), F32)], axis=0)
            out_ref[pl.ds(half * 128, 128), :] = mean.T[:, :total]
            continue
        back, cap = dense[1], 8
        each = back * cap + 1
        for t in range(back):
            block = mean[t * 128:(t + 1) * 128].T
            for s in range(128 // cap):
                to = (half * (128 // cap) + s) * each + t * cap
                out_ref[to:to + cap, :] = block[s * cap:(s + 1) * cap]
        tail = jnp.concatenate([mean[back * 128:]] * cap, axis=0).T
        group = lax.broadcasted_iota(jnp.int32, (128, 128), 1) // (128 // cap)
        tail = jnp.where(group == lax.broadcasted_iota(jnp.int32, (128, 128), 0) % cap, tail, 0.0)
        for s in range(128 // cap):
            to = (half * (128 // cap) + s) * each + back * cap
            out_ref[to:to + 1, :] = jnp.sum(tail[s * cap:(s + 1) * cap], axis=0, keepdims=True)


def finish_kernel(dense, dyn_ref, place_ref, back_ref, out_ref):
    cdev = dyn_ref.shape[1]
    rows = lax.broadcasted_iota(jnp.int32, (back_ref.shape[0], cdev), 0)
    count = 1 if dense is None else dense[1] + 1
    hot = [jnp.where(rows == place_ref[i:i + 1, :], 1.0, 0.0).astype(BF16) for i in range(count)]
    means = select_dot(back_ref[...], jnp.concatenate(hot, axis=1), TN)
    if dense is None:
        out_ref[...] = dyn_ref[...] + means
        return
    back = dense[1]
    for t in range(back):
        out_ref[t * 128:(t + 1) * 128] = dyn_ref[t * 128:(t + 1) * 128] + means[:, t * cdev:(t + 1) * cdev]
    tail = means[:, back * cdev:]
    size = dyn_ref.shape[0] - back * 128
    rank = place_ref[back + 1:back + 2, :]
    mine = sum(jnp.where(rank == q, tail[q * size:(q + 1) * size], 0.0) for q in range(128 // size))
    out_ref[back * 128:] = dyn_ref[back * 128:] + mine


def local(state, neighbors, owner, crm_state, phase_mask):
    ndev = lax.axis_size(AXES)
    me = lax.axis_index(AXES)
    fields, levels, cdev = state.shape
    rows = fields * levels
    slots, wide = crm_state.shape
    crmx = wide // rows
    cap = slots // ndev
    flat = state.reshape(rows, cdev)
    sds = jax.ShapeDtypeStruct
    dense = (2 * rows // 128, rows // 128) if cap == 8 and rows % 128 == 16 else None
    out_each, back_each = 2 * rows * cap // 128, rows * cap // 128
    far = [(i, (i + 1) % ndev if i % 2 else (i - 1) % ndev) for i in range(ndev)]
    mate = [(i, i ^ 1) for i in range(ndev)]
    odd = me % 2
    first, last = flat[:, :REACH], flat[:, cdev - REACH:]
    to_far, to_mate = jnp.where(odd == 1, last, first), jnp.where(odd == 1, first, last)
    from_far = lax.ppermute(to_far, AXES, far)
    from_mate = lax.ppermute(to_mate, AXES, mate)

    index_out = [sds((rows, cdev), F32)] * 2 + [sds((2 * REACH, cdev), BF16), sds((slots, cdev), BF16)]
    index_out.append(sds((1 if dense is None else dense[1] + 2, cdev), jnp.int32))
    if dense is not None:
        index_out.append(sds((slots // 4, 4 * cdev), BF16))
    same, part, edge, hot, place, *tail = pl.pallas_call(
        functools.partial(index_kernel, (cap, slots, cdev * ndev, dense)),
        in_specs=[VMEM] * 3,
        out_specs=[VMEM] * len(index_out),
        out_shape=index_out,
        compiler_params=pltpu.CompilerParams(vmem_limit_bytes=12 << 20),
        name="index",
    )(flat, neighbors, owner.reshape(1, cdev))
    outgoing, dyn = pl.pallas_call(
        functools.partial(pack_kernel, dense),
        in_specs=[VMEM] * (6 + len(tail)),
        out_specs=[VMEM] * 2,
        out_shape=[sds((slots, 2 * rows) if dense is None else (ndev * out_each, 128), F32), sds((rows, cdev), F32)],
        compiler_params=pltpu.CompilerParams(vmem_limit_bytes=12 << 20),
        name="pack",
    )(same, part, edge, hot, from_far, from_mate, *tail)
    arrived = lax.all_to_all(outgoing.reshape(ndev, cap * 2 * rows), AXES, split_axis=0, concat_axis=0, tiled=True)
    arrived = arrived.reshape(outgoing.shape)

    block = TRIO * GROUP * crmx
    count = levels * crmx // block
    take = lambda offset: pl.BlockSpec((slots, block), lambda g: (0, g + offset))
    rates_spec = [pl.BlockSpec((block, slots), lambda g: (g, 0))] * 2
    size = HEAD * crmx
    field, coef = sds((levels * crmx, slots), F32), sds((size, slots), F32)
    offset = levels // HEAD
    *rates, yt, ym, head_rate = pl.pallas_call(
        functools.partial(prepare_kernel, crmx),
        grid=(count,),
        in_specs=[take(0)] + [pl.BlockSpec((slots, size), lambda g, i=i: (0, i * offset)) for i in range(2)],
        out_specs=rates_spec + [VMEM] * 3,
        out_shape=[field] * 2 + [coef] * 3,
        compiler_params=pltpu.CompilerParams(vmem_limit_bytes=53000 << 10),
        cost_estimate=pl.CostEstimate(flops=2 * slots * levels * crmx * GROUP * crmx, transcendentals=0, bytes_accessed=6 * slots * wide),
        name="prepare",
    )(phase_mask, crm_state, crm_state)

    back = pl.pallas_call(
        functools.partial(physics_kernel, levels, crmx, dense),
        in_specs=[VMEM] * 4 + [pl.BlockSpec(memory_space=pl.ANY)] * 3,
        out_specs=VMEM,
        out_shape=sds((slots, rows) if dense is None else (ndev * back_each, 128), F32),
        scratch_shapes=[
            pltpu.VMEM((slots // 128, 2 * SUB * levels + 8, 128), F32),
            pltpu.VMEM((slots // 128, 8 * rows, 128), F32),
            pltpu.VMEM((GROUP * crmx, GROUP * crmx), BF16),
            pltpu.SemaphoreType.DMA((2, 2)),
            pltpu.SemaphoreType.DMA((2, 2)),
        ]
        + [pltpu.VMEM((size, slots), F32)] * 8
        + [pltpu.VMEM((slots, size), BF16)] * 4
        + [pltpu.VMEM((size, slots), F32)],
        compiler_params=pltpu.CompilerParams(vmem_limit_bytes=53000 << 10),
        name="physics",
    )(arrived, yt, ym, head_rate, crm_state, *rates)
    returned = lax.all_to_all(back.reshape(ndev, cap * rows), AXES, split_axis=0, concat_axis=0, tiled=True)
    out = pl.pallas_call(
        functools.partial(finish_kernel, dense),
        in_specs=[VMEM] * 3,
        out_specs=VMEM,
        out_shape=sds((rows, cdev), F32),
        compiler_params=pltpu.CompilerParams(vmem_limit_bytes=12 << 20),
        name="finish",
    )(dyn, place, returned.reshape(back.shape))
    return out.reshape(state.shape)


def solution(mesh):
    return jax.shard_map(
        local,
        mesh=mesh,
        in_specs=(
            P(None, None, AXES),
            P(None, AXES),
            P(AXES, None),
            P(AXES, None),
            P(AXES, None),
        ),
        out_specs=P(None, None, AXES),
        check_vma=False,
    )
```

```python
import functools
import math

import jax
import jax.numpy as jnp
from jax import lax
from jax.experimental import pallas as pl
from jax.experimental.pallas import tpu as pltpu
from jax.sharding import PartitionSpec as P


SUB = 4
REACH = 8
GROUP = 4
AXES = ("sec", "blk")
F32 = jnp.float32
BF16 = jnp.bfloat16
NT = (((1,), (1,)), ((), ()))
NN = (((1,), (0,)), ((), ()))
TN = (((0,), (0,)), ((), ()))
VMEM = pl.BlockSpec(memory_space=pltpu.VMEM)
LOG = 0.3 * math.log2(math.e)
TRIO = 3
HEAD = 8


def parts_of(x):
    high = x.astype(BF16)
    rest = x - high.astype(F32)
    middle = rest.astype(BF16)
    low = (rest - middle.astype(F32)).astype(BF16)
    return high, middle, low


def select_dot(x, onehot, dims, flip=False):
    axis = 1 - dims[0][1 if flip else 0][0]
    size = x.shape[axis]
    wide = jnp.concatenate(parts_of(x), axis=axis)
    pair = (onehot, wide) if flip else (wide, onehot)
    out = lax.dot_general(*pair, dims, preferred_element_type=F32)
    cut = (lambda i: out[:, i * size:(i + 1) * size]) if flip else (lambda i: out[i * size:(i + 1) * size])
    return (cut(0) + cut(1)) + cut(2)


def index_kernel(plan, state_ref, near_ref, owner_ref, base_ref, part_ref, edge_ref, share_ref, place_ref):
    cap, slots, total, dense = plan
    _, cdev = state_ref.shape
    state = state_ref[...]
    index = near_ref[...] - (lax.axis_index(AXES) * cdev - REACH)
    index = jnp.where(index < 0, index + total, index)
    index = jnp.where(index >= total, index - total, index)
    own = lax.broadcasted_iota(jnp.int32, (cdev, cdev), 0) + REACH
    edge = lax.broadcasted_iota(jnp.int32, (2 * REACH, cdev), 0)
    edge = jnp.where(edge < REACH, edge, edge + cdev)
    inner, outer = jnp.zeros((cdev, cdev), F32), jnp.zeros((2 * REACH, cdev), F32)
    for k in range(near_ref.shape[0]):
        row = index[k:k + 1, :]
        inner = inner + jnp.where(own == row, 1.0, 0.0)
        outer = outer + jnp.where(edge == row, 1.0, 0.0)
    outer = outer.astype(BF16)
    edge_ref[...] = outer
    part = 0.15 * (select_dot(state, inner.astype(BF16), NN) - 4.0 * state)
    part_ref[...] = part
    mine = jnp.broadcast_to(owner_ref[...], (cdev, cdev)).astype(F32)
    lower = lax.broadcasted_iota(jnp.int32, (cdev, cdev), 0) < lax.broadcasted_iota(jnp.int32, (cdev, cdev), 1)
    rank = jnp.sum(jnp.where((mine == mine.T) & lower, 1.0, 0.0), axis=0, keepdims=True).astype(jnp.int32)
    to = owner_ref[...]
    target = to * cap + rank
    load = jnp.concatenate([part, state], axis=0)

    def hot(count, place):
        return jnp.where(lax.broadcasted_iota(jnp.int32, (count, cdev), 0) == place, 1.0, 0.0).astype(BF16)

    def share(chosen):
        return lax.dot_general(chosen, outer, NT, preferred_element_type=F32).astype(BF16)

    if dense is None:
        place_ref[0:1, :] = target
        chosen = hot(slots, target)
        base_ref[...] = select_dot(load, chosen, NT, True)
        share_ref[...] = share(chosen)
        return
    tiles, back = dense
    for t in range(back):
        place_ref[t:t + 1, :] = to * (back * cap + 1) + t * cap + rank
    place_ref[back:back + 1, :] = to * (back * cap + 1) + back * cap
    place_ref[back + 1:back + 2, :] = rank
    each = tiles * cap + 2
    for t in range(2):
        share_ref[:, 2 * REACH * t:2 * REACH * (t + 1)] = share(hot(share_ref.shape[0], to * each + t * cap + rank))
    main = select_dot(load[:tiles * 128], hot(slots, target), NT, True)
    tail = load[tiles * 128:]
    blank = jnp.zeros_like(tail)
    tail = [jnp.concatenate([tail if i == q else blank for i in range(4)], axis=0) for q in range(4)]
    chosen = [hot(slots // 4, jnp.where(rank % 4 == q, target // 4, -1)) for q in range(4)]
    tail = select_dot(jnp.concatenate(tail, axis=1), jnp.concatenate(chosen, axis=1), NT, True)
    for s in range(slots // cap):
        for t in range(tiles):
            base_ref[s * each + t * cap:s * each + (t + 1) * cap, :] = main[s * cap:(s + 1) * cap, t * 128:(t + 1) * 128]
        base_ref[s * each + tiles * cap:(s + 1) * each, :] = tail[2 * s:2 * s + 2]


def pack_kernel(dense, base_ref, part_ref, edge_ref, share_ref, far_ref, mate_ref, out_ref, dyn_ref, halo_ref):
    rows = part_ref.shape[0]
    odd = jnp.broadcast_to(lax.axis_index(AXES) % 2, far_ref.shape) == 1
    before = 0.15 * jnp.where(odd, mate_ref[...], far_ref[...])
    after = 0.15 * jnp.where(odd, far_ref[...], mate_ref[...])
    if dense is None:
        halo_ref[:, :REACH], halo_ref[:, REACH:] = before, after
        out_ref[:, :rows] = base_ref[:, :rows] + select_dot(halo_ref[...], share_ref[...], NT, True)
        out_ref[:, rows:] = base_ref[:, rows:]
    else:
        halo_ref[:, 2 * REACH:] = jnp.zeros((128, 2 * REACH), F32)
        for i, side in enumerate((before, after)):
            halo_ref[:, i * REACH:(i + 1) * REACH] = side[:128]
            halo_ref[0:rows - 128, (2 + i) * REACH:(3 + i) * REACH] = side[128:]
        out_ref[...] = base_ref[...] + select_dot(halo_ref[...], share_ref[...], NT, True)
    dyn_ref[...] = part_ref[...] + (select_dot(before, edge_ref[:REACH], NN) + select_dot(after, edge_ref[REACH:], NN))


def near_matrix(rows, columns, crmx, centre, side):
    row = lax.broadcasted_iota(jnp.int32, (rows, columns), 0)
    col = lax.broadcasted_iota(jnp.int32, (rows, columns), 1)
    place = row & (crmx - 1)
    apart = (((place & 7) * (crmx // 8) + (place >> 3)) - col) & (crmx - 1)
    same = (row // crmx) == (col // crmx)
    off = jnp.where((apart == 1) | (apart == crmx - 1), side, 0.0)
    return jnp.where(same, jnp.where(apart == 0, centre, off), 0.0)


def diffusion(first, source):
    return lax.dot_general(first, source, NT, preferred_element_type=F32)


def prepare_kernel(crmx, mask_ref, ct_ref, cm_ref, rate_ref, both_ref, *head_refs):
    per = GROUP * crmx
    move = near_matrix(per, per, crmx, 1.0, 0.0).astype(BF16)
    for q in range(mask_ref.shape[1] // per):
        part = slice(q * per, (q + 1) * per)
        ice = lax.dot_general(move, mask_ref[:, part].astype(F32).astype(BF16), NT, preferred_element_type=F32)
        rate_ref[part, :] = 0.7 - 0.4 * ice
        both_ref[part, :] = 0.7 - 0.31 * ice

    @pl.when(pl.program_id(0) == 0)
    def _():
        yt_ref, ym_ref, head_rate_ref, first_ref = head_refs
        size = yt_ref.shape[0]
        first = near_matrix(per, per, crmx, 3.0, 1.0).astype(BF16)
        first_ref[...] = first
        for q in range(size // per):
            part = slice(q * per, (q + 1) * per)
            yt_ref[part, :] = diffusion(first, ct_ref[:, part])
            ym_ref[part, :] = diffusion(first, cm_ref[:, part])
        head_rate_ref[...] = rate_ref[:size]


def arrivals(dense, arrived_ref, slots, wide):
    columns = []
    if dense is None:
        for start in range(0, wide, 128):
            size = min(128, wide - start)
            block = arrived_ref[:, start:start + size]
            if size < 128:
                block = jnp.concatenate([block, jnp.zeros((slots, 128 - size), F32)], axis=1)
            columns.append(block.T[:size])
        return jnp.concatenate(columns, axis=0)
    tiles, cap = dense[0], 8
    each = tiles * cap + 2
    for t in range(tiles):
        block = [arrived_ref[s * each + t * cap:s * each + (t + 1) * cap, :] for s in range(slots // cap)]
        columns.append(jnp.concatenate(block, axis=0).T)
    low = lax.broadcasted_iota(jnp.int32, (cap, 128), 0) < 4
    block = []
    for s in range(slots // cap):
        pair = [arrived_ref[s * each + tiles * cap + i:s * each + tiles * cap + i + 1, :] for i in range(2)]
        block.append(jnp.where(low, *[jnp.broadcast_to(p, (cap, 128)) for p in pair]))
    tail = jnp.concatenate(block, axis=0).T
    which = lax.broadcasted_iota(jnp.int32, (32, slots), 1) % 4
    columns.append(sum(jnp.where(which == q, tail[q * 32:(q + 1) * 32], 0.0) for q in range(4)))
    return jnp.concatenate(columns, axis=0)


def physics_kernel(levels, crmx, dense, arrived_ref, *refs):
    head, (first_ref, crm_hbm, rate_hbm, both_hbm, out_ref), refs = refs[:3], refs[3:8], refs[8:]
    rows_ref, sums_ref, crm_sems, rate_sems = refs[:4]
    head = (*head, refs[4])
    fields, coefs, crm_bufs = (refs[5:7], refs[7:9]), refs[9:11], refs[11:13]
    slots = crm_hbm.shape[0]
    halves = slots // 128
    steps = crmx // 8
    part = GROUP * crmx
    size = head[0].shape[0]
    here = size // crmx
    count = levels // here
    shift = [math.log(0.8 * 5.0 ** j) / 0.3 for j in range(SUB + 1)]

    def crm_copies(group):
        width = levels * crmx
        at = [pl.ds(pl.multiple_of(i * width + group * size, 128), size) for i in range(2)]
        return [pltpu.make_async_copy(crm_hbm.at[:, at[i]], crm_bufs[i].at[group - 1], crm_sems.at[group - 1, i]) for i in range(2)]

    def rate_copies(group):
        at = pl.ds(pl.multiple_of(group * size, 8), size)
        return [
            pltpu.make_async_copy(ref.at[at, :], coefs[i].at[group - 1], rate_sems.at[group - 1, i])
            for i, ref in enumerate((rate_hbm, both_hbm))
        ]

    def start(copies):
        for copy in copies:
            copy.start()

    def wait(copies):
        for copy in copies:
            copy.wait()

    def diffuse(group, k):
        for ref, source in zip(fields[k], crm_bufs):
            for q in range(size // part):
                cut = slice(q * part, (q + 1) * part)
                ref[cut, :] = diffusion(first_ref[...], source[group - 1, :, cut])

    for group in range(1, count):
        start(crm_copies(group))
        start(rate_copies(group))
    arrived = arrivals(dense, arrived_ref, slots, 4 * levels)
    push, wet, temp, moist = [arrived[i * levels:(i + 1) * levels] for i in range(4)]
    push, wet = push * (1.0 / SUB), wet * (1.0 / SUB)
    tables = [5.0 * (temp + push + shift[1]), 5.0 * (moist + wet)]
    for j in range(2, SUB + 1):
        tables += [5.0 ** j * (push + (shift[j] - shift[j - 1])), 5.0 ** j * wet]
    for i, table in enumerate(tables):
        for half in range(halves):
            rows_ref[half, i * levels:(i + 1) * levels] = table[:, half * 128:(half + 1) * 128]

    def unit(group, inner, half, sources):
        lanes = pl.ds(half * 128, 128)
        base = inner * crmx
        level = group * here + inner
        get = lambda ref, k: ref[pl.ds(base + 8 * k, 8), lanes]
        const = lambda i: rows_ref[half, pl.ds(level + i * levels, 8, stride=0), :]
        temp, moist = [[get(sources[i], k) + add for k in range(steps)] for i, add in enumerate((const(0), const(1)))]
        for j in range(1, SUB + 1):
            if j > 1:
                spread = []
                for field, add in ((temp, const(2 * j - 2)), (moist, const(2 * j - 1))):
                    after = pltpu.roll(field[0], 7, 0)
                    before = pltpu.roll(field[steps - 1], 1, 0)
                    ring = [before] + field + [after]
                    spread.append([((ring[k] + ring[k + 2]) + 3.0 * field[k]) + add for k in range(steps)])
                temp, moist = spread
            for k in range(steps):
                over = jnp.maximum(moist[k] - jnp.exp2((LOG / 5.0 ** j) * temp[k]), 0.0)
                moist[k] = moist[k] - get(sources[2], k) * over
                temp[k] = temp[k] + get(sources[3], k) * over
        for i, field in enumerate((temp, moist)):
            while len(field) > 1:
                field = [a + b for a, b in zip(field[0::2], field[1::2])]
            sums_ref[half, pl.ds(pl.multiple_of((i * levels + level) * 8, 8), 8), :] = field[0]

    def run(group, sources):
        for inner in range(here):
            for half in range(halves):
                unit(group, inner, half, sources)

    head[3][...] = 0.7 - 0.775 * (0.7 - head[2][...])
    wait(crm_copies(1))
    diffuse(1, 0)
    run(0, head)

    @pl.loop(0, (count - 1) // 2)
    def _(trip):
        for k in range(2):
            group = 1 + 2 * trip + k
            ahead = jnp.minimum(group + 1, count - 1)
            wait(rate_copies(group))
            if k == 0:
                wait(crm_copies(ahead))
            else:
                @pl.when(group + 1 < count)
                def _():
                    wait(crm_copies(group + 1))
            diffuse(ahead, 1 - k)
            run(group, (*fields[k], coefs[0].at[group - 1], coefs[1].at[group - 1]))

    total = 2 * levels
    for half in range(halves):
        summed = sums_ref[half, pl.ds(0, total, stride=8), :]
        for s in range(1, 8):
            summed = summed + sums_ref[half, pl.ds(s, total, stride=8), :]
        mean = summed * (1.0 / (crmx * 5.0 ** SUB))
        mean = jnp.concatenate([mean[:levels] - shift[SUB], mean[levels:]], axis=0)
        if dense is None:
            mean = jnp.concatenate([mean, jnp.zeros((256 - total, 128), F32)], axis=0)
            out_ref[pl.ds(half * 128, 128), :] = mean.T[:, :total]
            continue
        back, cap = dense[1], 8
        each = back * cap + 1
        for t in range(back):
            block = mean[t * 128:(t + 1) * 128].T
            for s in range(128 // cap):
                to = (half * (128 // cap) + s) * each + t * cap
                out_ref[to:to + cap, :] = block[s * cap:(s + 1) * cap]
        tail = jnp.concatenate([mean[back * 128:]] * cap, axis=0).T
        group = lax.broadcasted_iota(jnp.int32, (128, 128), 1) // (128 // cap)
        tail = jnp.where(group == lax.broadcasted_iota(jnp.int32, (128, 128), 0) % cap, tail, 0.0)
        for s in range(128 // cap):
            to = (half * (128 // cap) + s) * each + back * cap
            out_ref[to:to + 1, :] = jnp.sum(tail[s * cap:(s + 1) * cap], axis=0, keepdims=True)


def finish_kernel(dense, dyn_ref, place_ref, back_ref, out_ref):
    cdev = dyn_ref.shape[1]
    rows = lax.broadcasted_iota(jnp.int32, (back_ref.shape[0], cdev), 0)
    count = 1 if dense is None else dense[1] + 1
    hot = [jnp.where(rows == place_ref[i:i + 1, :], 1.0, 0.0).astype(BF16) for i in range(count)]
    means = select_dot(back_ref[...], jnp.concatenate(hot, axis=1), TN)
    if dense is None:
        out_ref[...] = dyn_ref[...] + means
        return
    back = dense[1]
    for t in range(back):
        out_ref[t * 128:(t + 1) * 128] = dyn_ref[t * 128:(t + 1) * 128] + means[:, t * cdev:(t + 1) * cdev]
    tail = means[:, back * cdev:]
    size = dyn_ref.shape[0] - back * 128
    rank = place_ref[back + 1:back + 2, :]
    mine = sum(jnp.where(rank == q, tail[q * size:(q + 1) * size], 0.0) for q in range(128 // size))
    out_ref[back * 128:] = dyn_ref[back * 128:] + mine


def local(state, neighbors, owner, crm_state, phase_mask):
    ndev = lax.axis_size(AXES)
    me = lax.axis_index(AXES)
    fields, levels, cdev = state.shape
    rows = fields * levels
    slots, wide = crm_state.shape
    crmx = wide // rows
    cap = slots // ndev
    flat = state.reshape(rows, cdev)
    sds = jax.ShapeDtypeStruct
    dense = (2 * rows // 128, rows // 128) if cap == 8 and rows % 128 == 16 else None
    out_each, back_each = 2 * rows * cap // 128, rows * cap // 128
    far = [(i, (i + 1) % ndev if i % 2 else (i - 1) % ndev) for i in range(ndev)]
    mate = [(i, i ^ 1) for i in range(ndev)]
    odd = me % 2
    first, last = flat[:, :REACH], flat[:, cdev - REACH:]
    to_far, to_mate = jnp.where(odd == 1, last, first), jnp.where(odd == 1, first, last)
    from_far = lax.ppermute(to_far, AXES, far)
    from_mate = lax.ppermute(to_mate, AXES, mate)

    base_shape = (slots, 2 * rows) if dense is None else (ndev * out_each, 128)
    wide_halo = 1 if dense is None else 2
    base, part, edge, share, place = pl.pallas_call(
        functools.partial(index_kernel, (cap, slots, cdev * ndev, dense)),
        in_specs=[VMEM] * 3,
        out_specs=[VMEM] * 5,
        out_shape=[
            sds(base_shape, F32),
            sds((rows, cdev), F32),
            sds((2 * REACH, cdev), BF16),
            sds((base_shape[0], 2 * REACH * wide_halo), BF16),
            sds((1 if dense is None else dense[1] + 2, cdev), jnp.int32),
        ],
        compiler_params=pltpu.CompilerParams(vmem_limit_bytes=12 << 20),
        name="index",
    )(flat, neighbors, owner.reshape(1, cdev))
    outgoing, dyn = pl.pallas_call(
        functools.partial(pack_kernel, dense),
        in_specs=[VMEM] * 6,
        out_specs=[VMEM] * 2,
        out_shape=[sds(base_shape, F32), sds((rows, cdev), F32)],
        scratch_shapes=[pltpu.VMEM((rows if dense is None else 128, 2 * REACH * wide_halo), F32)],
        compiler_params=pltpu.CompilerParams(vmem_limit_bytes=12 << 20),
        name="pack",
    )(base, part, edge, share, from_far, from_mate)
    arrived = lax.all_to_all(outgoing.reshape(ndev, cap * 2 * rows), AXES, split_axis=0, concat_axis=0, tiled=True)
    arrived = arrived.reshape(outgoing.shape)

    block = TRIO * GROUP * crmx
    count = levels * crmx // block
    take = lambda offset: pl.BlockSpec((slots, block), lambda g: (0, g + offset))
    rates_spec = [pl.BlockSpec((block, slots), lambda g: (g, 0))] * 2
    size = HEAD * crmx
    field, coef = sds((levels * crmx, slots), F32), sds((size, slots), F32)
    offset = levels // HEAD
    *rates, yt, ym, head_rate, first_matrix = pl.pallas_call(
        functools.partial(prepare_kernel, crmx),
        grid=(count,),
        in_specs=[take(0)] + [pl.BlockSpec((slots, size), lambda g, i=i: (0, i * offset)) for i in range(2)],
        out_specs=rates_spec + [VMEM] * 4,
        out_shape=[field] * 2 + [coef] * 3 + [sds((GROUP * crmx, GROUP * crmx), BF16)],
        compiler_params=pltpu.CompilerParams(vmem_limit_bytes=53000 << 10),
        cost_estimate=pl.CostEstimate(flops=2 * slots * levels * crmx * GROUP * crmx, transcendentals=0, bytes_accessed=6 * slots * wide),
        name="prepare",
    )(phase_mask, crm_state, crm_state)

    back = pl.pallas_call(
        functools.partial(physics_kernel, levels, crmx, dense),
        in_specs=[VMEM] * 5 + [pl.BlockSpec(memory_space=pl.ANY)] * 3,
        out_specs=VMEM,
        out_shape=sds((slots, rows) if dense is None else (ndev * back_each, 128), F32),
        scratch_shapes=[
            pltpu.VMEM((slots // 128, 2 * SUB * levels + 8, 128), F32),
            pltpu.VMEM((slots // 128, 8 * rows, 128), F32),
            pltpu.SemaphoreType.DMA((offset - 1, 2)),
            pltpu.SemaphoreType.DMA((offset - 1, 2)),
        ]
        + [pltpu.VMEM((size, slots), F32)] * 5
        + [pltpu.VMEM((offset - 1, size, slots), F32)] * 2
        + [pltpu.VMEM((offset - 1, slots, size), BF16)] * 2,
        compiler_params=pltpu.CompilerParams(vmem_limit_bytes=53000 << 10),
        name="physics",
    )(arrived, yt, ym, head_rate, first_matrix, crm_state, *rates)
    returned = lax.all_to_all(back.reshape(ndev, cap * rows), AXES, split_axis=0, concat_axis=0, tiled=True)
    out = pl.pallas_call(
        functools.partial(finish_kernel, dense),
        in_specs=[VMEM] * 3,
        out_specs=VMEM,
        out_shape=sds((rows, cdev), F32),
        compiler_params=pltpu.CompilerParams(vmem_limit_bytes=12 << 20),
        name="finish",
    )(dyn, place, returned.reshape(back.shape))
    return out.reshape(state.shape)


def solution(mesh):
    return jax.shard_map(
        local,
        mesh=mesh,
        in_specs=(
            P(None, None, AXES),
            P(None, AXES),
            P(AXES, None),
            P(AXES, None),
            P(AXES, None),
        ),
        out_specs=P(None, None, AXES),
        check_vma=False,
    )
```

```python
import functools
import math

import jax
import jax.numpy as jnp
from jax import lax
from jax.experimental import pallas as pl
from jax.experimental.pallas import tpu as pltpu
from jax.sharding import PartitionSpec as P


SUB = 4
REACH = 8
GROUP = 4
AXES = ("sec", "blk")
F32 = jnp.float32
BF16 = jnp.bfloat16
NT = (((1,), (1,)), ((), ()))
NN = (((1,), (0,)), ((), ()))
TN = (((0,), (0,)), ((), ()))
VMEM = pl.BlockSpec(memory_space=pltpu.VMEM)
LOG = 0.3 * math.log2(math.e)
TRIO = 3
HEAD = 8


def parts_of(x):
    high = x.astype(BF16)
    rest = x - high.astype(F32)
    middle = rest.astype(BF16)
    low = (rest - middle.astype(F32)).astype(BF16)
    return high, middle, low


def select_dot(x, onehot, dims, flip=False):
    axis = 1 - dims[0][1 if flip else 0][0]
    size = x.shape[axis]
    wide = jnp.concatenate(parts_of(x), axis=axis)
    pair = (onehot, wide) if flip else (wide, onehot)
    out = lax.dot_general(*pair, dims, preferred_element_type=F32)
    cut = (lambda i: out[:, i * size:(i + 1) * size]) if flip else (lambda i: out[i * size:(i + 1) * size])
    return (cut(0) + cut(1)) + cut(2)


def edges_kernel(state_ref, far_ref, mate_ref, same_ref):
    rows, cdev = state_ref.shape
    state = state_ref[...]
    same_ref[...] = state
    turned = jnp.concatenate([state, jnp.zeros((256 - rows, cdev), F32)], axis=0).T[:, :rows]
    first, last = turned[:REACH], turned[cdev - REACH:]
    odd = jnp.broadcast_to(lax.axis_index(AXES) % 2, first.shape) == 1
    far_ref[...] = jnp.where(odd, last, first)
    mate_ref[...] = jnp.where(odd, first, last)


def index_kernel(plan, state_ref, near_ref, owner_ref, base_ref, part_ref, edge_ref, share_ref, place_ref):
    cap, slots, total, dense = plan
    _, cdev = state_ref.shape
    state = state_ref[...]
    index = near_ref[...] - (lax.axis_index(AXES) * cdev - REACH)
    index = jnp.where(index < 0, index + total, index)
    index = jnp.where(index >= total, index - total, index)
    own = lax.broadcasted_iota(jnp.int32, (cdev, cdev), 0) + REACH
    edge = lax.broadcasted_iota(jnp.int32, (2 * REACH, cdev), 0)
    edge = jnp.where(edge < REACH, edge, edge + cdev)
    inner, outer = jnp.zeros((cdev, cdev), F32), jnp.zeros((2 * REACH, cdev), F32)
    for k in range(near_ref.shape[0]):
        row = index[k:k + 1, :]
        inner = inner + jnp.where(own == row, 1.0, 0.0)
        outer = outer + jnp.where(edge == row, 1.0, 0.0)
    outer = outer.astype(BF16)
    edge_ref[...] = outer
    part = 0.15 * (select_dot(state, inner.astype(BF16), NN) - 4.0 * state)
    part_ref[...] = part
    mine = jnp.broadcast_to(owner_ref[...], (cdev, cdev)).astype(F32)
    lower = lax.broadcasted_iota(jnp.int32, (cdev, cdev), 0) < lax.broadcasted_iota(jnp.int32, (cdev, cdev), 1)
    rank = jnp.sum(jnp.where((mine == mine.T) & lower, 1.0, 0.0), axis=0, keepdims=True).astype(jnp.int32)
    to = owner_ref[...]
    target = to * cap + rank
    load = jnp.concatenate([part, state], axis=0)

    def hot(count, place):
        return jnp.where(lax.broadcasted_iota(jnp.int32, (count, cdev), 0) == place, 1.0, 0.0).astype(BF16)

    def share(chosen):
        return lax.dot_general(chosen, outer, NT, preferred_element_type=F32).astype(BF16)

    if dense is None:
        place_ref[0:1, :] = target
        chosen = hot(slots, target)
        base_ref[...] = select_dot(load, chosen, NT, True)
        share_ref[...] = share(chosen)
        return
    tiles, back = dense
    for t in range(back):
        place_ref[t:t + 1, :] = to * (back * cap + 1) + t * cap + rank
    place_ref[back:back + 1, :] = to * (back * cap + 1) + back * cap
    place_ref[back + 1:back + 2, :] = rank
    each = tiles * cap + 2
    for t in range(2):
        share_ref[:, 2 * REACH * t:2 * REACH * (t + 1)] = share(hot(share_ref.shape[0], to * each + t * cap + rank))
    main = select_dot(load[:tiles * 128], hot(slots, target), NT, True)
    tail = load[tiles * 128:]
    blank = jnp.zeros_like(tail)
    tail = [jnp.concatenate([tail if i == q else blank for i in range(4)], axis=0) for q in range(4)]
    chosen = [hot(slots // 4, jnp.where(rank % 4 == q, target // 4, -1)) for q in range(4)]
    tail = select_dot(jnp.concatenate(tail, axis=1), jnp.concatenate(chosen, axis=1), NT, True)
    for s in range(slots // cap):
        for t in range(tiles):
            base_ref[s * each + t * cap:s * each + (t + 1) * cap, :] = main[s * cap:(s + 1) * cap, t * 128:(t + 1) * 128]
        base_ref[s * each + tiles * cap:(s + 1) * each, :] = tail[2 * s:2 * s + 2]


def pack_kernel(dense, base_ref, part_ref, edge_ref, share_ref, far_ref, mate_ref, out_ref, dyn_ref, halo_ref):
    rows = part_ref.shape[0]
    odd = jnp.broadcast_to(lax.axis_index(AXES) % 2, far_ref.shape) == 1
    before = 0.15 * jnp.where(odd, mate_ref[...], far_ref[...])
    after = 0.15 * jnp.where(odd, far_ref[...], mate_ref[...])
    for i, side in enumerate((before, after)):
        halo_ref[i * REACH:(i + 1) * REACH, :] = side if dense is None else side[:, :128]
        if dense is not None:
            pad = jnp.zeros((REACH, 256 - rows), F32)
            halo_ref[(2 + i) * REACH:(3 + i) * REACH, :] = jnp.concatenate([side[:, 128:], pad], axis=1)
    moved = select_dot(halo_ref[...], share_ref[...], NN, True)
    if dense is None:
        out_ref[:, :rows] = base_ref[:, :rows] + moved
        out_ref[:, rows:] = base_ref[:, rows:]
    else:
        out_ref[...] = base_ref[...] + moved
    dyn_ref[...] = part_ref[...] + (select_dot(before, edge_ref[:REACH], TN) + select_dot(after, edge_ref[REACH:], TN))


def near_matrix(rows, columns, crmx, centre, side):
    row = lax.broadcasted_iota(jnp.int32, (rows, columns), 0)
    col = lax.broadcasted_iota(jnp.int32, (rows, columns), 1)
    place = row & (crmx - 1)
    apart = (((place & 7) * (crmx // 8) + (place >> 3)) - col) & (crmx - 1)
    same = (row // crmx) == (col // crmx)
    off = jnp.where((apart == 1) | (apart == crmx - 1), side, 0.0)
    return jnp.where(same, jnp.where(apart == 0, centre, off), 0.0)


def diffusion(first, source):
    return lax.dot_general(first, source, NT, preferred_element_type=F32)


def prepare_kernel(crmx, mask_ref, ct_ref, cm_ref, rate_ref, both_ref, *head_refs):
    per = GROUP * crmx
    move = near_matrix(per, per, crmx, 1.0, 0.0).astype(BF16)
    for q in range(mask_ref.shape[1] // per):
        part = slice(q * per, (q + 1) * per)
        ice = lax.dot_general(move, mask_ref[:, part].astype(F32).astype(BF16), NT, preferred_element_type=F32)
        rate_ref[part, :] = 0.7 - 0.4 * ice
        both_ref[part, :] = 0.7 - 0.31 * ice

    @pl.when(pl.program_id(0) == 0)
    def _():
        yt_ref, ym_ref, head_rate_ref, first_ref = head_refs
        size = yt_ref.shape[0]
        first = near_matrix(per, per, crmx, 3.0, 1.0).astype(BF16)
        first_ref[...] = first
        for q in range(size // per):
            part = slice(q * per, (q + 1) * per)
            yt_ref[part, :] = diffusion(first, ct_ref[:, part])
            ym_ref[part, :] = diffusion(first, cm_ref[:, part])
        head_rate_ref[...] = rate_ref[:size]


def arrivals(dense, arrived_ref, slots, wide):
    columns = []
    if dense is None:
        for start in range(0, wide, 128):
            size = min(128, wide - start)
            block = arrived_ref[:, start:start + size]
            if size < 128:
                block = jnp.concatenate([block, jnp.zeros((slots, 128 - size), F32)], axis=1)
            columns.append(block.T[:size])
        return jnp.concatenate(columns, axis=0)
    tiles, cap = dense[0], 8
    each = tiles * cap + 2
    for t in range(tiles):
        block = [arrived_ref[s * each + t * cap:s * each + (t + 1) * cap, :] for s in range(slots // cap)]
        columns.append(jnp.concatenate(block, axis=0).T)
    low = lax.broadcasted_iota(jnp.int32, (cap, 128), 0) < 4
    block = []
    for s in range(slots // cap):
        pair = [arrived_ref[s * each + tiles * cap + i:s * each + tiles * cap + i + 1, :] for i in range(2)]
        block.append(jnp.where(low, *[jnp.broadcast_to(p, (cap, 128)) for p in pair]))
    tail = jnp.concatenate(block, axis=0).T
    which = lax.broadcasted_iota(jnp.int32, (32, slots), 1) % 4
    columns.append(sum(jnp.where(which == q, tail[q * 32:(q + 1) * 32], 0.0) for q in range(4)))
    return jnp.concatenate(columns, axis=0)


def physics_kernel(levels, crmx, dense, arrived_ref, *refs):
    head, (first_ref, crm_hbm, rate_hbm, both_hbm, out_ref), refs = refs[:3], refs[3:8], refs[8:]
    rows_ref, sums_ref, crm_sems, rate_sems = refs[:4]
    head = (*head, refs[4])
    fields, coefs, crm_bufs = (refs[5:7], refs[7:9]), refs[9:11], refs[11:13]
    slots = crm_hbm.shape[0]
    halves = slots // 128
    steps = crmx // 8
    part = GROUP * crmx
    size = head[0].shape[0]
    here = size // crmx
    count = levels // here
    shift = [math.log(0.8 * 5.0 ** j) / 0.3 for j in range(SUB + 1)]

    def crm_copies(group):
        width = levels * crmx
        at = [pl.ds(pl.multiple_of(i * width + group * size, 128), size) for i in range(2)]
        return [pltpu.make_async_copy(crm_hbm.at[:, at[i]], crm_bufs[i].at[group - 1], crm_sems.at[group - 1, i]) for i in range(2)]

    def rate_copies(group):
        at = pl.ds(pl.multiple_of(group * size, 8), size)
        return [
            pltpu.make_async_copy(ref.at[at, :], coefs[i].at[group - 1], rate_sems.at[group - 1, i])
            for i, ref in enumerate((rate_hbm, both_hbm))
        ]

    def start(copies):
        for copy in copies:
            copy.start()

    def wait(copies):
        for copy in copies:
            copy.wait()

    def diffuse(group, k):
        for ref, source in zip(fields[k], crm_bufs):
            for q in range(size // part):
                cut = slice(q * part, (q + 1) * part)
                ref[cut, :] = diffusion(first_ref[...], source[group - 1, :, cut])

    for group in range(1, count):
        start(crm_copies(group))
        start(rate_copies(group))
    arrived = arrivals(dense, arrived_ref, slots, 4 * levels)
    push, wet, temp, moist = [arrived[i * levels:(i + 1) * levels] for i in range(4)]
    push, wet = push * (1.0 / SUB), wet * (1.0 / SUB)
    tables = [5.0 * (temp + push + shift[1]), 5.0 * (moist + wet)]
    for j in range(2, SUB + 1):
        tables += [5.0 ** j * (push + (shift[j] - shift[j - 1])), 5.0 ** j * wet]
    for i, table in enumerate(tables):
        for half in range(halves):
            rows_ref[half, i * levels:(i + 1) * levels] = table[:, half * 128:(half + 1) * 128]

    def unit(group, inner, half, sources):
        lanes = pl.ds(half * 128, 128)
        base = inner * crmx
        level = group * here + inner
        get = lambda ref, k: ref[pl.ds(base + 8 * k, 8), lanes]
        const = lambda i: rows_ref[half, pl.ds(level + i * levels, 8, stride=0), :]
        temp, moist = [[get(sources[i], k) + add for k in range(steps)] for i, add in enumerate((const(0), const(1)))]
        for j in range(1, SUB + 1):
            if j > 1:
                spread = []
                for field, add in ((temp, const(2 * j - 2)), (moist, const(2 * j - 1))):
                    after = pltpu.roll(field[0], 7, 0)
                    before = pltpu.roll(field[steps - 1], 1, 0)
                    ring = [before] + field + [after]
                    spread.append([((ring[k] + ring[k + 2]) + 3.0 * field[k]) + add for k in range(steps)])
                temp, moist = spread
            for k in range(steps):
                over = jnp.maximum(moist[k] - jnp.exp2((LOG / 5.0 ** j) * temp[k]), 0.0)
                moist[k] = moist[k] - get(sources[2], k) * over
                temp[k] = temp[k] + get(sources[3], k) * over
        for i, field in enumerate((temp, moist)):
            while len(field) > 1:
                field = [a + b for a, b in zip(field[0::2], field[1::2])]
            sums_ref[half, pl.ds(pl.multiple_of((i * levels + level) * 8, 8), 8), :] = field[0]

    def run(group, sources):
        for inner in range(here):
            for half in range(halves):
                unit(group, inner, half, sources)

    head[3][...] = 0.7 - 0.775 * (0.7 - head[2][...])
    wait(crm_copies(1))
    diffuse(1, 0)
    run(0, head)

    @pl.loop(0, (count - 1) // 2)
    def _(trip):
        for k in range(2):
            group = 1 + 2 * trip + k
            ahead = jnp.minimum(group + 1, count - 1)
            wait(rate_copies(group))
            if k == 0:
                wait(crm_copies(ahead))
            else:
                @pl.when(group + 1 < count)
                def _():
                    wait(crm_copies(group + 1))
            diffuse(ahead, 1 - k)
            run(group, (*fields[k], coefs[0].at[group - 1], coefs[1].at[group - 1]))

    total = 2 * levels
    for half in range(halves):
        summed = sums_ref[half, pl.ds(0, total, stride=8), :]
        for s in range(1, 8):
            summed = summed + sums_ref[half, pl.ds(s, total, stride=8), :]
        mean = summed * (1.0 / (crmx * 5.0 ** SUB))
        mean = jnp.concatenate([mean[:levels] - shift[SUB], mean[levels:]], axis=0)
        if dense is None:
            mean = jnp.concatenate([mean, jnp.zeros((256 - total, 128), F32)], axis=0)
            out_ref[pl.ds(half * 128, 128), :] = mean.T[:, :total]
            continue
        back, cap = dense[1], 8
        each = back * cap + 1
        for t in range(back):
            block = mean[t * 128:(t + 1) * 128].T
            for s in range(128 // cap):
                to = (half * (128 // cap) + s) * each + t * cap
                out_ref[to:to + cap, :] = block[s * cap:(s + 1) * cap]
        tail = jnp.concatenate([mean[back * 128:]] * cap, axis=0).T
        group = lax.broadcasted_iota(jnp.int32, (128, 128), 1) // (128 // cap)
        tail = jnp.where(group == lax.broadcasted_iota(jnp.int32, (128, 128), 0) % cap, tail, 0.0)
        for s in range(128 // cap):
            to = (half * (128 // cap) + s) * each + back * cap
            out_ref[to:to + 1, :] = jnp.sum(tail[s * cap:(s + 1) * cap], axis=0, keepdims=True)


def finish_kernel(dense, dyn_ref, place_ref, back_ref, out_ref):
    cdev = dyn_ref.shape[1]
    rows = lax.broadcasted_iota(jnp.int32, (back_ref.shape[0], cdev), 0)
    count = 1 if dense is None else dense[1] + 1
    hot = [jnp.where(rows == place_ref[i:i + 1, :], 1.0, 0.0).astype(BF16) for i in range(count)]
    means = select_dot(back_ref[...], jnp.concatenate(hot, axis=1), TN)
    if dense is None:
        out_ref[...] = dyn_ref[...] + means
        return
    back = dense[1]
    for t in range(back):
        out_ref[t * 128:(t + 1) * 128] = dyn_ref[t * 128:(t + 1) * 128] + means[:, t * cdev:(t + 1) * cdev]
    tail = means[:, back * cdev:]
    size = dyn_ref.shape[0] - back * 128
    rank = place_ref[back + 1:back + 2, :]
    mine = sum(jnp.where(rank == q, tail[q * size:(q + 1) * size], 0.0) for q in range(128 // size))
    out_ref[back * 128:] = dyn_ref[back * 128:] + mine


def local(state, neighbors, owner, crm_state, phase_mask):
    ndev = lax.axis_size(AXES)
    fields, levels, cdev = state.shape
    rows = fields * levels
    slots, wide = crm_state.shape
    crmx = wide // rows
    cap = slots // ndev
    flat = state.reshape(rows, cdev)
    sds = jax.ShapeDtypeStruct
    dense = (2 * rows // 128, rows // 128) if cap == 8 and rows % 128 == 16 else None
    out_each, back_each = 2 * rows * cap // 128, rows * cap // 128
    far = [(i, (i + 1) % ndev if i % 2 else (i - 1) % ndev) for i in range(ndev)]
    mate = [(i, i ^ 1) for i in range(ndev)]
    to_far, to_mate, same = pl.pallas_call(
        edges_kernel,
        in_specs=[VMEM],
        out_specs=[VMEM] * 3,
        out_shape=[sds((REACH, rows), F32)] * 2 + [sds((rows, cdev), F32)],
        compiler_params=pltpu.CompilerParams(vmem_limit_bytes=8 << 20),
        name="edges",
    )(flat)
    from_far = lax.ppermute(to_far, AXES, far)
    from_mate = lax.ppermute(to_mate, AXES, mate)

    base_shape = (slots, 2 * rows) if dense is None else (ndev * out_each, 128)
    wide_halo = 1 if dense is None else 2
    base, part, edge, share, place = pl.pallas_call(
        functools.partial(index_kernel, (cap, slots, cdev * ndev, dense)),
        in_specs=[VMEM] * 3,
        out_specs=[VMEM] * 5,
        out_shape=[
            sds(base_shape, F32),
            sds((rows, cdev), F32),
            sds((2 * REACH, cdev), BF16),
            sds((base_shape[0], 2 * REACH * wide_halo), BF16),
            sds((1 if dense is None else dense[1] + 2, cdev), jnp.int32),
        ],
        compiler_params=pltpu.CompilerParams(vmem_limit_bytes=12 << 20),
        name="index",
    )(same, neighbors, owner.reshape(1, cdev))
    outgoing, dyn = pl.pallas_call(
        functools.partial(pack_kernel, dense),
        in_specs=[VMEM] * 6,
        out_specs=[VMEM] * 2,
        out_shape=[sds(base_shape, F32), sds((rows, cdev), F32)],
        scratch_shapes=[pltpu.VMEM((2 * REACH * wide_halo, rows if dense is None else 128), F32)],
        compiler_params=pltpu.CompilerParams(vmem_limit_bytes=12 << 20),
        name="pack",
    )(base, part, edge, share, from_far, from_mate)
    arrived = lax.all_to_all(outgoing.reshape(ndev, cap * 2 * rows), AXES, split_axis=0, concat_axis=0, tiled=True)
    arrived = arrived.reshape(outgoing.shape)

    block = TRIO * GROUP * crmx
    count = levels * crmx // block
    take = lambda offset: pl.BlockSpec((slots, block), lambda g: (0, g + offset))
    rates_spec = [pl.BlockSpec((block, slots), lambda g: (g, 0))] * 2
    size = HEAD * crmx
    field, coef = sds((levels * crmx, slots), F32), sds((size, slots), F32)
    offset = levels // HEAD
    *rates, yt, ym, head_rate, first_matrix = pl.pallas_call(
        functools.partial(prepare_kernel, crmx),
        grid=(count,),
        in_specs=[take(0)] + [pl.BlockSpec((slots, size), lambda g, i=i: (0, i * offset)) for i in range(2)],
        out_specs=rates_spec + [VMEM] * 4,
        out_shape=[field] * 2 + [coef] * 3 + [sds((GROUP * crmx, GROUP * crmx), BF16)],
        compiler_params=pltpu.CompilerParams(vmem_limit_bytes=53000 << 10),
        cost_estimate=pl.CostEstimate(flops=2 * slots * levels * crmx * GROUP * crmx, transcendentals=0, bytes_accessed=6 * slots * wide),
        name="prepare",
    )(phase_mask, crm_state, crm_state)

    back = pl.pallas_call(
        functools.partial(physics_kernel, levels, crmx, dense),
        in_specs=[VMEM] * 5 + [pl.BlockSpec(memory_space=pl.ANY)] * 3,
        out_specs=VMEM,
        out_shape=sds((slots, rows) if dense is None else (ndev * back_each, 128), F32),
        scratch_shapes=[
            pltpu.VMEM((slots // 128, 2 * SUB * levels + 8, 128), F32),
            pltpu.VMEM((slots // 128, 8 * rows, 128), F32),
            pltpu.SemaphoreType.DMA((offset - 1, 2)),
            pltpu.SemaphoreType.DMA((offset - 1, 2)),
        ]
        + [pltpu.VMEM((size, slots), F32)] * 5
        + [pltpu.VMEM((offset - 1, size, slots), F32)] * 2
        + [pltpu.VMEM((offset - 1, slots, size), BF16)] * 2,
        compiler_params=pltpu.CompilerParams(vmem_limit_bytes=53000 << 10),
        name="physics",
    )(arrived, yt, ym, head_rate, first_matrix, crm_state, *rates)
    returned = lax.all_to_all(back.reshape(ndev, cap * rows), AXES, split_axis=0, concat_axis=0, tiled=True)
    out = pl.pallas_call(
        functools.partial(finish_kernel, dense),
        in_specs=[VMEM] * 3,
        out_specs=VMEM,
        out_shape=sds((rows, cdev), F32),
        compiler_params=pltpu.CompilerParams(vmem_limit_bytes=12 << 20),
        name="finish",
    )(dyn, place, returned.reshape(back.shape))
    return out.reshape(state.shape)


def solution(mesh):
    return jax.shard_map(
        local,
        mesh=mesh,
        in_specs=(
            P(None, None, AXES),
            P(None, AXES),
            P(AXES, None),
            P(AXES, None),
            P(AXES, None),
        ),
        out_specs=P(None, None, AXES),
        check_vma=False,
    )
```

```python
import functools
import math

import jax
import jax.numpy as jnp
from jax import lax
from jax.experimental import pallas as pl
from jax.experimental.pallas import tpu as pltpu
from jax.sharding import PartitionSpec as P


SUB = 4
REACH = 8
GROUP = 4
AXES = ("sec", "blk")
F32 = jnp.float32
BF16 = jnp.bfloat16
NT = (((1,), (1,)), ((), ()))
NN = (((1,), (0,)), ((), ()))
TN = (((0,), (0,)), ((), ()))
VMEM = pl.BlockSpec(memory_space=pltpu.VMEM)
LOG = 0.3 * math.log2(math.e)
PREP = 24
HEAD = 8


def parts_of(x):
    high = x.astype(BF16)
    rest = x - high.astype(F32)
    middle = rest.astype(BF16)
    low = (rest - middle.astype(F32)).astype(BF16)
    return high, middle, low


def select_dot(x, onehot, dims, flip=False):
    axis = 1 - dims[0][1 if flip else 0][0]
    size = x.shape[axis]
    wide = jnp.concatenate(parts_of(x), axis=axis)
    pair = (onehot, wide) if flip else (wide, onehot)
    out = lax.dot_general(*pair, dims, preferred_element_type=F32)
    cut = (lambda i: out[:, i * size:(i + 1) * size]) if flip else (lambda i: out[i * size:(i + 1) * size])
    return (cut(0) + cut(1)) + cut(2)


def edges_kernel(state_ref, far_ref, mate_ref, same_ref):
    rows, cdev = state_ref.shape
    state = state_ref[...]
    same_ref[...] = state
    turned = jnp.concatenate([state, jnp.zeros((256 - rows, cdev), F32)], axis=0).T[:, :rows]
    first, last = turned[:REACH], turned[cdev - REACH:]
    odd = jnp.broadcast_to(lax.axis_index(AXES) % 2, first.shape) == 1
    far_ref[...] = jnp.where(odd, last, first)
    mate_ref[...] = jnp.where(odd, first, last)


def index_kernel(plan, state_ref, near_ref, owner_ref, base_ref, part_ref, edge_ref, share_ref, place_ref):
    cap, slots, total, dense = plan
    _, cdev = state_ref.shape
    state = state_ref[...]
    index = near_ref[...] - (lax.axis_index(AXES) * cdev - REACH)
    index = jnp.where(index < 0, index + total, index)
    index = jnp.where(index >= total, index - total, index)
    own = lax.broadcasted_iota(jnp.int32, (cdev, cdev), 0) + REACH
    edge = lax.broadcasted_iota(jnp.int32, (2 * REACH, cdev), 0)
    edge = jnp.where(edge < REACH, edge, edge + cdev)
    inner, outer = jnp.zeros((cdev, cdev), F32), jnp.zeros((2 * REACH, cdev), F32)
    for k in range(near_ref.shape[0]):
        row = index[k:k + 1, :]
        inner = inner + jnp.where(own == row, 1.0, 0.0)
        outer = outer + jnp.where(edge == row, 1.0, 0.0)
    outer = outer.astype(BF16)
    edge_ref[...] = outer
    part = 0.15 * (select_dot(state, inner.astype(BF16), NN) - 4.0 * state)
    part_ref[...] = part
    mine = jnp.broadcast_to(owner_ref[...], (cdev, cdev)).astype(F32)
    lower = lax.broadcasted_iota(jnp.int32, (cdev, cdev), 0) < lax.broadcasted_iota(jnp.int32, (cdev, cdev), 1)
    rank = jnp.sum(jnp.where((mine == mine.T) & lower, 1.0, 0.0), axis=0, keepdims=True).astype(jnp.int32)
    to = owner_ref[...]
    target = to * cap + rank
    load = jnp.concatenate([part, state], axis=0)

    def hot(count, place):
        return jnp.where(lax.broadcasted_iota(jnp.int32, (count, cdev), 0) == place, 1.0, 0.0).astype(BF16)

    def share(chosen):
        return lax.dot_general(chosen, outer, NT, preferred_element_type=F32).astype(BF16)

    if dense is None:
        place_ref[0:1, :] = target
        chosen = hot(slots, target)
        base_ref[...] = select_dot(load, chosen, NT, True)
        share_ref[...] = share(chosen)
        return
    tiles, back = dense
    for t in range(back):
        place_ref[t:t + 1, :] = to * (back * cap + 1) + t * cap + rank
    place_ref[back:back + 1, :] = to * (back * cap + 1) + back * cap
    place_ref[back + 1:back + 2, :] = rank
    each = tiles * cap + 2
    for t in range(2):
        share_ref[:, 2 * REACH * t:2 * REACH * (t + 1)] = share(hot(share_ref.shape[0], to * each + t * cap + rank))
    main = select_dot(load[:tiles * 128], hot(slots, target), NT, True)
    tail = load[tiles * 128:]
    blank = jnp.zeros_like(tail)
    tail = [jnp.concatenate([tail if i == q else blank for i in range(4)], axis=0) for q in range(4)]
    chosen = [hot(slots // 4, jnp.where(rank % 4 == q, target // 4, -1)) for q in range(4)]
    tail = select_dot(jnp.concatenate(tail, axis=1), jnp.concatenate(chosen, axis=1), NT, True)
    for s in range(slots // cap):
        for t in range(tiles):
            base_ref[s * each + t * cap:s * each + (t + 1) * cap, :] = main[s * cap:(s + 1) * cap, t * 128:(t + 1) * 128]
        base_ref[s * each + tiles * cap:(s + 1) * each, :] = tail[2 * s:2 * s + 2]


def pack_kernel(dense, base_ref, part_ref, edge_ref, share_ref, far_ref, mate_ref, out_ref, dyn_ref, halo_ref):
    rows = part_ref.shape[0]
    odd = jnp.broadcast_to(lax.axis_index(AXES) % 2, far_ref.shape) == 1
    before = 0.15 * jnp.where(odd, mate_ref[...], far_ref[...])
    after = 0.15 * jnp.where(odd, far_ref[...], mate_ref[...])
    for i, side in enumerate((before, after)):
        halo_ref[i * REACH:(i + 1) * REACH, :] = side if dense is None else side[:, :128]
        if dense is not None:
            pad = jnp.zeros((REACH, 256 - rows), F32)
            halo_ref[(2 + i) * REACH:(3 + i) * REACH, :] = jnp.concatenate([side[:, 128:], pad], axis=1)
    moved = select_dot(halo_ref[...], share_ref[...], NN, True)
    if dense is None:
        out_ref[:, :rows] = base_ref[:, :rows] + moved
        out_ref[:, rows:] = base_ref[:, rows:]
    else:
        out_ref[...] = base_ref[...] + moved
    dyn_ref[...] = part_ref[...] + (select_dot(before, edge_ref[:REACH], TN) + select_dot(after, edge_ref[REACH:], TN))


def near_matrix(rows, columns, crmx, centre, side):
    row = lax.broadcasted_iota(jnp.int32, (rows, columns), 0)
    col = lax.broadcasted_iota(jnp.int32, (rows, columns), 1)
    place = row & (crmx - 1)
    apart = (((place & 7) * (crmx // 8) + (place >> 3)) - col) & (crmx - 1)
    same = (row // crmx) == (col // crmx)
    off = jnp.where((apart == 1) | (apart == crmx - 1), side, 0.0)
    return jnp.where(same, jnp.where(apart == 0, centre, off), 0.0)


def diffusion(first, source):
    return lax.dot_general(first, source, NT, preferred_element_type=F32)


def prepare_kernel(crmx, mask_ref, ct_ref, cm_ref, rate_ref, both_ref, *refs):
    yt_ref, ym_ref, head_rate_ref, first_ref, move_ref = refs
    per = GROUP * crmx
    size = yt_ref.shape[0]

    @pl.when(pl.program_id(0) == 0)
    def _():
        move_ref[...] = near_matrix(per, per, crmx, 1.0, 0.0).astype(BF16)
        first = near_matrix(per, per, crmx, 3.0, 1.0).astype(BF16)
        first_ref[...] = first
        for q in range(size // per):
            part = slice(q * per, (q + 1) * per)
            yt_ref[part, :] = diffusion(first, ct_ref[:, part])
            ym_ref[part, :] = diffusion(first, cm_ref[:, part])

    for q in range(mask_ref.shape[1] // per):
        part = slice(q * per, (q + 1) * per)
        ice = mask_ref[:, part].astype(F32).astype(BF16)
        ice = lax.dot_general(move_ref[...], ice, NT, preferred_element_type=F32)
        rate_ref[part, :] = 0.7 - 0.4 * ice
        both_ref[part, :] = 0.7 - 0.31 * ice

    @pl.when(pl.program_id(0) == 0)
    def _():
        head_rate_ref[...] = rate_ref[:size]


def arrivals(dense, arrived_ref, slots, wide):
    columns = []
    if dense is None:
        for start in range(0, wide, 128):
            size = min(128, wide - start)
            block = arrived_ref[:, start:start + size]
            if size < 128:
                block = jnp.concatenate([block, jnp.zeros((slots, 128 - size), F32)], axis=1)
            columns.append(block.T[:size])
        return jnp.concatenate(columns, axis=0)
    tiles, cap = dense[0], 8
    each = tiles * cap + 2
    for t in range(tiles):
        block = [arrived_ref[s * each + t * cap:s * each + (t + 1) * cap, :] for s in range(slots // cap)]
        columns.append(jnp.concatenate(block, axis=0).T)
    low = lax.broadcasted_iota(jnp.int32, (cap, 128), 0) < 4
    block = []
    for s in range(slots // cap):
        pair = [arrived_ref[s * each + tiles * cap + i:s * each + tiles * cap + i + 1, :] for i in range(2)]
        block.append(jnp.where(low, *[jnp.broadcast_to(p, (cap, 128)) for p in pair]))
    tail = jnp.concatenate(block, axis=0).T
    which = lax.broadcasted_iota(jnp.int32, (32, slots), 1) % 4
    columns.append(sum(jnp.where(which == q, tail[q * 32:(q + 1) * 32], 0.0) for q in range(4)))
    return jnp.concatenate(columns, axis=0)


def physics_kernel(levels, crmx, dense, arrived_ref, *refs):
    head, (first_ref, crm_hbm, rate_hbm, both_hbm, out_ref), refs = refs[:3], refs[3:8], refs[8:]
    rows_ref, sums_ref, crm_sems, rate_sems = refs[:4]
    head = (*head, refs[4])
    fields, coefs, crm_bufs = (refs[5:7], refs[7:9]), refs[9:11], refs[11:13]
    slots = crm_hbm.shape[0]
    halves = slots // 128
    steps = crmx // 8
    part = GROUP * crmx
    size = head[0].shape[0]
    here = size // crmx
    count = levels // here
    shift = [math.log(0.8 * 5.0 ** j) / 0.3 for j in range(SUB + 1)]

    def crm_copies(group):
        width = levels * crmx
        at = [pl.ds(pl.multiple_of(i * width + group * size, 128), size) for i in range(2)]
        return [pltpu.make_async_copy(crm_hbm.at[:, at[i]], crm_bufs[i].at[group - 1], crm_sems.at[group - 1, i]) for i in range(2)]

    def rate_copies(group):
        at = pl.ds(pl.multiple_of(group * size, 8), size)
        return [
            pltpu.make_async_copy(ref.at[at, :], coefs[i].at[group - 1], rate_sems.at[group - 1, i])
            for i, ref in enumerate((rate_hbm, both_hbm))
        ]

    def start(copies):
        for copy in copies:
            copy.start()

    def wait(copies):
        for copy in copies:
            copy.wait()

    def diffuse(group, k):
        for ref, source in zip(fields[k], crm_bufs):
            for q in range(size // part):
                cut = slice(q * part, (q + 1) * part)
                ref[cut, :] = diffusion(first_ref[...], source[group - 1, :, cut])

    for group in range(1, count):
        start(crm_copies(group))
        start(rate_copies(group))
    arrived = arrivals(dense, arrived_ref, slots, 4 * levels)
    push, wet, temp, moist = [arrived[i * levels:(i + 1) * levels] for i in range(4)]
    push, wet = push * (1.0 / SUB), wet * (1.0 / SUB)
    tables = [5.0 * (temp + push + shift[1]), 5.0 * (moist + wet)]
    for j in range(2, SUB + 1):
        tables += [5.0 ** j * (push + (shift[j] - shift[j - 1])), 5.0 ** j * wet]
    for i, table in enumerate(tables):
        for half in range(halves):
            rows_ref[half, i * levels:(i + 1) * levels] = table[:, half * 128:(half + 1) * 128]

    def unit(group, inner, half, sources):
        lanes = pl.ds(half * 128, 128)
        base = inner * crmx
        level = group * here + inner
        get = lambda ref, k: ref[pl.ds(base + 8 * k, 8), lanes]
        const = lambda i: rows_ref[half, pl.ds(level + i * levels, 8, stride=0), :]
        temp, moist = [[get(sources[i], k) + add for k in range(steps)] for i, add in enumerate((const(0), const(1)))]
        for j in range(1, SUB + 1):
            if j > 1:
                spread = []
                for field, add in ((temp, const(2 * j - 2)), (moist, const(2 * j - 1))):
                    after = pltpu.roll(field[0], 7, 0)
                    before = pltpu.roll(field[steps - 1], 1, 0)
                    ring = [before] + field + [after]
                    spread.append([((ring[k] + ring[k + 2]) + 3.0 * field[k]) + add for k in range(steps)])
                temp, moist = spread
            for k in range(steps):
                over = jnp.maximum(moist[k] - jnp.exp2((LOG / 5.0 ** j) * temp[k]), 0.0)
                moist[k] = moist[k] - get(sources[2], k) * over
                temp[k] = temp[k] + get(sources[3], k) * over
        for i, field in enumerate((temp, moist)):
            while len(field) > 1:
                field = [a + b for a, b in zip(field[0::2], field[1::2])]
            sums_ref[half, pl.ds(pl.multiple_of((i * levels + level) * 8, 8), 8), :] = field[0]

    def run(group, sources):
        for inner in range(here):
            for half in range(halves):
                unit(group, inner, half, sources)

    head[3][...] = 0.7 - 0.775 * (0.7 - head[2][...])
    wait(crm_copies(1))
    diffuse(1, 0)
    run(0, head)

    @pl.loop(0, (count - 1) // 2)
    def _(trip):
        for k in range(2):
            group = 1 + 2 * trip + k
            ahead = jnp.minimum(group + 1, count - 1)
            wait(rate_copies(group))
            if k == 0:
                wait(crm_copies(ahead))
            else:
                @pl.when(group + 1 < count)
                def _():
                    wait(crm_copies(group + 1))
            diffuse(ahead, 1 - k)
            run(group, (*fields[k], coefs[0].at[group - 1], coefs[1].at[group - 1]))

    total = 2 * levels
    for half in range(halves):
        summed = sums_ref[half, pl.ds(0, total, stride=8), :]
        for s in range(1, 8):
            summed = summed + sums_ref[half, pl.ds(s, total, stride=8), :]
        mean = summed * (1.0 / (crmx * 5.0 ** SUB))
        mean = jnp.concatenate([mean[:levels] - shift[SUB], mean[levels:]], axis=0)
        if dense is None:
            mean = jnp.concatenate([mean, jnp.zeros((256 - total, 128), F32)], axis=0)
            out_ref[pl.ds(half * 128, 128), :] = mean.T[:, :total]
            continue
        back, cap = dense[1], 8
        each = back * cap + 1
        for t in range(back):
            block = mean[t * 128:(t + 1) * 128].T
            for s in range(128 // cap):
                to = (half * (128 // cap) + s) * each + t * cap
                out_ref[to:to + cap, :] = block[s * cap:(s + 1) * cap]
        tail = jnp.concatenate([mean[back * 128:]] * cap, axis=0).T
        group = lax.broadcasted_iota(jnp.int32, (128, 128), 1) // (128 // cap)
        tail = jnp.where(group == lax.broadcasted_iota(jnp.int32, (128, 128), 0) % cap, tail, 0.0)
        for s in range(128 // cap):
            to = (half * (128 // cap) + s) * each + back * cap
            out_ref[to:to + 1, :] = jnp.sum(tail[s * cap:(s + 1) * cap], axis=0, keepdims=True)


def finish_kernel(dense, dyn_ref, place_ref, back_ref, out_ref):
    cdev = dyn_ref.shape[1]
    rows = lax.broadcasted_iota(jnp.int32, (back_ref.shape[0], cdev), 0)
    count = 1 if dense is None else dense[1] + 1
    hot = [jnp.where(rows == place_ref[i:i + 1, :], 1.0, 0.0).astype(BF16) for i in range(count)]
    means = select_dot(back_ref[...], jnp.concatenate(hot, axis=1), TN)
    if dense is None:
        out_ref[...] = dyn_ref[...] + means
        return
    back = dense[1]
    for t in range(back):
        out_ref[t * 128:(t + 1) * 128] = dyn_ref[t * 128:(t + 1) * 128] + means[:, t * cdev:(t + 1) * cdev]
    tail = means[:, back * cdev:]
    size = dyn_ref.shape[0] - back * 128
    rank = place_ref[back + 1:back + 2, :]
    mine = sum(jnp.where(rank == q, tail[q * size:(q + 1) * size], 0.0) for q in range(128 // size))
    out_ref[back * 128:] = dyn_ref[back * 128:] + mine


def local(state, neighbors, owner, crm_state, phase_mask):
    ndev = lax.axis_size(AXES)
    fields, levels, cdev = state.shape
    rows = fields * levels
    slots, wide = crm_state.shape
    crmx = wide // rows
    cap = slots // ndev
    flat = state.reshape(rows, cdev)
    sds = jax.ShapeDtypeStruct
    dense = (2 * rows // 128, rows // 128) if cap == 8 and rows % 128 == 16 else None
    out_each, back_each = 2 * rows * cap // 128, rows * cap // 128
    far = [(i, (i + 1) % ndev if i % 2 else (i - 1) % ndev) for i in range(ndev)]
    mate = [(i, i ^ 1) for i in range(ndev)]
    to_far, to_mate, same = pl.pallas_call(
        edges_kernel,
        in_specs=[VMEM],
        out_specs=[VMEM] * 3,
        out_shape=[sds((REACH, rows), F32)] * 2 + [sds((rows, cdev), F32)],
        compiler_params=pltpu.CompilerParams(vmem_limit_bytes=8 << 20),
        name="edges",
    )(flat)
    from_far = lax.ppermute(to_far, AXES, far)
    from_mate = lax.ppermute(to_mate, AXES, mate)

    base_shape = (slots, 2 * rows) if dense is None else (ndev * out_each, 128)
    wide_halo = 1 if dense is None else 2
    base, part, edge, share, place = pl.pallas_call(
        functools.partial(index_kernel, (cap, slots, cdev * ndev, dense)),
        in_specs=[VMEM] * 3,
        out_specs=[VMEM] * 5,
        out_shape=[
            sds(base_shape, F32),
            sds((rows, cdev), F32),
            sds((2 * REACH, cdev), BF16),
            sds((base_shape[0], 2 * REACH * wide_halo), BF16),
            sds((1 if dense is None else dense[1] + 2, cdev), jnp.int32),
        ],
        compiler_params=pltpu.CompilerParams(vmem_limit_bytes=12 << 20),
        name="index",
    )(same, neighbors, owner.reshape(1, cdev))
    outgoing, dyn = pl.pallas_call(
        functools.partial(pack_kernel, dense),
        in_specs=[VMEM] * 6,
        out_specs=[VMEM] * 2,
        out_shape=[sds(base_shape, F32), sds((rows, cdev), F32)],
        scratch_shapes=[pltpu.VMEM((2 * REACH * wide_halo, rows if dense is None else 128), F32)],
        compiler_params=pltpu.CompilerParams(vmem_limit_bytes=12 << 20),
        name="pack",
    )(base, part, edge, share, from_far, from_mate)
    arrived = lax.all_to_all(outgoing.reshape(ndev, cap * 2 * rows), AXES, split_axis=0, concat_axis=0, tiled=True)
    arrived = arrived.reshape(outgoing.shape)

    block = PREP * crmx
    count = levels * crmx // block
    take = lambda offset: pl.BlockSpec((slots, block), lambda g: (0, g + offset))
    rates_spec = [pl.BlockSpec((block, slots), lambda g: (g, 0))] * 2
    size = HEAD * crmx
    field, coef = sds((levels * crmx, slots), F32), sds((size, slots), F32)
    offset = levels // HEAD
    *rates, yt, ym, head_rate, first_matrix = pl.pallas_call(
        functools.partial(prepare_kernel, crmx),
        grid=(count,),
        in_specs=[take(0)] + [pl.BlockSpec((slots, size), lambda g, i=i: (0, i * offset)) for i in range(2)],
        out_specs=rates_spec + [VMEM] * 4,
        out_shape=[field] * 2 + [coef] * 3 + [sds((GROUP * crmx, GROUP * crmx), BF16)],
        scratch_shapes=[pltpu.VMEM((GROUP * crmx, GROUP * crmx), BF16)],
        compiler_params=pltpu.CompilerParams(vmem_limit_bytes=53000 << 10),
        cost_estimate=pl.CostEstimate(flops=2 * slots * levels * crmx * GROUP * crmx, transcendentals=0, bytes_accessed=6 * slots * wide),
        name="prepare",
    )(phase_mask, crm_state, crm_state)

    back = pl.pallas_call(
        functools.partial(physics_kernel, levels, crmx, dense),
        in_specs=[VMEM] * 5 + [pl.BlockSpec(memory_space=pl.ANY)] * 3,
        out_specs=VMEM,
        out_shape=sds((slots, rows) if dense is None else (ndev * back_each, 128), F32),
        scratch_shapes=[
            pltpu.VMEM((slots // 128, 2 * SUB * levels + 8, 128), F32),
            pltpu.VMEM((slots // 128, 8 * rows, 128), F32),
            pltpu.SemaphoreType.DMA((offset - 1, 2)),
            pltpu.SemaphoreType.DMA((offset - 1, 2)),
        ]
        + [pltpu.VMEM((size, slots), F32)] * 5
        + [pltpu.VMEM((offset - 1, size, slots), F32)] * 2
        + [pltpu.VMEM((offset - 1, slots, size), BF16)] * 2,
        compiler_params=pltpu.CompilerParams(vmem_limit_bytes=53000 << 10),
        name="physics",
    )(arrived, yt, ym, head_rate, first_matrix, crm_state, *rates)
    returned = lax.all_to_all(back.reshape(ndev, cap * rows), AXES, split_axis=0, concat_axis=0, tiled=True)
    out = pl.pallas_call(
        functools.partial(finish_kernel, dense),
        in_specs=[VMEM] * 3,
        out_specs=VMEM,
        out_shape=sds((rows, cdev), F32),
        compiler_params=pltpu.CompilerParams(vmem_limit_bytes=12 << 20),
        name="finish",
    )(dyn, place, returned.reshape(back.shape))
    return out.reshape(state.shape)


def solution(mesh):
    return jax.shard_map(
        local,
        mesh=mesh,
        in_specs=(
            P(None, None, AXES),
            P(None, AXES),
            P(AXES, None),
            P(AXES, None),
            P(AXES, None),
        ),
        out_specs=P(None, None, AXES),
        check_vma=False,
    )
```

```python
import functools
import math

import jax
import jax.numpy as jnp
from jax import lax
from jax.experimental import pallas as pl
from jax.experimental.pallas import tpu as pltpu
from jax.sharding import PartitionSpec as P


SUB = 4
REACH = 8
GROUP = 4
AXES = ("sec", "blk")
F32 = jnp.float32
BF16 = jnp.bfloat16
NT = (((1,), (1,)), ((), ()))
NN = (((1,), (0,)), ((), ()))
TN = (((0,), (0,)), ((), ()))
VMEM = pl.BlockSpec(memory_space=pltpu.VMEM)
LOG = 0.3 * math.log2(math.e)
PREP = 24
HEAD = 8


def parts_of(x):
    high = x.astype(BF16)
    rest = x - high.astype(F32)
    middle = rest.astype(BF16)
    low = (rest - middle.astype(F32)).astype(BF16)
    return high, middle, low


def select_dot(x, onehot, dims, flip=False):
    axis = 1 - dims[0][1 if flip else 0][0]
    size = x.shape[axis]
    wide = jnp.concatenate(parts_of(x), axis=axis)
    pair = (onehot, wide) if flip else (wide, onehot)
    out = lax.dot_general(*pair, dims, preferred_element_type=F32)
    cut = (lambda i: out[:, i * size:(i + 1) * size]) if flip else (lambda i: out[i * size:(i + 1) * size])
    return (cut(0) + cut(1)) + cut(2)


def edges_kernel(state_ref, far_ref, mate_ref, same_ref):
    rows, cdev = state_ref.shape
    state = state_ref[...]
    same_ref[...] = state
    turned = jnp.concatenate([state, jnp.zeros((256 - rows, cdev), F32)], axis=0).T[:, :rows]
    first, last = turned[:REACH], turned[cdev - REACH:]
    odd = jnp.broadcast_to(lax.axis_index(AXES) % 2, first.shape) == 1
    far_ref[...] = jnp.where(odd, last, first)
    mate_ref[...] = jnp.where(odd, first, last)


def index_kernel(plan, state_ref, near_ref, owner_ref, base_ref, part_ref, edge_ref, share_ref, place_ref):
    cap, slots, total, dense = plan
    _, cdev = state_ref.shape
    state = state_ref[...]
    index = near_ref[...] - (lax.axis_index(AXES) * cdev - REACH)
    index = jnp.where(index < 0, index + total, index)
    index = jnp.where(index >= total, index - total, index)
    own = lax.broadcasted_iota(jnp.int32, (cdev, cdev), 0) + REACH
    edge = lax.broadcasted_iota(jnp.int32, (2 * REACH, cdev), 0)
    edge = jnp.where(edge < REACH, edge, edge + cdev)
    inner, outer = jnp.zeros((cdev, cdev), F32), jnp.zeros((2 * REACH, cdev), F32)
    for k in range(near_ref.shape[0]):
        row = index[k:k + 1, :]
        inner = inner + jnp.where(own == row, 1.0, 0.0)
        outer = outer + jnp.where(edge == row, 1.0, 0.0)
    outer = outer.astype(BF16)
    edge_ref[...] = outer
    part = 0.15 * (select_dot(state, inner.astype(BF16), NN) - 4.0 * state)
    part_ref[...] = part
    mine = jnp.broadcast_to(owner_ref[...], (cdev, cdev)).astype(F32)
    lower = lax.broadcasted_iota(jnp.int32, (cdev, cdev), 0) < lax.broadcasted_iota(jnp.int32, (cdev, cdev), 1)
    rank = jnp.sum(jnp.where((mine == mine.T) & lower, 1.0, 0.0), axis=0, keepdims=True).astype(jnp.int32)
    to = owner_ref[...]
    target = to * cap + rank
    load = jnp.concatenate([part, state], axis=0)

    def hot(count, place):
        return jnp.where(lax.broadcasted_iota(jnp.int32, (count, cdev), 0) == place, 1.0, 0.0).astype(BF16)

    def share(chosen):
        return lax.dot_general(chosen, outer, NT, preferred_element_type=F32).astype(BF16)

    if dense is None:
        place_ref[0:1, :] = target
        chosen = hot(slots, target)
        base_ref[...] = select_dot(load, chosen, NT, True)
        share_ref[...] = share(chosen)
        return
    tiles, back = dense
    for t in range(back):
        place_ref[t:t + 1, :] = to * (back * cap + 1) + t * cap + rank
    place_ref[back:back + 1, :] = to * (back * cap + 1) + back * cap
    place_ref[back + 1:back + 2, :] = rank
    each = tiles * cap + 2
    for t in range(2):
        share_ref[:, 2 * REACH * t:2 * REACH * (t + 1)] = share(hot(share_ref.shape[0], to * each + t * cap + rank))
    main = select_dot(load[:tiles * 128], hot(slots, target), NT, True)
    tail = load[tiles * 128:]
    blank = jnp.zeros_like(tail)
    tail = [jnp.concatenate([tail if i == q else blank for i in range(4)], axis=0) for q in range(4)]
    chosen = [hot(slots // 4, jnp.where(rank % 4 == q, target // 4, -1)) for q in range(4)]
    tail = select_dot(jnp.concatenate(tail, axis=1), jnp.concatenate(chosen, axis=1), NT, True)
    for s in range(slots // cap):
        for t in range(tiles):
            base_ref[s * each + t * cap:s * each + (t + 1) * cap, :] = main[s * cap:(s + 1) * cap, t * 128:(t + 1) * 128]
        base_ref[s * each + tiles * cap:(s + 1) * each, :] = tail[2 * s:2 * s + 2]


def pack_kernel(dense, base_ref, part_ref, edge_ref, share_ref, far_ref, mate_ref, out_ref, dyn_ref, halo_ref):
    rows = part_ref.shape[0]
    odd = jnp.broadcast_to(lax.axis_index(AXES) % 2, far_ref.shape) == 1
    before = 0.15 * jnp.where(odd, mate_ref[...], far_ref[...])
    after = 0.15 * jnp.where(odd, far_ref[...], mate_ref[...])
    for i, side in enumerate((before, after)):
        halo_ref[i * REACH:(i + 1) * REACH, :] = side if dense is None else side[:, :128]
        if dense is not None:
            pad = jnp.zeros((REACH, 256 - rows), F32)
            halo_ref[(2 + i) * REACH:(3 + i) * REACH, :] = jnp.concatenate([side[:, 128:], pad], axis=1)
    moved = select_dot(halo_ref[...], share_ref[...], NN, True)
    if dense is None:
        out_ref[:, :rows] = base_ref[:, :rows] + moved
        out_ref[:, rows:] = base_ref[:, rows:]
    else:
        out_ref[...] = base_ref[...] + moved
    dyn_ref[...] = part_ref[...] + (select_dot(before, edge_ref[:REACH], TN) + select_dot(after, edge_ref[REACH:], TN))


def near_matrix(rows, columns, crmx, centre, side):
    row = lax.broadcasted_iota(jnp.int32, (rows, columns), 0)
    col = lax.broadcasted_iota(jnp.int32, (rows, columns), 1)
    place = row & (crmx - 1)
    apart = (((place & 7) * (crmx // 8) + (place >> 3)) - col) & (crmx - 1)
    same = (row // crmx) == (col // crmx)
    off = jnp.where((apart == 1) | (apart == crmx - 1), side, 0.0)
    return jnp.where(same, jnp.where(apart == 0, centre, off), 0.0)


def diffusion(first, source):
    return lax.dot_general(first, source, NT, preferred_element_type=F32)


def prepare_kernel(crmx, mask_ref, ct_ref, cm_ref, rate_ref, both_ref, *refs):
    yt_ref, ym_ref, head_rate_ref, first_ref, move_ref = refs
    per = GROUP * crmx
    size = yt_ref.shape[0]

    @pl.when(pl.program_id(0) == 0)
    def _():
        move_ref[...] = near_matrix(per, per, crmx, 1.0, 0.0).astype(BF16)
        first = near_matrix(per, per, crmx, 3.0, 1.0).astype(BF16)
        first_ref[...] = first
        for q in range(size // per):
            part = slice(q * per, (q + 1) * per)
            yt_ref[part, :] = diffusion(first, ct_ref[:, part])
            ym_ref[part, :] = diffusion(first, cm_ref[:, part])

    for q in range(mask_ref.shape[1] // per):
        part = slice(q * per, (q + 1) * per)
        ice = mask_ref[:, part].astype(F32).astype(BF16)
        ice = lax.dot_general(move_ref[...], ice, NT, preferred_element_type=F32)
        rate_ref[part, :] = 0.7 - 0.4 * ice
        both_ref[part, :] = 0.7 - 0.31 * ice

    @pl.when(pl.program_id(0) == 0)
    def _():
        head_rate_ref[...] = rate_ref[:size]


def arrivals(dense, arrived_ref, slots, wide):
    columns = []
    if dense is None:
        for start in range(0, wide, 128):
            size = min(128, wide - start)
            block = arrived_ref[:, start:start + size]
            if size < 128:
                block = jnp.concatenate([block, jnp.zeros((slots, 128 - size), F32)], axis=1)
            columns.append(block.T[:size])
        return jnp.concatenate(columns, axis=0)
    tiles, cap = dense[0], 8
    each = tiles * cap + 2
    for t in range(tiles):
        block = [arrived_ref[s * each + t * cap:s * each + (t + 1) * cap, :] for s in range(slots // cap)]
        columns.append(jnp.concatenate(block, axis=0).T)
    low = lax.broadcasted_iota(jnp.int32, (cap, 128), 0) < 4
    block = []
    for s in range(slots // cap):
        pair = [arrived_ref[s * each + tiles * cap + i:s * each + tiles * cap + i + 1, :] for i in range(2)]
        block.append(jnp.where(low, *[jnp.broadcast_to(p, (cap, 128)) for p in pair]))
    tail = jnp.concatenate(block, axis=0).T
    which = lax.broadcasted_iota(jnp.int32, (32, slots), 1) % 4
    columns.append(sum(jnp.where(which == q, tail[q * 32:(q + 1) * 32], 0.0) for q in range(4)))
    return jnp.concatenate(columns, axis=0)


def physics_kernel(levels, crmx, dense, arrived_ref, *refs):
    head, (first_ref, crm_hbm, rate_hbm, both_hbm, out_ref), refs = refs[:3], refs[3:8], refs[8:]
    rows_ref, sums_ref, crm_sems, rate_sems = refs[:4]
    head = (*head, refs[4])
    fields, coefs, crm_bufs = (refs[5:7], refs[7:9]), refs[9:11], refs[11:13]
    slots = crm_hbm.shape[0]
    halves = slots // 128
    steps = crmx // 8
    part = GROUP * crmx
    size = head[0].shape[0]
    here = size // crmx
    count = levels // here
    shift = [math.log(0.8 * 5.0 ** j) / 0.3 for j in range(SUB + 1)]

    def crm_copies(group):
        width = levels * crmx
        at = [pl.ds(pl.multiple_of(i * width + group * size, 128), size) for i in range(2)]
        return [pltpu.make_async_copy(crm_hbm.at[:, at[i]], crm_bufs[i].at[group - 1], crm_sems.at[group - 1, i]) for i in range(2)]

    def rate_copies(group):
        at = pl.ds(pl.multiple_of(group * size, 8), size)
        return [
            pltpu.make_async_copy(ref.at[at, :], coefs[i].at[group - 1], rate_sems.at[group - 1, i])
            for i, ref in enumerate((rate_hbm, both_hbm))
        ]

    def start(copies):
        for copy in copies:
            copy.start()

    def wait(copies):
        for copy in copies:
            copy.wait()

    def diffuse(group, k):
        for ref, source in zip(fields[k], crm_bufs):
            for q in range(size // part):
                cut = slice(q * part, (q + 1) * part)
                ref[cut, :] = diffusion(first_ref[...], source[group - 1, :, cut])

    for group in (1, 2):
        start(crm_copies(group))
        start(rate_copies(group))
    arrived = arrivals(dense, arrived_ref, slots, 4 * levels)
    push, wet, temp, moist = [arrived[i * levels:(i + 1) * levels] for i in range(4)]
    push, wet = push * (1.0 / SUB), wet * (1.0 / SUB)
    tables = [5.0 * (temp + push + shift[1]), 5.0 * (moist + wet)]
    for j in range(2, SUB + 1):
        tables += [5.0 ** j * (push + (shift[j] - shift[j - 1])), 5.0 ** j * wet]
    for i, table in enumerate(tables):
        for half in range(halves):
            rows_ref[half, i * levels:(i + 1) * levels] = table[:, half * 128:(half + 1) * 128]

    def unit(group, inner, half, sources):
        lanes = pl.ds(half * 128, 128)
        base = inner * crmx
        level = group * here + inner
        get = lambda ref, k: ref[pl.ds(base + 8 * k, 8), lanes]
        const = lambda i: rows_ref[half, pl.ds(level + i * levels, 8, stride=0), :]
        temp, moist = [[get(sources[i], k) + add for k in range(steps)] for i, add in enumerate((const(0), const(1)))]
        for j in range(1, SUB + 1):
            if j > 1:
                spread = []
                for field, add in ((temp, const(2 * j - 2)), (moist, const(2 * j - 1))):
                    after = pltpu.roll(field[0], 7, 0)
                    before = pltpu.roll(field[steps - 1], 1, 0)
                    ring = [before] + field + [after]
                    spread.append([((ring[k] + ring[k + 2]) + 3.0 * field[k]) + add for k in range(steps)])
                temp, moist = spread
            for k in range(steps):
                over = jnp.maximum(moist[k] - jnp.exp2((LOG / 5.0 ** j) * temp[k]), 0.0)
                moist[k] = moist[k] - get(sources[2], k) * over
                temp[k] = temp[k] + get(sources[3], k) * over
        for i, field in enumerate((temp, moist)):
            while len(field) > 1:
                field = [a + b for a, b in zip(field[0::2], field[1::2])]
            sums_ref[half, pl.ds(pl.multiple_of((i * levels + level) * 8, 8), 8), :] = field[0]

    def run(group, sources, levels_of_group):
        for inner in levels_of_group:
            for half in range(halves):
                unit(group, inner, half, sources)

    head[3][...] = 0.7 - 0.775 * (0.7 - head[2][...])
    run(0, head, range(here // 2))
    wait(crm_copies(1))
    diffuse(1, 0)
    run(0, head, range(here // 2, here))

    @pl.loop(0, (count - 1) // 2)
    def _(trip):
        for k in range(2):
            group = 1 + 2 * trip + k
            ahead = jnp.minimum(group + 1, count - 1)

            @pl.when(group + 2 < count)
            def _():
                start(crm_copies(group + 2))
                start(rate_copies(group + 2))

            wait(rate_copies(group))
            if k == 0:
                wait(crm_copies(ahead))
            else:
                @pl.when(group + 1 < count)
                def _():
                    wait(crm_copies(group + 1))
            diffuse(ahead, 1 - k)
            run(group, (*fields[k], coefs[0].at[group - 1], coefs[1].at[group - 1]), range(here))

    total = 2 * levels
    for half in range(halves):
        summed = sums_ref[half, pl.ds(0, total, stride=8), :]
        for s in range(1, 8):
            summed = summed + sums_ref[half, pl.ds(s, total, stride=8), :]
        mean = summed * (1.0 / (crmx * 5.0 ** SUB))
        mean = jnp.concatenate([mean[:levels] - shift[SUB], mean[levels:]], axis=0)
        if dense is None:
            mean = jnp.concatenate([mean, jnp.zeros((256 - total, 128), F32)], axis=0)
            out_ref[pl.ds(half * 128, 128), :] = mean.T[:, :total]
            continue
        back, cap = dense[1], 8
        each = back * cap + 1
        for t in range(back):
            block = mean[t * 128:(t + 1) * 128].T
            for s in range(128 // cap):
                to = (half * (128 // cap) + s) * each + t * cap
                out_ref[to:to + cap, :] = block[s * cap:(s + 1) * cap]
        tail = jnp.concatenate([mean[back * 128:]] * cap, axis=0).T
        group = lax.broadcasted_iota(jnp.int32, (128, 128), 1) // (128 // cap)
        tail = jnp.where(group == lax.broadcasted_iota(jnp.int32, (128, 128), 0) % cap, tail, 0.0)
        for s in range(128 // cap):
            to = (half * (128 // cap) + s) * each + back * cap
            out_ref[to:to + 1, :] = jnp.sum(tail[s * cap:(s + 1) * cap], axis=0, keepdims=True)


def finish_kernel(dense, dyn_ref, place_ref, back_ref, out_ref):
    cdev = dyn_ref.shape[1]
    rows = lax.broadcasted_iota(jnp.int32, (back_ref.shape[0], cdev), 0)
    count = 1 if dense is None else dense[1] + 1
    hot = [jnp.where(rows == place_ref[i:i + 1, :], 1.0, 0.0).astype(BF16) for i in range(count)]
    means = select_dot(back_ref[...], jnp.concatenate(hot, axis=1), TN)
    if dense is None:
        out_ref[...] = dyn_ref[...] + means
        return
    back = dense[1]
    for t in range(back):
        out_ref[t * 128:(t + 1) * 128] = dyn_ref[t * 128:(t + 1) * 128] + means[:, t * cdev:(t + 1) * cdev]
    tail = means[:, back * cdev:]
    size = dyn_ref.shape[0] - back * 128
    rank = place_ref[back + 1:back + 2, :]
    mine = sum(jnp.where(rank == q, tail[q * size:(q + 1) * size], 0.0) for q in range(128 // size))
    out_ref[back * 128:] = dyn_ref[back * 128:] + mine


def local(state, neighbors, owner, crm_state, phase_mask):
    ndev = lax.axis_size(AXES)
    fields, levels, cdev = state.shape
    rows = fields * levels
    slots, wide = crm_state.shape
    crmx = wide // rows
    cap = slots // ndev
    flat = state.reshape(rows, cdev)
    sds = jax.ShapeDtypeStruct
    dense = (2 * rows // 128, rows // 128) if cap == 8 and rows % 128 == 16 else None
    out_each, back_each = 2 * rows * cap // 128, rows * cap // 128
    far = [(i, (i + 1) % ndev if i % 2 else (i - 1) % ndev) for i in range(ndev)]
    mate = [(i, i ^ 1) for i in range(ndev)]
    to_far, to_mate, same = pl.pallas_call(
        edges_kernel,
        in_specs=[VMEM],
        out_specs=[VMEM] * 3,
        out_shape=[sds((REACH, rows), F32)] * 2 + [sds((rows, cdev), F32)],
        compiler_params=pltpu.CompilerParams(vmem_limit_bytes=8 << 20),
        name="edges",
    )(flat)
    from_far = lax.ppermute(to_far, AXES, far)
    from_mate = lax.ppermute(to_mate, AXES, mate)

    base_shape = (slots, 2 * rows) if dense is None else (ndev * out_each, 128)
    wide_halo = 1 if dense is None else 2
    base, part, edge, share, place = pl.pallas_call(
        functools.partial(index_kernel, (cap, slots, cdev * ndev, dense)),
        in_specs=[VMEM] * 3,
        out_specs=[VMEM] * 5,
        out_shape=[
            sds(base_shape, F32),
            sds((rows, cdev), F32),
            sds((2 * REACH, cdev), BF16),
            sds((base_shape[0], 2 * REACH * wide_halo), BF16),
            sds((1 if dense is None else dense[1] + 2, cdev), jnp.int32),
        ],
        compiler_params=pltpu.CompilerParams(vmem_limit_bytes=12 << 20),
        name="index",
    )(same, neighbors, owner.reshape(1, cdev))
    outgoing, dyn = pl.pallas_call(
        functools.partial(pack_kernel, dense),
        in_specs=[VMEM] * 6,
        out_specs=[VMEM] * 2,
        out_shape=[sds(base_shape, F32), sds((rows, cdev), F32)],
        scratch_shapes=[pltpu.VMEM((2 * REACH * wide_halo, rows if dense is None else 128), F32)],
        compiler_params=pltpu.CompilerParams(vmem_limit_bytes=12 << 20),
        name="pack",
    )(base, part, edge, share, from_far, from_mate)
    arrived = lax.all_to_all(outgoing.reshape(ndev, cap * 2 * rows), AXES, split_axis=0, concat_axis=0, tiled=True)
    arrived = arrived.reshape(outgoing.shape)

    block = PREP * crmx
    count = levels * crmx // block
    take = lambda offset: pl.BlockSpec((slots, block), lambda g: (0, g + offset))
    rates_spec = [pl.BlockSpec((block, slots), lambda g: (g, 0))] * 2
    size = HEAD * crmx
    field, coef = sds((levels * crmx, slots), F32), sds((size, slots), F32)
    offset = levels // HEAD
    *rates, yt, ym, head_rate, first_matrix = pl.pallas_call(
        functools.partial(prepare_kernel, crmx),
        grid=(count,),
        in_specs=[take(0)] + [pl.BlockSpec((slots, size), lambda g, i=i: (0, i * offset)) for i in range(2)],
        out_specs=rates_spec + [VMEM] * 4,
        out_shape=[field] * 2 + [coef] * 3 + [sds((GROUP * crmx, GROUP * crmx), BF16)],
        scratch_shapes=[pltpu.VMEM((GROUP * crmx, GROUP * crmx), BF16)],
        compiler_params=pltpu.CompilerParams(vmem_limit_bytes=53000 << 10),
        cost_estimate=pl.CostEstimate(flops=2 * slots * levels * crmx * GROUP * crmx, transcendentals=0, bytes_accessed=6 * slots * wide),
        name="prepare",
    )(phase_mask, crm_state, crm_state)

    back = pl.pallas_call(
        functools.partial(physics_kernel, levels, crmx, dense),
        in_specs=[VMEM] * 5 + [pl.BlockSpec(memory_space=pl.ANY)] * 3,
        out_specs=VMEM,
        out_shape=sds((slots, rows) if dense is None else (ndev * back_each, 128), F32),
        scratch_shapes=[
            pltpu.VMEM((slots // 128, 2 * SUB * levels + 8, 128), F32),
            pltpu.VMEM((slots // 128, 8 * rows, 128), F32),
            pltpu.SemaphoreType.DMA((offset - 1, 2)),
            pltpu.SemaphoreType.DMA((offset - 1, 2)),
        ]
        + [pltpu.VMEM((size, slots), F32)] * 5
        + [pltpu.VMEM((offset - 1, size, slots), F32)] * 2
        + [pltpu.VMEM((offset - 1, slots, size), BF16)] * 2,
        compiler_params=pltpu.CompilerParams(vmem_limit_bytes=53000 << 10),
        name="physics",
    )(arrived, yt, ym, head_rate, first_matrix, crm_state, *rates)
    returned = lax.all_to_all(back.reshape(ndev, cap * rows), AXES, split_axis=0, concat_axis=0, tiled=True)
    out = pl.pallas_call(
        functools.partial(finish_kernel, dense),
        in_specs=[VMEM] * 3,
        out_specs=VMEM,
        out_shape=sds((rows, cdev), F32),
        compiler_params=pltpu.CompilerParams(vmem_limit_bytes=12 << 20),
        name="finish",
    )(dyn, place, returned.reshape(back.shape))
    return out.reshape(state.shape)


def solution(mesh):
    return jax.shard_map(
        local,
        mesh=mesh,
        in_specs=(
            P(None, None, AXES),
            P(None, AXES),
            P(AXES, None),
            P(AXES, None),
            P(AXES, None),
        ),
        out_specs=P(None, None, AXES),
        check_vma=False,
    )
```

```python
import functools
import math

import jax
import jax.numpy as jnp
from jax import lax
from jax.experimental import pallas as pl
from jax.experimental.pallas import tpu as pltpu
from jax.sharding import PartitionSpec as P


SUB = 4
REACH = 8
GROUP = 4
AXES = ("sec", "blk")
F32 = jnp.float32
BF16 = jnp.bfloat16
NT = (((1,), (1,)), ((), ()))
NN = (((1,), (0,)), ((), ()))
TN = (((0,), (0,)), ((), ()))
VMEM = pl.BlockSpec(memory_space=pltpu.VMEM)
LOG = 0.3 * math.log2(math.e)
PREP = 24
HEAD = 8


def parts_of(x):
    high = x.astype(BF16)
    rest = x - high.astype(F32)
    middle = rest.astype(BF16)
    low = (rest - middle.astype(F32)).astype(BF16)
    return high, middle, low


def select_dot(x, onehot, dims, flip=False):
    axis = 1 - dims[0][1 if flip else 0][0]
    size = x.shape[axis]
    wide = jnp.concatenate(parts_of(x), axis=axis)
    pair = (onehot, wide) if flip else (wide, onehot)
    out = lax.dot_general(*pair, dims, preferred_element_type=F32)
    cut = (lambda i: out[:, i * size:(i + 1) * size]) if flip else (lambda i: out[i * size:(i + 1) * size])
    return (cut(0) + cut(1)) + cut(2)


def edges_kernel(state_ref, far_ref, mate_ref, same_ref):
    rows, cdev = state_ref.shape
    state = state_ref[...]
    same_ref[...] = state
    turned = jnp.concatenate([state, jnp.zeros((256 - rows, cdev), F32)], axis=0).T[:, :rows]
    first, last = turned[:REACH], turned[cdev - REACH:]
    odd = jnp.broadcast_to(lax.axis_index(AXES) % 2, first.shape) == 1
    far_ref[...] = jnp.where(odd, last, first)
    mate_ref[...] = jnp.where(odd, first, last)


def index_kernel(plan, state_ref, near_ref, owner_ref, base_ref, part_ref, edge_ref, share_ref, place_ref):
    cap, slots, total, dense = plan
    _, cdev = state_ref.shape
    state = state_ref[...]
    index = near_ref[...] - (lax.axis_index(AXES) * cdev - REACH)
    index = jnp.where(index < 0, index + total, index)
    index = jnp.where(index >= total, index - total, index)
    own = lax.broadcasted_iota(jnp.int32, (cdev, cdev), 0) + REACH
    edge = lax.broadcasted_iota(jnp.int32, (2 * REACH, cdev), 0)
    edge = jnp.where(edge < REACH, edge, edge + cdev)
    inner, outer = jnp.zeros((cdev, cdev), F32), jnp.zeros((2 * REACH, cdev), F32)
    for k in range(near_ref.shape[0]):
        row = index[k:k + 1, :]
        inner = inner + jnp.where(own == row, 1.0, 0.0)
        outer = outer + jnp.where(edge == row, 1.0, 0.0)
    outer = outer.astype(BF16)
    edge_ref[...] = outer
    part = 0.15 * (select_dot(state, inner.astype(BF16), NN) - 4.0 * state)
    part_ref[...] = part
    mine = jnp.broadcast_to(owner_ref[...], (cdev, cdev)).astype(F32)
    lower = lax.broadcasted_iota(jnp.int32, (cdev, cdev), 0) < lax.broadcasted_iota(jnp.int32, (cdev, cdev), 1)
    rank = jnp.sum(jnp.where((mine == mine.T) & lower, 1.0, 0.0), axis=0, keepdims=True).astype(jnp.int32)
    to = owner_ref[...]
    target = to * cap + rank
    load = jnp.concatenate([part, state], axis=0)

    def hot(count, place):
        return jnp.where(lax.broadcasted_iota(jnp.int32, (count, cdev), 0) == place, 1.0, 0.0).astype(BF16)

    def share(chosen):
        return lax.dot_general(chosen, outer, NT, preferred_element_type=F32).astype(BF16)

    if dense is None:
        place_ref[0:1, :] = target
        chosen = hot(slots, target)
        base_ref[...] = select_dot(load, chosen, NT, True)
        share_ref[...] = share(chosen)
        return
    tiles, back = dense
    for t in range(back):
        place_ref[t:t + 1, :] = to * (back * cap + 1) + t * cap + rank
    place_ref[back:back + 1, :] = to * (back * cap + 1) + back * cap
    place_ref[back + 1:back + 2, :] = rank
    each = tiles * cap + 2
    for t in range(2):
        share_ref[:, 2 * REACH * t:2 * REACH * (t + 1)] = share(hot(share_ref.shape[0], to * each + t * cap + rank))
    main = select_dot(load[:tiles * 128], hot(slots, target), NT, True)
    tail = load[tiles * 128:]
    blank = jnp.zeros_like(tail)
    tail = [jnp.concatenate([tail if i == q else blank for i in range(4)], axis=0) for q in range(4)]
    chosen = [hot(slots // 4, jnp.where(rank % 4 == q, target // 4, -1)) for q in range(4)]
    tail = select_dot(jnp.concatenate(tail, axis=1), jnp.concatenate(chosen, axis=1), NT, True)
    for s in range(slots // cap):
        for t in range(tiles):
            base_ref[s * each + t * cap:s * each + (t + 1) * cap, :] = main[s * cap:(s + 1) * cap, t * 128:(t + 1) * 128]
        base_ref[s * each + tiles * cap:(s + 1) * each, :] = tail[2 * s:2 * s + 2]


def pack_kernel(dense, base_ref, part_ref, edge_ref, share_ref, far_ref, mate_ref, out_ref, dyn_ref, halo_ref):
    rows = part_ref.shape[0]
    odd = jnp.broadcast_to(lax.axis_index(AXES) % 2, far_ref.shape) == 1
    before = 0.15 * jnp.where(odd, mate_ref[...], far_ref[...])
    after = 0.15 * jnp.where(odd, far_ref[...], mate_ref[...])
    for i, side in enumerate((before, after)):
        halo_ref[i * REACH:(i + 1) * REACH, :] = side if dense is None else side[:, :128]
        if dense is not None:
            pad = jnp.zeros((REACH, 256 - rows), F32)
            halo_ref[(2 + i) * REACH:(3 + i) * REACH, :] = jnp.concatenate([side[:, 128:], pad], axis=1)
    moved = select_dot(halo_ref[...], share_ref[...], NN, True)
    if dense is None:
        out_ref[:, :rows] = base_ref[:, :rows] + moved
        out_ref[:, rows:] = base_ref[:, rows:]
    else:
        out_ref[...] = base_ref[...] + moved
    dyn_ref[...] = part_ref[...] + (select_dot(before, edge_ref[:REACH], TN) + select_dot(after, edge_ref[REACH:], TN))


def near_matrix(rows, columns, crmx, centre, side):
    row = lax.broadcasted_iota(jnp.int32, (rows, columns), 0)
    col = lax.broadcasted_iota(jnp.int32, (rows, columns), 1)
    place = row & (crmx - 1)
    apart = (((place & 7) * (crmx // 8) + (place >> 3)) - col) & (crmx - 1)
    same = (row // crmx) == (col // crmx)
    off = jnp.where((apart == 1) | (apart == crmx - 1), side, 0.0)
    return jnp.where(same, jnp.where(apart == 0, centre, off), 0.0)


def diffusion(first, source):
    return lax.dot_general(first, source, NT, preferred_element_type=F32)


def prepare_kernel(crmx, mask_ref, ct_ref, cm_ref, rate_ref, both_ref, *refs):
    yt_ref, ym_ref, head_rate_ref, first_ref, move_ref = refs
    per = GROUP * crmx
    size = yt_ref.shape[0]

    @pl.when(pl.program_id(0) == 0)
    def _():
        move_ref[...] = near_matrix(per, per, crmx, 1.0, 0.0).astype(BF16)
        first = near_matrix(per, per, crmx, 3.0, 1.0).astype(BF16)
        first_ref[...] = first
        for q in range(size // per):
            part = slice(q * per, (q + 1) * per)
            yt_ref[part, :] = diffusion(first, ct_ref[:, part])
            ym_ref[part, :] = diffusion(first, cm_ref[:, part])

    for q in range(mask_ref.shape[1] // per):
        part = slice(q * per, (q + 1) * per)
        ice = mask_ref[:, part].astype(F32).astype(BF16)
        ice = lax.dot_general(move_ref[...], ice, NT, preferred_element_type=F32)
        rate_ref[part, :] = 0.7 - 0.4 * ice
        both_ref[part, :] = 0.7 - 0.31 * ice

    @pl.when(pl.program_id(0) == 0)
    def _():
        head_rate_ref[...] = rate_ref[:size]


def arrivals(dense, arrived_ref, slots, wide):
    columns = []
    if dense is None:
        for start in range(0, wide, 128):
            size = min(128, wide - start)
            block = arrived_ref[:, start:start + size]
            if size < 128:
                block = jnp.concatenate([block, jnp.zeros((slots, 128 - size), F32)], axis=1)
            columns.append(block.T[:size])
        return jnp.concatenate(columns, axis=0)
    tiles, cap = dense[0], 8
    each = tiles * cap + 2
    for t in range(tiles):
        block = [arrived_ref[s * each + t * cap:s * each + (t + 1) * cap, :] for s in range(slots // cap)]
        columns.append(jnp.concatenate(block, axis=0).T)
    low = lax.broadcasted_iota(jnp.int32, (cap, 128), 0) < 4
    block = []
    for s in range(slots // cap):
        pair = [arrived_ref[s * each + tiles * cap + i:s * each + tiles * cap + i + 1, :] for i in range(2)]
        block.append(jnp.where(low, *[jnp.broadcast_to(p, (cap, 128)) for p in pair]))
    tail = jnp.concatenate(block, axis=0).T
    which = lax.broadcasted_iota(jnp.int32, (32, slots), 1) % 4
    columns.append(sum(jnp.where(which == q, tail[q * 32:(q + 1) * 32], 0.0) for q in range(4)))
    return jnp.concatenate(columns, axis=0)


def physics_kernel(levels, crmx, dense, arrived_ref, *refs):
    head, (first_ref, crm_hbm, rate_hbm, both_hbm, out_ref), refs = refs[:3], refs[3:8], refs[8:]
    rows_ref, sums_ref, crm_sems, rate_sems = refs[:4]
    head = (*head, refs[4])
    fields, coefs, crm_bufs = (refs[5:7], refs[7:9]), refs[9:11], refs[11:13]
    slots = crm_hbm.shape[0]
    halves = slots // 128
    steps = crmx // 8
    part = GROUP * crmx
    size = head[0].shape[0]
    here = size // crmx
    count = levels // here
    shift = [math.log(0.8 * 5.0 ** j) / 0.3 for j in range(SUB + 1)]

    def crm_copies(group):
        width = levels * crmx
        at = [pl.ds(pl.multiple_of(i * width + group * size, 128), size) for i in range(2)]
        return [pltpu.make_async_copy(crm_hbm.at[:, at[i]], crm_bufs[i].at[group - 1], crm_sems.at[group - 1, i]) for i in range(2)]

    def rate_copies(group):
        at = pl.ds(pl.multiple_of(group * size, 8), size)
        return [
            pltpu.make_async_copy(ref.at[at, :], coefs[i].at[group - 1], rate_sems.at[group - 1, i])
            for i, ref in enumerate((rate_hbm, both_hbm))
        ]

    def start(copies):
        for copy in copies:
            copy.start()

    def wait(copies):
        for copy in copies:
            copy.wait()

    def diffuse(group, k):
        for ref, source in zip(fields[k], crm_bufs):
            for q in range(size // part):
                cut = slice(q * part, (q + 1) * part)
                ref[cut, :] = diffusion(first_ref[...], source[group - 1, :, cut])

    for group in range(1, count):
        start(crm_copies(group))
        start(rate_copies(group))
    arrived = arrivals(dense, arrived_ref, slots, 4 * levels)
    push, wet, temp, moist = [arrived[i * levels:(i + 1) * levels] for i in range(4)]
    push, wet = push * (1.0 / SUB), wet * (1.0 / SUB)
    tables = [5.0 * (temp + push + shift[1]), 5.0 * (moist + wet)]
    for j in range(2, SUB + 1):
        tables += [5.0 ** j * (push + (shift[j] - shift[j - 1])), 5.0 ** j * wet]
    for i, table in enumerate(tables):
        for half in range(halves):
            rows_ref[half, i * levels:(i + 1) * levels] = table[:, half * 128:(half + 1) * 128]

    def unit(group, inner, half, sources):
        lanes = pl.ds(half * 128, 128)
        base = inner * crmx
        level = group * here + inner
        get = lambda ref, k: ref[pl.ds(base + 8 * k, 8), lanes]
        const = lambda i: rows_ref[half, pl.ds(level + i * levels, 8, stride=0), :]
        temp, moist = [[get(sources[i], k) + add for k in range(steps)] for i, add in enumerate((const(0), const(1)))]
        for j in range(1, SUB + 1):
            if j > 1:
                spread = []
                for field, add in ((temp, const(2 * j - 2)), (moist, const(2 * j - 1))):
                    after = pltpu.roll(field[0], 7, 0)
                    before = pltpu.roll(field[steps - 1], 1, 0)
                    ring = [before] + field + [after]
                    spread.append([((ring[k] + ring[k + 2]) + 3.0 * field[k]) + add for k in range(steps)])
                temp, moist = spread
            for k in range(steps):
                over = jnp.maximum(moist[k] - jnp.exp2((LOG / 5.0 ** j) * temp[k]), 0.0)
                moist[k] = moist[k] - get(sources[2], k) * over
                temp[k] = temp[k] + get(sources[3], k) * over
        for i, field in enumerate((temp, moist)):
            while len(field) > 1:
                field = [a + b for a, b in zip(field[0::2], field[1::2])]
            sums_ref[half, pl.ds(pl.multiple_of((i * levels + level) * 8, 8), 8), :] = field[0]

    def run(group, sources, inners):
        for inner in inners:
            for half in range(halves):
                unit(group, inner, half, sources)

    head[3][...] = 0.7 - 0.775 * (0.7 - head[2][...])
    run(0, head, range(here // 2))
    wait(crm_copies(1))
    diffuse(1, 0)
    run(0, head, range(here // 2, here))

    @pl.loop(0, (count - 1) // 2)
    def _(trip):
        for k in range(2):
            group = 1 + 2 * trip + k
            ahead = jnp.minimum(group + 1, count - 1)
            wait(rate_copies(group))
            if k == 0:
                wait(crm_copies(ahead))
            else:
                @pl.when(group + 1 < count)
                def _():
                    wait(crm_copies(group + 1))
            diffuse(ahead, 1 - k)
            run(group, (*fields[k], coefs[0].at[group - 1], coefs[1].at[group - 1]), range(here))

    total = 2 * levels
    for half in range(halves):
        summed = sums_ref[half, pl.ds(0, total, stride=8), :]
        for s in range(1, 8):
            summed = summed + sums_ref[half, pl.ds(s, total, stride=8), :]
        mean = summed * (1.0 / (crmx * 5.0 ** SUB))
        mean = jnp.concatenate([mean[:levels] - shift[SUB], mean[levels:]], axis=0)
        if dense is None:
            mean = jnp.concatenate([mean, jnp.zeros((256 - total, 128), F32)], axis=0)
            out_ref[pl.ds(half * 128, 128), :] = mean.T[:, :total]
            continue
        back, cap = dense[1], 8
        each = back * cap + 1
        for t in range(back):
            block = mean[t * 128:(t + 1) * 128].T
            for s in range(128 // cap):
                to = (half * (128 // cap) + s) * each + t * cap
                out_ref[to:to + cap, :] = block[s * cap:(s + 1) * cap]
        tail = jnp.concatenate([mean[back * 128:]] * cap, axis=0).T
        group = lax.broadcasted_iota(jnp.int32, (128, 128), 1) // (128 // cap)
        tail = jnp.where(group == lax.broadcasted_iota(jnp.int32, (128, 128), 0) % cap, tail, 0.0)
        for s in range(128 // cap):
            to = (half * (128 // cap) + s) * each + back * cap
            out_ref[to:to + 1, :] = jnp.sum(tail[s * cap:(s + 1) * cap], axis=0, keepdims=True)


def finish_kernel(dense, dyn_ref, place_ref, back_ref, out_ref):
    cdev = dyn_ref.shape[1]
    rows = lax.broadcasted_iota(jnp.int32, (back_ref.shape[0], cdev), 0)
    count = 1 if dense is None else dense[1] + 1
    hot = [jnp.where(rows == place_ref[i:i + 1, :], 1.0, 0.0).astype(BF16) for i in range(count)]
    means = select_dot(back_ref[...], jnp.concatenate(hot, axis=1), TN)
    if dense is None:
        out_ref[...] = dyn_ref[...] + means
        return
    back = dense[1]
    for t in range(back):
        out_ref[t * 128:(t + 1) * 128] = dyn_ref[t * 128:(t + 1) * 128] + means[:, t * cdev:(t + 1) * cdev]
    tail = means[:, back * cdev:]
    size = dyn_ref.shape[0] - back * 128
    rank = place_ref[back + 1:back + 2, :]
    mine = sum(jnp.where(rank == q, tail[q * size:(q + 1) * size], 0.0) for q in range(128 // size))
    out_ref[back * 128:] = dyn_ref[back * 128:] + mine


def local(state, neighbors, owner, crm_state, phase_mask):
    ndev = lax.axis_size(AXES)
    fields, levels, cdev = state.shape
    rows = fields * levels
    slots, wide = crm_state.shape
    crmx = wide // rows
    cap = slots // ndev
    flat = state.reshape(rows, cdev)
    sds = jax.ShapeDtypeStruct
    dense = (2 * rows // 128, rows // 128) if cap == 8 and rows % 128 == 16 else None
    out_each, back_each = 2 * rows * cap // 128, rows * cap // 128
    far = [(i, (i + 1) % ndev if i % 2 else (i - 1) % ndev) for i in range(ndev)]
    mate = [(i, i ^ 1) for i in range(ndev)]
    to_far, to_mate, same = pl.pallas_call(
        edges_kernel,
        in_specs=[VMEM],
        out_specs=[VMEM] * 3,
        out_shape=[sds((REACH, rows), F32)] * 2 + [sds((rows, cdev), F32)],
        compiler_params=pltpu.CompilerParams(vmem_limit_bytes=8 << 20),
        name="edges",
    )(flat)
    from_far = lax.ppermute(to_far, AXES, far)
    from_mate = lax.ppermute(to_mate, AXES, mate)

    base_shape = (slots, 2 * rows) if dense is None else (ndev * out_each, 128)
    wide_halo = 1 if dense is None else 2
    base, part, edge, share, place = pl.pallas_call(
        functools.partial(index_kernel, (cap, slots, cdev * ndev, dense)),
        in_specs=[VMEM] * 3,
        out_specs=[VMEM] * 5,
        out_shape=[
            sds(base_shape, F32),
            sds((rows, cdev), F32),
            sds((2 * REACH, cdev), BF16),
            sds((base_shape[0], 2 * REACH * wide_halo), BF16),
            sds((1 if dense is None else dense[1] + 2, cdev), jnp.int32),
        ],
        compiler_params=pltpu.CompilerParams(vmem_limit_bytes=12 << 20),
        name="index",
    )(same, neighbors, owner.reshape(1, cdev))
    outgoing, dyn = pl.pallas_call(
        functools.partial(pack_kernel, dense),
        in_specs=[VMEM] * 6,
        out_specs=[VMEM] * 2,
        out_shape=[sds(base_shape, F32), sds((rows, cdev), F32)],
        scratch_shapes=[pltpu.VMEM((2 * REACH * wide_halo, rows if dense is None else 128), F32)],
        compiler_params=pltpu.CompilerParams(vmem_limit_bytes=12 << 20),
        name="pack",
    )(base, part, edge, share, from_far, from_mate)
    arrived = lax.all_to_all(outgoing.reshape(ndev, cap * 2 * rows), AXES, split_axis=0, concat_axis=0, tiled=True)
    arrived = arrived.reshape(outgoing.shape)

    block = PREP * crmx
    count = levels * crmx // block
    take = lambda offset: pl.BlockSpec((slots, block), lambda g: (0, g + offset))
    rates_spec = [pl.BlockSpec((block, slots), lambda g: (g, 0))] * 2
    size = HEAD * crmx
    field, coef = sds((levels * crmx, slots), F32), sds((size, slots), F32)
    offset = levels // HEAD
    *rates, yt, ym, head_rate, first_matrix = pl.pallas_call(
        functools.partial(prepare_kernel, crmx),
        grid=(count,),
        in_specs=[take(0)] + [pl.BlockSpec((slots, size), lambda g, i=i: (0, i * offset)) for i in range(2)],
        out_specs=rates_spec + [VMEM] * 4,
        out_shape=[field] * 2 + [coef] * 3 + [sds((GROUP * crmx, GROUP * crmx), BF16)],
        scratch_shapes=[pltpu.VMEM((GROUP * crmx, GROUP * crmx), BF16)],
        compiler_params=pltpu.CompilerParams(vmem_limit_bytes=53000 << 10),
        cost_estimate=pl.CostEstimate(flops=2 * slots * levels * crmx * GROUP * crmx, transcendentals=0, bytes_accessed=6 * slots * wide),
        name="prepare",
    )(phase_mask, crm_state, crm_state)

    back = pl.pallas_call(
        functools.partial(physics_kernel, levels, crmx, dense),
        in_specs=[VMEM] * 5 + [pl.BlockSpec(memory_space=pl.ANY)] * 3,
        out_specs=VMEM,
        out_shape=sds((slots, rows) if dense is None else (ndev * back_each, 128), F32),
        scratch_shapes=[
            pltpu.VMEM((slots // 128, 2 * SUB * levels + 8, 128), F32),
            pltpu.VMEM((slots // 128, 8 * rows, 128), F32),
            pltpu.SemaphoreType.DMA((offset - 1, 2)),
            pltpu.SemaphoreType.DMA((offset - 1, 2)),
        ]
        + [pltpu.VMEM((size, slots), F32)] * 5
        + [pltpu.VMEM((offset - 1, size, slots), F32)] * 2
        + [pltpu.VMEM((offset - 1, slots, size), BF16)] * 2,
        compiler_params=pltpu.CompilerParams(vmem_limit_bytes=53000 << 10),
        name="physics",
    )(arrived, yt, ym, head_rate, first_matrix, crm_state, *rates)
    returned = lax.all_to_all(back.reshape(ndev, cap * rows), AXES, split_axis=0, concat_axis=0, tiled=True)
    out = pl.pallas_call(
        functools.partial(finish_kernel, dense),
        in_specs=[VMEM] * 3,
        out_specs=VMEM,
        out_shape=sds((rows, cdev), F32),
        compiler_params=pltpu.CompilerParams(vmem_limit_bytes=12 << 20),
        name="finish",
    )(dyn, place, returned.reshape(back.shape))
    return out.reshape(state.shape)


def solution(mesh):
    return jax.shard_map(
        local,
        mesh=mesh,
        in_specs=(
            P(None, None, AXES),
            P(None, AXES),
            P(AXES, None),
            P(AXES, None),
            P(AXES, None),
        ),
        out_specs=P(None, None, AXES),
        check_vma=False,
    )
```
